32 devices in a mesh: dp: 4 (over x, core), section: 2 (over y), tensor: 4 (over z).
Axes of the slice: x: 2, y: 2, z: 4, core: 2. Of those that a mesh axis runs over, the one named last changes fastest.
Arguments:
- section_input: bfloat16 [2, 512, 3072], P('section', 'dp'), may hold values from -6 to 6
- norm_gain: float32 [2, 3072], P('section'), may hold values from 0.25 to 1.75
- value_weight: bfloat16 [2, 1536, 3072], P('section', 'tensor'), may hold values from -0.109375 to 0.109375
- attn_probs: bfloat16 [2, 12, 512, 128], P('section', 'tensor', 'dp'), may hold values from 0 to 1, as said below
- out_weight: bfloat16 [2, 3072, 1536], P('section', None, 'tensor'), may hold values from -0.15625 to 0.15625
- direction: bfloat16 [2, 3072, 1536], P('section', None, 'tensor'), may hold values from -0.15625 to 0.15625
- curvature: bfloat16 [512, 3072], P('dp'), may hold values from 0.19921875 to 2
Outputs:
- curvature_product: float32 [2, 3072, 1536], P('section', 'dp', 'tensor')
The draws below stay inside these ranges and needn't reach their ends.
Inputs may be any that keep to these rules, and one draw needn't show every extreme that they name: `attn_probs`: each row is a causal attention distribution over the 128 tokens of its sequence: nonnegative, summing to one up to rounding, zero for keys after the query's position in the sequence.
All inputs are finite; a program needn't handle non-finite values.
Results may differ from the reference program's by a relative error of at most 0.013.
Values may be sent and summed in bfloat16 or wider, within the bound.
A program may use at most 64 MiB of HBM per device.

```python
import math
import jax
import jax.numpy as jnp
from jax import lax

D = 3072
HEAD_DIM = 128
TOK_DEV = 128
HEADS = 12
SECTIONS = 2
TOKENS = 512
N_DP = 4


def draw_attn_probs(key, part):
    shape = (SECTIONS, HEADS, TOKENS, TOK_DEV)
    logits = 1.5 * jax.random.normal(key, shape, jnp.float32)
    query = (jnp.arange(TOKENS, dtype=jnp.int32) % TOK_DEV)[:, None]
    keypos = jnp.arange(TOK_DEV, dtype=jnp.int32)[None, :]
    allowed = keypos <= query
    weights = jnp.where(allowed, jnp.exp(logits), 0.0)
    probs = weights / jnp.sum(weights, axis=-1, keepdims=True)
    return probs.astype(jnp.bfloat16)


def shard_levels(rng, shape, pieces, smallest, high):
    factor_of, own = 1.0, jax.random.fold_in(rng, 6)
    for dim, shards_of in pieces:
        heights = jnp.exp(jax.random.uniform(jax.random.fold_in(own, dim), (shards_of,), jnp.float32, smallest / len(pieces), high / len(pieces)))
        factor_of = factor_of * jnp.repeat(heights, shape[dim] // shards_of).reshape([-1 if axis == dim else 1 for axis in range(len(shape))])
    return factor_of


def gaussian(key, dims, deviation, most, split=(), kind=jnp.bfloat16):
    values = jax.random.normal(key, dims, jnp.float32) * deviation
    if len(split) > 0:
        values = shard_levels(key, dims, split, -0.22, 0.18) * values
    return jnp.clip(values, min=-most, max=most).astype(kind)


def setup_inputs(seed: int = 0) -> dict:
    key_list = jax.random.split(jax.random.key(seed), 8)
    section_input = gaussian(key_list[0], (SECTIONS, TOKENS, D), 1.0, 6.0, ((0, 2), (1, 4)))
    norm_gain = jnp.clip(1.0 + 0.15 * jax.random.normal(key_list[1], (SECTIONS, D), jnp.float32), 0.25, 1.75)
    value_weight = gaussian(key_list[2], (SECTIONS, HEADS * HEAD_DIM, D), D ** -0.5, 0.109375, ((0, 2), (1, 4)))
    attn_probs = draw_attn_probs(jax.random.fold_in(key_list[7], 71), 0)
    out_weight = gaussian(key_list[4], (SECTIONS, D, HEADS * HEAD_DIM), (HEADS * HEAD_DIM) ** -0.5, 0.15625, ((0, 2), (2, 4)))
    direction = gaussian(key_list[5], (SECTIONS, D, HEADS * HEAD_DIM), (HEADS * HEAD_DIM) ** -0.5, 0.15625, ((0, 2), (2, 4)))
    curvature = jnp.clip(jnp.exp(math.log(2.0) - 2.306499 * jax.random.uniform(key_list[6], (TOKENS, D), jnp.float32) ** shard_levels(key_list[6], (TOKENS, D), ((0, 4),), -0.2, 0.2)), 0.19921875, 2.0).astype(jnp.bfloat16)
    return {"section_input": section_input, "norm_gain": norm_gain, "value_weight": value_weight, "attn_probs": attn_probs, "out_weight": out_weight, "direction": direction, "curvature": curvature}


def mixing(probs, vals):
    wide = probs.astype(jnp.float32).reshape(HEADS, N_DP, TOK_DEV, TOK_DEV)
    cols = vals.astype(jnp.float32).reshape(N_DP, TOK_DEV, HEADS, HEAD_DIM)
    return jnp.einsum('hbqk,bkhd->bqhd', wide, cols).reshape(TOKENS, HEADS * HEAD_DIM)

def mixing_back(probs, grads):
    wide = probs.astype(jnp.float32).reshape(HEADS, N_DP, TOK_DEV, TOK_DEV)
    cols = grads.astype(jnp.float32).reshape(N_DP, TOK_DEV, HEADS, HEAD_DIM)
    return jnp.einsum('hbqk,bqhd->bkhd', wide, cols).reshape(TOKENS, HEADS * HEAD_DIM)

def reference(section_input, norm_gain, value_weight, attn_probs, out_weight, direction, curvature):
    saved = []
    tangent = jnp.zeros((TOKENS, D), jnp.bfloat16)
    for layer in range(SECTIONS):
        xval = section_input[layer].astype(jnp.float32)
        gain = norm_gain[layer]
        rnorm = lax.rsqrt(lax.optimization_barrier(jnp.mean(xval * xval, axis=-1, keepdims=True)) + 1e-06)
        normed = (xval * rnorm * gain).astype(jnp.bfloat16)
        values = jnp.dot(normed, value_weight[layer].T, preferred_element_type=jnp.float32).astype(jnp.bfloat16)
        act = mixing(attn_probs[layer], values).astype(jnp.bfloat16)
        tfloat = tangent.astype(jnp.float32)
        tnorm = (gain * (rnorm * tfloat - rnorm ** 3 * xval * lax.optimization_barrier(jnp.mean(xval * tfloat, axis=-1, keepdims=True)))).astype(jnp.bfloat16)
        tvals = jnp.dot(tnorm, value_weight[layer].T, preferred_element_type=jnp.float32).astype(jnp.bfloat16)
        tmix = mixing(attn_probs[layer], tvals).astype(jnp.bfloat16)
        total = jnp.dot(tmix, out_weight[layer].T, preferred_element_type=jnp.float32) + jnp.dot(act, direction[layer].T, preferred_element_type=jnp.float32)
        tangent = (tfloat + total).astype(jnp.bfloat16)
        saved.append((xval, gain, rnorm, act))
    adjoint = (curvature.astype(jnp.float32) * tangent.astype(jnp.float32)).astype(jnp.bfloat16)
    results = [None] * SECTIONS
    for layer in range(SECTIONS - 1, -1, -1):
        xval, gain, rnorm, act = saved[layer]
        results[layer] = jnp.dot(adjoint.T, act, preferred_element_type=jnp.float32)
        if layer > 0:
            gmix = jnp.dot(adjoint, out_weight[layer], preferred_element_type=jnp.float32)
            gvals = mixing_back(attn_probs[layer], gmix).astype(jnp.bfloat16)
            gnorm = jnp.dot(gvals, value_weight[layer], preferred_element_type=jnp.float32)
            gxval = rnorm * gain * gnorm - rnorm ** 3 * xval * lax.optimization_barrier(jnp.mean(xval * gain * gnorm, axis=-1, keepdims=True))
            adjoint = (adjoint.astype(jnp.float32) + gxval).astype(jnp.bfloat16)
    return jnp.stack(results)
```

```python
import functools

import jax
import jax.numpy as jnp
from jax import lax
from jax.experimental import pallas as pl
from jax.experimental.pallas import tpu as pltpu
from jax.sharding import PartitionSpec as P

MESH = pl.DeviceIdType.MESH
BF = jnp.bfloat16
F32 = jnp.float32
TOKEN_CHUNKS = 2


def dot_nt(a, b):
    return lax.dot_general(a, b, (((1,), (1,)), ((), ())), preferred_element_type=F32)


def dot_tn(a, b):
    return lax.dot_general(a, b, (((0,), (0,)), ((), ())), preferred_element_type=F32)


def dot_nn(a, b):
    return lax.dot_general(a, b, (((1,), (0,)), ((), ())), preferred_element_type=F32)


def kernel(
    fused, S, T, N,
    x_ref, gain_ref, probs_ref, wv_hbm, wd_hbm, wo_hbm, curv_hbm,
    *rest,
):
    if fused:
        prod_ref, rest = rest[0], rest[1:]
    else:
        gout_ref, actout_ref, rest = rest[0], rest[1], rest[2:]
    (
        wv, wd, wo, curv, act, part, partb, in_a, in_d, in_f, gpartb, normed, tn, gfull, trow, grow,
        actall, gall,
        load_sem, act_send, act_recv, a_send, a_recv, tn_send, tn_recv, d_send, d_recv,
        s_send, s_recv, f_send, f_recv, h_send, h_recv, x_send, x_recv,
    ) = rest
    d = lax.axis_index("dp")
    s = lax.axis_index("section")
    i = lax.axis_index("tensor")
    tok, width = x_ref.shape
    rows = tok // T
    heads = probs_ref.shape[0]
    hd = wv.shape[0] // heads
    feats = width // N
    CH = 512 if width % 512 == 0 else width
    chunks = [slice(c, c + CH) for c in range(0, width, CH)]

    def rows_at(j):
        return pl.ds(pl.multiple_of(j * rows, rows), rows)

    def feats_at(j):
        return pl.ds(pl.multiple_of(j * feats, 128), feats)

    def peer(me, k, n):
        return lax.rem(me + k, n)

    loads = [
        pltpu.make_async_copy(src, dst, load_sem.at[k])
        for k, (src, dst) in enumerate(((wv_hbm, wv), (wd_hbm, wd), (wo_hbm, wo), (curv_hbm, curv)))
    ]
    for copy in loads:
        copy.start()

    barrier = pltpu.get_barrier_semaphore()

    def greet(dev):
        pl.semaphore_signal(barrier, inc=1, device_id=dev, device_id_type=MESH)

    for k in range(1, T):
        greet({"dp": d, "section": s, "tensor": peer(i, k, T)})
    for k in range(1, N):
        greet({"dp": peer(d, k, N), "section": s, "tensor": i})
    for low in range(S - 1):
        wide = N if (fused and low == 0) else 1

        @pl.when(s == low)
        def _():
            for k in range(wide):
                for j in range(T):
                    greet({"dp": peer(d, k, N), "section": s + 1, "tensor": j})

        @pl.when(s == low + 1)
        def _():
            for k in range(wide):
                for j in range(T):
                    greet({"dp": peer(d, k, N), "section": s - 1, "tensor": j})

    gain = gain_ref[...]
    xf = x_ref[...].astype(F32)
    rnorm = lax.rsqrt(jnp.mean(xf * xf, axis=-1, keepdims=True) + 1e-06)
    normed[...] = (xf * rnorm * gain).astype(BF)

    def mix(vals):
        return jnp.concatenate(
            [dot_nn(probs_ref[h], vals[:, h * hd : (h + 1) * hd]) for h in range(heads)], axis=1
        )

    loads[0].wait()
    act[...] = mix(dot_nt(normed[...], wv[...]).astype(BF)).astype(BF)

    for here in range(S):
        count = T - 1 + N - 1
        for low in (here - 1, here):
            if 0 <= low < S - 1:
                count += T * (N if (fused and low == 0) else 1)

        @pl.when(s == here)
        def _():
            pl.semaphore_wait(barrier, count)

    def remote(src, dst, send, recv, dev):
        return pltpu.make_async_remote_copy(
            src_ref=src, dst_ref=dst, send_sem=send, recv_sem=recv,
            device_id=dev, device_id_type=MESH,
        )

    def at(dd, ss, jj):
        return {"dp": dd, "section": ss, "tensor": jj}

    def copy_act(k, owner):
        return remote(act, actall.at[owner], act_send.at[k], act_recv.at[k], at(peer(d, k, N), s, i))

    def copy_a(j, owner):
        return remote(partb.at[rows_at(j)], in_a.at[owner], a_send.at[j], a_recv.at[owner], at(d, s + 1, j))

    def copy_tn(k, owner):
        return remote(
            tn.at[rows_at(owner)], tn.at[rows_at(owner)], tn_send.at[k], tn_recv.at[k], at(d, s, peer(i, k, T))
        )

    def copy_d(k):
        j = peer(i, k, T)
        return remote(partb.at[rows_at(j)], in_d.at[k - 1], d_send.at[k], d_recv.at[k], at(d, s, j))

    def copy_s(k, owner):
        return remote(
            gfull.at[rows_at(owner)], gfull.at[rows_at(owner)], s_send.at[k], s_recv.at[k],
            at(d, s, peer(i, k, T)),
        )

    def copy_f(k):
        j = peer(i, k, T)
        return remote(gpartb.at[rows_at(j)], in_f.at[k - 1], f_send.at[k], f_recv.at[k], at(d, s, j))

    def copy_h(j, owner):
        return remote(grow, gfull.at[rows_at(owner)], h_send.at[0, j], h_recv.at[0, owner], at(d, s - 1, j))

    def copy_hd(k, j, owner):
        dd = peer(d, k, N)
        return remote(
            grow.at[:, feats_at(dd)], gall.at[lax.rem(d, N), rows_at(owner)],
            h_send.at[k, j], h_recv.at[k, owner], at(dd, s - 1, j),
        )

    def land_hd(k, owner):
        src = peer(d, N - k, N)
        return remote(
            grow.at[:, feats_at(d)], gall.at[src, rows_at(owner)],
            h_send.at[k, owner], h_recv.at[k, owner], at(d, s, i),
        )

    def copy_x(k):
        dd = peer(d, k, N)
        return remote(gfull.at[:, feats_at(dd)], gall.at[d], x_send.at[k], x_recv.at[k], at(dd, s, i))

    def land_x(k):
        src = peer(d, N - k, N)
        return remote(gfull.at[:, feats_at(d)], gall.at[src], x_send.at[k], x_recv.at[k], at(d, s, i))

    if fused:
        for k in range(1, N):
            copy_act(k, d).start()
        actall[d] = act[...]

    xrows = x_ref[rows_at(i)].astype(F32)
    rrows = lax.rsqrt(jnp.mean(xrows * xrows, axis=-1, keepdims=True) + 1e-06)

    loads[1].wait()
    for c in chunks:
        base = dot_nt(act[...], wd[c, :])
        part[:, c] = base

    loads[2].wait()
    loads[3].wait()

    @pl.when(s == 0)
    def _():
        partb[...] = part[...].astype(BF)

    @pl.when(s > 0)
    def _():
        total = None
        for j in range(T):
            remote(partb.at[rows_at(j)], in_a.at[j], a_send.at[j], a_recv.at[j], at(d, s, i)).wait_recv()
        for j in range(T):
            piece = in_a[j].astype(F32)
            total = piece if total is None else total + piece
        tfloat = total.astype(BF).astype(F32)
        trow[...] = tfloat
        tn[rows_at(i)] = (
            gain * (rrows * tfloat - rrows**3 * xrows * jnp.mean(xrows * tfloat, axis=-1, keepdims=True))
        ).astype(BF)
        for k in range(1, T):
            copy_tn(k, i).start()
        for k in range(1, T):
            copy_tn(k, peer(i, T - k, T)).wait_recv()
        tmix = mix(dot_nt(tn[...], wv[...]).astype(BF)).astype(BF)
        for c in chunks:
            part[:, c] = part[:, c] + dot_nt(tmix, wo[c, :])
        part[rows_at(i)] = part[rows_at(i)] + trow[...]
        partb[...] = part[...].astype(BF)
        for k in range(1, T):
            copy_tn(k, i).wait_send()

    if S > 1:

        @pl.when(s < S - 1)
        def _():
            for j in range(T):
                copy_a(j, i).start()

    @pl.when(s == S - 1)
    def _():
        for k in range(1, T):
            copy_d(k).start()
        total = part[rows_at(i)]
        for k in range(1, T):
            copy_d(k).wait_recv()
        for k in range(1, T):
            total = total + in_d[k - 1].astype(F32)
        tlast = total.astype(BF).astype(F32)
        gfull[rows_at(i)] = (curv[rows_at(i)].astype(F32) * tlast).astype(BF)
        for k in range(1, T):
            copy_s(k, i).start()
        for k in range(1, T):
            copy_s(k, peer(i, T - k, T)).wait_recv()
        for k in range(1, T):
            copy_s(k, i).wait_send()
            copy_d(k).wait_send()

    if S > 1:

        @pl.when(s < S - 1)
        def _():
            for j in range(T):
                copy_a(j, i).wait_send()

        def gather_rows():
            for j in range(T):
                remote(grow, gfull.at[rows_at(j)], h_send.at[0, j], h_recv.at[0, j], at(d, s, i)).wait_recv()

        if fused:
            if S > 2:

                @pl.when(jnp.logical_and(s > 0, s < S - 1))
                def _():
                    gather_rows()

            @pl.when(s == 0)
            def _():
                for k in range(N):
                    for j in range(T):
                        land_hd(k, j).wait_recv()
        else:

            @pl.when(s < S - 1)
            def _():
                gather_rows()

        @pl.when(s > 0)
        def _():
            gm = dot_nn(gfull[...], wo[...]).astype(BF)
            gv = jnp.concatenate(
                [dot_tn(probs_ref[h], gm[:, h * hd : (h + 1) * hd]) for h in range(heads)], axis=1
            ).astype(BF)
            for c in chunks:
                gc = dot_nn(gv, wv[:, c])
                part[:, c] = gc
                gpartb[:, c] = gc.astype(BF)
            for k in range(1, T):
                copy_f(k).start()
            total = part[rows_at(i)]
            for k in range(1, T):
                copy_f(k).wait_recv()
            for k in range(1, T):
                total = total + in_f[k - 1].astype(F32)
            scaled = gain * total
            gx = rrows * scaled - rrows**3 * xrows * jnp.mean(xrows * scaled, axis=-1, keepdims=True)
            grow[...] = (gfull[rows_at(i)].astype(F32) + gx).astype(BF)

            def plain():
                for j in range(T):
                    copy_h(j, i).start()
                for j in range(T):
                    copy_h(j, i).wait_send()

            if fused:

                @pl.when(s == 1)
                def _():
                    for k in range(N):
                        for j in range(T):
                            copy_hd(k, j, i).start()
                    for k in range(N):
                        for j in range(T):
                            copy_hd(k, j, i).wait_send()

                if S > 2:
                    pl.when(s > 1)(plain)
            else:
                plain()
            for k in range(1, T):
                copy_f(k).wait_send()

    if fused:

        def spread():
            for k in range(1, N):
                copy_x(k).start()
            gall[d] = gfull[:, feats_at(d)]
            for k in range(1, N):
                land_x(k).wait_recv()
            for k in range(1, N):
                copy_x(k).wait_send()

        if S > 1:
            pl.when(s > 0)(spread)
        else:
            spread()
        for k in range(1, N):
            copy_act(k, peer(d, N - k, N)).wait_recv()
        prod_ref[...] = dot_tn(
            gall[...].reshape(N * tok, feats), actall[...].reshape(N * tok, act.shape[1])
        )
        for k in range(1, N):
            copy_act(k, d).wait_send()
    else:
        gout_ref[...] = gfull[...]
        actout_ref[...] = act[...]


def kernel_pair(
    T, N,
    x_ref, gain_ref, probs_ref, wv_hbm, wd_hbm, wo_hbm, curv_hbm,
    prod_ref,
    wv, wd, wo, curv, act, vals, tvals, part, tbuf, gbuf, xrow, gain1,
    a_src, a_hop, a_land, d_src, d_hop, d_land, f_src, f_hop, f_land,
    grow, actall, gall,
    load_sem, lend_send, lend_recv, act_send, act_recv,
    hop_send, hop_recv, rs_send, rs_recv, ag_send, ag_recv,
    h_send, h_self, h_recv, x_send, x_recv,
):
    d = lax.axis_index("dp")
    s = lax.axis_index("section")
    i = lax.axis_index("tensor")
    tok, width = x_ref.shape
    K = TOKEN_CHUNKS
    Q = N // 2
    ck = tok // K
    blk = ck // T
    wide = width // N
    heads = probs_ref.shape[0]
    hd = wv.shape[0] // heads
    far = [k for k in range(2, T - 1)] + [k for k in range(1, T) if k in (1, T - 1)]
    subs = range(Q)

    def peer(me, k, n):
        return lax.rem(me + k, n)

    def at(dd, ss, jj):
        return {"dp": dd, "section": ss, "tensor": jj}

    def chunk(kk):
        return slice(kk * ck, (kk + 1) * ck)

    def rows(kk, j):
        return pl.ds(pl.multiple_of(kk * ck + j * blk, blk), blk)

    def col(y, q):
        return slice((2 * q + y) * wide, (2 * q + y + 1) * wide)

    def feats_at(j):
        return pl.ds(pl.multiple_of(j * wide, 128), wide)

    def seq_rows():
        return pl.ds(pl.multiple_of(d * ck, ck), ck)

    def own_rows():
        return pl.ds(pl.multiple_of(d * ck + i * blk, blk), blk)

    def remote(src, dst, send, recv, dev):
        return pltpu.make_async_remote_copy(
            src_ref=src, dst_ref=dst, send_sem=send, recv_sem=recv,
            device_id=dev, device_id_type=MESH,
        )

    def landed(ref, sem):
        remote(ref, ref, sem, sem, at(d, s, i)).wait_recv()

    def sent(ref, sem):
        remote(ref, ref, sem, sem, at(d, s, i)).wait_send()

    loads = [
        pltpu.make_async_copy(src, dst, load_sem.at[k])
        for k, (src, dst) in enumerate(((wv_hbm, wv), (wd_hbm, wd), (wo_hbm, wo), (curv_hbm, curv)))
    ]
    loads[0].start()
    loads[1].start()

    barrier = pltpu.get_barrier_semaphore()
    for a in range(N):
        for b in range(2):
            for c in range(T):
                if a or b or c:
                    pl.semaphore_signal(
                        barrier, inc=1, device_id=at(peer(d, a, N), peer(s, b, 2), peer(i, c, T)),
                        device_id_type=MESH,
                    )
    loads[2].start()
    loads[3].start()

    def mix(kk, buf):
        r = chunk(kk)
        return jnp.concatenate(
            [dot_nn(probs_ref[h, r, :], buf[:, h * hd : (h + 1) * hd]) for h in range(heads)], axis=1
        ).astype(BF)

    def rnorm_of(xf):
        return lax.rsqrt(jnp.mean(xf * xf, axis=-1, keepdims=True) + 1e-06)

    gain = gain_ref[...]

    def values_of(kk):
        r = chunk(kk)
        xf = x_ref[r, :].astype(F32)
        normed = (xf * rnorm_of(xf) * gain).astype(BF)
        vals[r, :] = dot_nt(normed, wv[...]).astype(BF)

    def acts_of(kk):
        act[chunk(kk), :] = mix(kk, vals)

    for kk in range(1, K):
        vals[chunk(kk), :] = jnp.zeros((ck, vals.shape[1]), BF)
        tvals[chunk(kk), :] = jnp.zeros((ck, vals.shape[1]), BF)

    def copy_act(k, owner):
        return remote(act, actall.at[owner], act_send.at[k], act_recv.at[k], at(peer(d, k, N), s, i))

    lend = [
        remote(x_ref.at[rows(kk, i)], xrow.at[kk], lend_send.at[kk], lend_recv.at[kk], at(d, 0, i))
        for kk in range(K)
    ] + [remote(gain_ref, gain1, lend_send.at[K], lend_recv.at[K], at(d, 0, i))]

    A, D_, F_ = (0, a_src, a_hop, a_land, 0), (1, d_src, d_hop, d_land, 1), (2, f_src, f_hop, f_land, 1)

    def cw(p, q):
        return slice(0, f_src.shape[-1] if p[0] == 2 and q == 0 else wide)

    def hop(p, kk, q):
        c = cw(p, q)
        y = 1 - p[4]
        r = chunk(kk)
        remote(
            p[1].at[y, q, r, c], p[2].at[q, r, c], hop_send.at[p[0], kk, q], hop_recv.at[p[0], kk, q], at(d, y, i)
        ).start()

    def hop_done(p, kk, q):
        sent(p[1].at[1 - p[4], q, chunk(kk), cw(p, q)], hop_send.at[p[0], kk, q])

    def scatter(p, me, kk, q):
        c = cw(p, q)
        if me != p[4]:
            landed(p[2].at[q, chunk(kk), c], hop_recv.at[p[0], kk, q])
        buf = p[1].at[me, q] if me == p[4] else p[2].at[q]
        for k in far:
            j = peer(i, k, T)
            remote(
                buf.at[rows(kk, j), c], p[3].at[q, kk, k - 1, :, c], rs_send.at[p[0], kk, q],
                rs_recv.at[p[0], kk, q], at(d, me, j),
            ).start()

    def scatter_done(p, kk, q):
        sent(p[3].at[q, kk, :, :, cw(p, q)], rs_send.at[p[0], kk, q])

    def collect(p, me, kk, q, local):
        c = cw(p, q)
        total = p[2][q, rows(kk, i), c].astype(F32) if me != p[4] else local
        landed(p[3].at[q, kk, :, :, c], rs_recv.at[p[0], kk, q])
        for k in range(T - 1):
            total = total + p[3][q, kk, k, :, c].astype(F32)
        return total

    def spread(n, buf, me, kk, q):
        src = buf.at[rows(kk, i), col(me, q)]
        for k in far + ([0] if me == 0 else []):
            remote(
                src, src, ag_send.at[n, kk, q], ag_recv.at[n, me, kk, q], at(d, 1, peer(i, k, T))
            ).start()

    def spread_done(n, buf, me, kk, q):
        count = T if me == 0 else T - 1
        sent(buf.at[kk * ck : kk * ck + count * blk, col(me, q)], ag_send.at[n, kk, q])

    def gathered(n, buf, y, kk, q):
        count = T if y == 0 else T - 1
        landed(buf.at[kk * ck : kk * ck + count * blk, col(y, q)], ag_recv.at[n, y, kk, q])

    def tangent(me, kk, q):
        r = rows(kk, i)
        tb = collect(A, me, kk, q, part[r, col(me, q)]).astype(BF)
        tbuf[r, col(me, q)] = tb
        spread(0, tbuf, me, kk, q)

    def seed(me, kk, q):
        r = rows(kk, i)
        c = col(me, q)
        total = collect(D_, me, kk, q, part[r, c]) + tbuf[r, c].astype(F32)
        gbuf[r, c] = (curv[r, c].astype(F32) * total.astype(BF).astype(F32)).astype(BF)
        spread(1, gbuf, me, kk, q)

    def hand(me, kk, q, start):
        dd = 2 * q + me
        src = grow.at[kk, q]
        dst = gall.at[kk, own_rows()]

        if start:
            for k in far:
                remote(src, dst, h_send.at[kk, q], h_recv.at[kk], at(dd, 0, peer(i, k, T))).start()
        else:
            sent(gall.at[kk, 0 : (T - 1) * blk], h_send.at[kk, q])

        def direct():
            if start:
                remote(src, dst, h_self.at[kk, q], h_recv.at[kk], at(dd, 0, i)).start()
            else:
                sent(src, h_self.at[kk, q])

        if me == 1:
            direct()
        else:
            pl.when(d != dd)(direct)
            if start:

                @pl.when(d == dd)
                def _():
                    gall[kk, own_rows()] = grow[kk, q]

    def adjoint(me, kk, xr, gn, rr):
        weight = None
        for q in subs:
            c = col(me, q)
            local = f_src[1, q, rows(kk, i), cw(F_, q)].astype(F32) if me == 1 else None
            total = collect(F_, me, kk, q, local)
            if q == 0:
                weight = jnp.sum(total[:, wide:], axis=-1, keepdims=True) * (rr * rr * (2.0 / 128 / width))
                total = total[:, :wide]
            g1 = gbuf[rows(kk, i), c].astype(F32) + (rr * gn[:, c]) * total - xr[:, c] * weight
            grow[kk, q] = g1.astype(BF)
            hand(me, kk, q, True)

    @pl.when(s == 0)
    def _():
        loads[0].wait()
        values_of(0)
        acts_of(0)
        pl.semaphore_wait(barrier, N * 2 * T - 1)
        loads[1].wait()
        for kk in range(K):
            if kk:
                values_of(kk)
                acts_of(kk)
            for y in (1, 0):
                for q in subs:
                    base = dot_nt(act[chunk(kk), :], wd[col(y, q), :])
                    a_src[y, q, chunk(kk), :] = base.astype(BF)
                    if y == 1:
                        hop(A, kk, q)
                    else:
                        part[chunk(kk), col(y, q)] = base
                        scatter(A, 0, kk, q)
        for k in range(1, N):
            copy_act(k, d).start()
        actall[d] = act[...]
        for kk in range(K):
            for q in subs:
                tangent(0, kk, q)
        for copy in lend:
            copy.wait_recv()
        loads[2].wait()
        loads[3].wait()
        for kk in range(K):
            for q in subs:
                scatter(D_, 0, kk, q)
            for q in subs:
                seed(0, kk, q)
        gn = gain1[...]
        for kk in reversed(range(K)):
            xr = xrow[kk].astype(F32)
            rr = rnorm_of(xr)
            for q in subs:
                scatter(F_, 0, kk, q)
            adjoint(0, kk, xr, gn, rr)
        for k in range(1, N):
            copy_act(k, peer(d, N - k, N)).wait_recv()
        for n, kk in enumerate(reversed(range(K))):

            @pl.when(lax.rem(d, 2) == 0)
            def _():
                landed(gall.at[kk, 0 : N * ck - blk], h_recv.at[kk])

            @pl.when(lax.rem(d, 2) == 1)
            def _():
                landed(gall.at[kk], h_recv.at[kk])

            more = dot_tn(
                gall[kk], actall[:, chunk(kk), :].reshape(N * ck, act.shape[1])
            )
            if n:
                prod_ref[...] = prod_ref[...] + more
            else:
                prod_ref[...] = more
        for kk in range(K):
            for q in subs:
                hop_done(A, kk, q)
                for p in (A, D_, F_):
                    scatter_done(p, kk, q)
                spread_done(0, tbuf, 0, kk, q)
                spread_done(1, gbuf, 0, kk, q)
                hand(0, kk, q, False)

    @pl.when(s == 1)
    def _():
        loads[0].wait()
        for kk in range(K):
            values_of(kk)
            acts_of(kk)
        pl.semaphore_wait(barrier, N * 2 * T - 1)
        for copy in lend:
            copy.start()
        for k in range(1, N):
            copy_act(k, d).start()
        actall[d] = act[...]
        loads[1].wait()
        for y in (0, 1):
            for q in subs:
                part[:, col(y, q)] = dot_nt(act[...], wd[col(y, q), :])
        loads[2].wait()
        loads[3].wait()
        for kk in range(K):
            for q in subs:
                scatter(A, 1, kk, q)
            for q in subs:
                r = rows(kk, i)
                c = col(1, q)
                tb = collect(A, 1, kk, q, None).astype(BF)
                tbuf[r, c] = tb
                spread(0, tbuf, 1, kk, q)
        for kk in range(K):
            r = chunk(kk)
            tv = None
            mean = None
            for q in subs:
                for y in (1, 0):
                    gathered(0, tbuf, y, kk, q)
                    c = col(y, q)
                    tf = tbuf[r, c].astype(F32)
                    dotted = jnp.sum(x_ref[r, c].astype(F32) * tf, axis=-1, keepdims=True)
                    more = dot_nt((gain[:, c] * tf).astype(BF), wv[:, c])
                    tv = more if tv is None else tv + more
                    mean = dotted if mean is None else mean + dotted
            rr = rnorm_of(x_ref[r, :].astype(F32))
            tvals[r, :] = (rr * tv - (rr * rr * (1.0 / width) * mean) * vals[r, :].astype(F32)).astype(BF)
            tmix = mix(kk, tvals)
            for y in (0, 1):
                for q in subs:
                    c = col(y, q)
                    more = part[r, c] + dot_nt(tmix, wo[c, :])
                    part[r, c] = more
                    d_src[y, q, r, :] = more.astype(BF)
                    if y == 0:
                        hop(D_, kk, q)
                    else:
                        scatter(D_, 1, kk, q)
        for kk in range(K):
            for q in subs:
                seed(1, kk, q)

        def copy_x(kk, k):
            dd = peer(d, k, N)
            return remote(
                gbuf.at[chunk(kk), feats_at(dd)], gall.at[kk, seq_rows()], x_send.at[kk], x_recv.at[kk], at(dd, s, i)
            )

        gms = []
        for kk in range(K):
            gm = None
            for q in subs:
                for y in (1, 0):
                    gathered(1, gbuf, y, kk, q)
                    c = col(y, q)
                    more = dot_nn(gbuf[chunk(kk), c], wo[c, :])
                    gm = more if gm is None else gm + more
            gms.append(gm.astype(BF))
        pending = None
        for kk in reversed(range(K)):
            r = chunk(kk)
            more = jnp.concatenate(
                [dot_tn(probs_ref[h, r, :], gms[kk][:, h * hd : (h + 1) * hd]) for h in range(heads)], axis=1
            )
            pending = more if pending is None else pending + more
            gv = pending[r, :].astype(BF)
            weight = jnp.sum(gv.astype(F32) * vals[r, :].astype(F32), axis=-1, keepdims=True)
            high = weight.astype(BF).astype(F32)
            lane = lax.broadcasted_iota(jnp.int32, (ck, 128), 1)
            extra = jnp.where(lane < 64, high, weight - high).astype(BF)
            for y in (0, 1):
                for q in subs:
                    gc = dot_nn(gv, wv[:, col(y, q)])
                    f_src[y, q, r, 0:wide] = gc.astype(BF)
                    if q == 0:
                        f_src[y, q, r, wide:] = extra
                    if y == 0:
                        hop(F_, kk, q)
                    else:
                        scatter(F_, 1, kk, q)
        for kk in range(K):
            for k in range(1, N):
                copy_x(kk, k).start()
        for kk in reversed(range(K)):
            xr = x_ref[rows(kk, i), :].astype(F32)
            adjoint(1, kk, xr, gain, rnorm_of(xr))
        for kk in range(K):
            gall[kk, seq_rows()] = gbuf[chunk(kk), feats_at(d)]
        for k in range(1, N):
            copy_act(k, peer(d, N - k, N)).wait_recv()
        for kk in range(K):
            landed(gall.at[kk, 0 : (N - 1) * ck], x_recv.at[kk])
        total = None
        for kk in range(K):
            more = dot_tn(
                gall[kk], actall[:, chunk(kk), :].reshape(N * ck, act.shape[1])
            )
            total = more if total is None else total + more
        prod_ref[...] = total
        for copy in lend:
            copy.wait_send()
        for kk in range(K):
            sent(gall.at[kk, 0 : (N - 1) * ck], x_send.at[kk])
            for q in subs:
                hop_done(D_, kk, q)
                hop_done(F_, kk, q)
                for p in (A, D_, F_):
                    scatter_done(p, kk, q)
                spread_done(0, tbuf, 1, kk, q)
                spread_done(1, gbuf, 1, kk, q)
                hand(1, kk, q, False)

    for k in range(1, N):
        copy_act(k, d).wait_send()


def call_pair(T, N, x, norm_gain, probs, w_val, w_dir, w_out, curvature):
    tok, width = x.shape
    hf = w_val.shape[0]
    K = TOKEN_CHUNKS
    Q = N // 2
    ck = tok // K
    blk = ck // T
    feats = width // N
    vm = functools.partial(pl.BlockSpec, memory_space=pltpu.VMEM)
    hbm = functools.partial(pl.BlockSpec, memory_space=pl.ANY)
    sem = pltpu.SemaphoreType.DMA

    def sums(cols):
        return [
            pltpu.VMEM((2, Q, tok, cols), BF),
            pltpu.VMEM((Q, tok, cols), BF),
            pltpu.VMEM((Q, K, T - 1, blk, cols), BF),
        ]

    scratch = [
        pltpu.VMEM((hf, width), BF),
        pltpu.VMEM((width, hf), BF),
        pltpu.VMEM((width, hf), BF),
        pltpu.VMEM((tok, width), BF),
        pltpu.VMEM((tok, hf), BF),
        pltpu.VMEM((tok, hf), BF),
        pltpu.VMEM((tok, hf), BF),
        pltpu.VMEM((tok, width), F32),
        pltpu.VMEM((tok, width), BF),
        pltpu.VMEM((tok, width), BF),
        pltpu.VMEM((K, blk, width), BF),
        pltpu.VMEM((1, width), F32),
        *sums(feats), *sums(feats), *sums(feats + 128),
        pltpu.VMEM((K, Q, blk, feats), BF),
        pltpu.VMEM((N, tok, hf), BF),
        pltpu.VMEM((K, N * ck, feats), BF),
        sem((4,)),
        sem((K + 1,)), sem((K + 1,)),
        sem((N,)), sem((N,)),
        sem((3, K, Q)), sem((3, K, Q)),
        sem((3, K, Q)), sem((3, K, Q)),
        sem((2, K, Q)), sem((2, 2, K, Q)),
        sem((K, Q)), sem((K, Q)), sem((K,)),
        sem((K,)), sem((K,)),
    ]
    return pl.pallas_call(
        functools.partial(kernel_pair, T, N),
        out_shape=jax.ShapeDtypeStruct((feats, hf), F32),
        in_specs=[vm(), vm(), vm(), hbm(), hbm(), hbm(), hbm()],
        out_specs=vm(),
        scratch_shapes=scratch,
        compiler_params=pltpu.CompilerParams(
            collective_id=0, has_side_effects=True, vmem_limit_bytes=56 * 1024 * 1024
        ),
    )(x, norm_gain, probs, w_val, w_dir, w_out, curvature)


def per_device(section_input, norm_gain, value_weight, attn_probs, out_weight, direction, curvature):
    x = section_input[0]
    w_val = value_weight[0]
    w_out = out_weight[0]
    w_dir = direction[0]
    probs = attn_probs[0]
    S = lax.axis_size("section")
    T = lax.axis_size("tensor")
    N = lax.axis_size("dp")
    tok, width = x.shape
    hf = w_val.shape[0]
    rows = tok // T
    feats = width // N
    fused = feats % 128 == 0 and feats * N == width
    blocks = tok % (16 * T * TOKEN_CHUNKS) == 0
    if fused and S == 2 and T > 2 and N % 2 == 0 and blocks:
        return call_pair(T, N, x, norm_gain, probs, w_val, w_dir, w_out, curvature)[None]
    vm = functools.partial(pl.BlockSpec, memory_space=pltpu.VMEM)
    hbm = functools.partial(pl.BlockSpec, memory_space=pl.ANY)
    if fused:
        outs = jax.ShapeDtypeStruct((feats, hf), F32)
        out_specs = vm()
    else:
        outs = (jax.ShapeDtypeStruct((tok, width), BF), jax.ShapeDtypeStruct((tok, hf), BF))
        out_specs = (vm(), vm())
    sem = pltpu.SemaphoreType.DMA
    wide = N if fused else 1
    scratch = [
        pltpu.VMEM((hf, width), BF),
        pltpu.VMEM((width, hf), BF),
        pltpu.VMEM((width, hf), BF),
        pltpu.VMEM((tok, width), BF),
        pltpu.VMEM((tok, hf), BF),
        pltpu.VMEM((tok, width), F32),
        pltpu.VMEM((tok, width), BF),
        pltpu.VMEM((T, rows, width), BF),
        pltpu.VMEM((T, rows, width), BF),
        pltpu.VMEM((T, rows, width), BF),
        pltpu.VMEM((tok, width), BF),
        pltpu.VMEM((tok, width), BF),
        pltpu.VMEM((tok, width), BF),
        pltpu.VMEM((tok, width), BF),
        pltpu.VMEM((rows, width), F32),
        pltpu.VMEM((rows, width), BF),
        pltpu.VMEM((wide, tok, hf), BF),
        pltpu.VMEM((wide, tok, feats if fused else 128), BF),
        sem((4,)),
        sem((N,)), sem((N,)),
        sem((T,)), sem((T,)),
        sem((T,)), sem((T,)),
        sem((T,)), sem((T,)),
        sem((T,)), sem((T,)),
        sem((T,)), sem((T,)),
        sem((wide, T)), sem((wide, T)),
        sem((N,)), sem((N,)),
    ]
    result = pl.pallas_call(
        functools.partial(kernel, fused, S, T, N),
        out_shape=outs,
        in_specs=[vm(), vm(), vm(), hbm(), hbm(), hbm(), hbm()],
        out_specs=out_specs,
        scratch_shapes=scratch,
        compiler_params=pltpu.CompilerParams(
            collective_id=0, has_side_effects=True, vmem_limit_bytes=56 * 1024 * 1024
        ),
    )(x, norm_gain, probs, w_val, w_dir, w_out, curvature)
    if fused:
        return result[None]
    adjoint, act = result
    product = lax.psum_scatter(
        dot_tn(adjoint, act).astype(BF), "dp", scatter_dimension=0, tiled=True
    ).astype(F32)
    return product[None]


def solution(mesh):
    in_specs = (
        P("section", "dp", None),
        P("section", None),
        P("section", "tensor", None),
        P("section", "tensor", "dp", None),
        P("section", None, "tensor"),
        P("section", None, "tensor"),
        P("dp", None),
    )
    out_specs = P("section", "dp", "tensor")
    return jax.shard_map(
        per_device, mesh=mesh, in_specs=in_specs, out_specs=out_specs, check_vma=False
    )
```

```python
import functools

import jax
import jax.numpy as jnp
from jax import lax
from jax.experimental import pallas as pl
from jax.experimental.pallas import tpu as pltpu
from jax.sharding import PartitionSpec as P

MESH = pl.DeviceIdType.MESH
BF = jnp.bfloat16
F32 = jnp.float32
TOKEN_CHUNKS = 2
MORE = (1, 0)
RELAY = (False, False)


def dot_nt(a, b):
    return lax.dot_general(a, b, (((1,), (1,)), ((), ())), preferred_element_type=F32)


def dot_tn(a, b):
    return lax.dot_general(a, b, (((0,), (0,)), ((), ())), preferred_element_type=F32)


def dot_nn(a, b):
    return lax.dot_general(a, b, (((1,), (0,)), ((), ())), preferred_element_type=F32)


def kernel(
    fused, S, T, N,
    x_ref, gain_ref, probs_ref, wv_hbm, wd_hbm, wo_hbm, curv_hbm,
    *rest,
):
    if fused:
        prod_ref, rest = rest[0], rest[1:]
    else:
        gout_ref, actout_ref, rest = rest[0], rest[1], rest[2:]
    (
        wv, wd, wo, curv, act, part, partb, in_a, in_d, in_f, gpartb, normed, tn, gfull, trow, grow,
        actall, gall,
        load_sem, act_send, act_recv, a_send, a_recv, tn_send, tn_recv, d_send, d_recv,
        s_send, s_recv, f_send, f_recv, h_send, h_recv, x_send, x_recv,
    ) = rest
    d = lax.axis_index("dp")
    s = lax.axis_index("section")
    i = lax.axis_index("tensor")
    tok, width = x_ref.shape
    rows = tok // T
    heads = probs_ref.shape[0]
    hd = wv.shape[0] // heads
    feats = width // N
    CH = 512 if width % 512 == 0 else width
    chunks = [slice(c, c + CH) for c in range(0, width, CH)]

    def rows_at(j):
        return pl.ds(pl.multiple_of(j * rows, rows), rows)

    def feats_at(j):
        return pl.ds(pl.multiple_of(j * feats, 128), feats)

    def peer(me, k, n):
        return lax.rem(me + k, n)

    loads = [
        pltpu.make_async_copy(src, dst, load_sem.at[k])
        for k, (src, dst) in enumerate(((wv_hbm, wv), (wd_hbm, wd), (wo_hbm, wo), (curv_hbm, curv)))
    ]
    for copy in loads:
        copy.start()

    barrier = pltpu.get_barrier_semaphore()

    def greet(dev):
        pl.semaphore_signal(barrier, inc=1, device_id=dev, device_id_type=MESH)

    for k in range(1, T):
        greet({"dp": d, "section": s, "tensor": peer(i, k, T)})
    for k in range(1, N):
        greet({"dp": peer(d, k, N), "section": s, "tensor": i})
    for low in range(S - 1):
        wide = N if (fused and low == 0) else 1

        @pl.when(s == low)
        def _():
            for k in range(wide):
                for j in range(T):
                    greet({"dp": peer(d, k, N), "section": s + 1, "tensor": j})

        @pl.when(s == low + 1)
        def _():
            for k in range(wide):
                for j in range(T):
                    greet({"dp": peer(d, k, N), "section": s - 1, "tensor": j})

    gain = gain_ref[...]
    xf = x_ref[...].astype(F32)
    rnorm = lax.rsqrt(jnp.mean(xf * xf, axis=-1, keepdims=True) + 1e-06)
    normed[...] = (xf * rnorm * gain).astype(BF)

    def mix(vals):
        return jnp.concatenate(
            [dot_nn(probs_ref[h], vals[:, h * hd : (h + 1) * hd]) for h in range(heads)], axis=1
        )

    loads[0].wait()
    act[...] = mix(dot_nt(normed[...], wv[...]).astype(BF)).astype(BF)

    for here in range(S):
        count = T - 1 + N - 1
        for low in (here - 1, here):
            if 0 <= low < S - 1:
                count += T * (N if (fused and low == 0) else 1)

        @pl.when(s == here)
        def _():
            pl.semaphore_wait(barrier, count)

    def remote(src, dst, send, recv, dev):
        return pltpu.make_async_remote_copy(
            src_ref=src, dst_ref=dst, send_sem=send, recv_sem=recv,
            device_id=dev, device_id_type=MESH,
        )

    def at(dd, ss, jj):
        return {"dp": dd, "section": ss, "tensor": jj}

    def copy_act(k, owner):
        return remote(act, actall.at[owner], act_send.at[k], act_recv.at[k], at(peer(d, k, N), s, i))

    def copy_a(j, owner):
        return remote(partb.at[rows_at(j)], in_a.at[owner], a_send.at[j], a_recv.at[owner], at(d, s + 1, j))

    def copy_tn(k, owner):
        return remote(
            tn.at[rows_at(owner)], tn.at[rows_at(owner)], tn_send.at[k], tn_recv.at[k], at(d, s, peer(i, k, T))
        )

    def copy_d(k):
        j = peer(i, k, T)
        return remote(partb.at[rows_at(j)], in_d.at[k - 1], d_send.at[k], d_recv.at[k], at(d, s, j))

    def copy_s(k, owner):
        return remote(
            gfull.at[rows_at(owner)], gfull.at[rows_at(owner)], s_send.at[k], s_recv.at[k],
            at(d, s, peer(i, k, T)),
        )

    def copy_f(k):
        j = peer(i, k, T)
        return remote(gpartb.at[rows_at(j)], in_f.at[k - 1], f_send.at[k], f_recv.at[k], at(d, s, j))

    def copy_h(j, owner):
        return remote(grow, gfull.at[rows_at(owner)], h_send.at[0, j], h_recv.at[0, owner], at(d, s - 1, j))

    def copy_hd(k, j, owner):
        dd = peer(d, k, N)
        return remote(
            grow.at[:, feats_at(dd)], gall.at[lax.rem(d, N), rows_at(owner)],
            h_send.at[k, j], h_recv.at[k, owner], at(dd, s - 1, j),
        )

    def land_hd(k, owner):
        src = peer(d, N - k, N)
        return remote(
            grow.at[:, feats_at(d)], gall.at[src, rows_at(owner)],
            h_send.at[k, owner], h_recv.at[k, owner], at(d, s, i),
        )

    def copy_x(k):
        dd = peer(d, k, N)
        return remote(gfull.at[:, feats_at(dd)], gall.at[d], x_send.at[k], x_recv.at[k], at(dd, s, i))

    def land_x(k):
        src = peer(d, N - k, N)
        return remote(gfull.at[:, feats_at(d)], gall.at[src], x_send.at[k], x_recv.at[k], at(d, s, i))

    if fused:
        for k in range(1, N):
            copy_act(k, d).start()
        actall[d] = act[...]

    xrows = x_ref[rows_at(i)].astype(F32)
    rrows = lax.rsqrt(jnp.mean(xrows * xrows, axis=-1, keepdims=True) + 1e-06)

    loads[1].wait()
    for c in chunks:
        base = dot_nt(act[...], wd[c, :])
        part[:, c] = base

    loads[2].wait()
    loads[3].wait()

    @pl.when(s == 0)
    def _():
        partb[...] = part[...].astype(BF)

    @pl.when(s > 0)
    def _():
        total = None
        for j in range(T):
            remote(partb.at[rows_at(j)], in_a.at[j], a_send.at[j], a_recv.at[j], at(d, s, i)).wait_recv()
        for j in range(T):
            piece = in_a[j].astype(F32)
            total = piece if total is None else total + piece
        tfloat = total.astype(BF).astype(F32)
        trow[...] = tfloat
        tn[rows_at(i)] = (
            gain * (rrows * tfloat - rrows**3 * xrows * jnp.mean(xrows * tfloat, axis=-1, keepdims=True))
        ).astype(BF)
        for k in range(1, T):
            copy_tn(k, i).start()
        for k in range(1, T):
            copy_tn(k, peer(i, T - k, T)).wait_recv()
        tmix = mix(dot_nt(tn[...], wv[...]).astype(BF)).astype(BF)
        for c in chunks:
            part[:, c] = part[:, c] + dot_nt(tmix, wo[c, :])
        part[rows_at(i)] = part[rows_at(i)] + trow[...]
        partb[...] = part[...].astype(BF)
        for k in range(1, T):
            copy_tn(k, i).wait_send()

    if S > 1:

        @pl.when(s < S - 1)
        def _():
            for j in range(T):
                copy_a(j, i).start()

    @pl.when(s == S - 1)
    def _():
        for k in range(1, T):
            copy_d(k).start()
        total = part[rows_at(i)]
        for k in range(1, T):
            copy_d(k).wait_recv()
        for k in range(1, T):
            total = total + in_d[k - 1].astype(F32)
        tlast = total.astype(BF).astype(F32)
        gfull[rows_at(i)] = (curv[rows_at(i)].astype(F32) * tlast).astype(BF)
        for k in range(1, T):
            copy_s(k, i).start()
        for k in range(1, T):
            copy_s(k, peer(i, T - k, T)).wait_recv()
        for k in range(1, T):
            copy_s(k, i).wait_send()
            copy_d(k).wait_send()

    if S > 1:

        @pl.when(s < S - 1)
        def _():
            for j in range(T):
                copy_a(j, i).wait_send()

        def gather_rows():
            for j in range(T):
                remote(grow, gfull.at[rows_at(j)], h_send.at[0, j], h_recv.at[0, j], at(d, s, i)).wait_recv()

        if fused:
            if S > 2:

                @pl.when(jnp.logical_and(s > 0, s < S - 1))
                def _():
                    gather_rows()

            @pl.when(s == 0)
            def _():
                for k in range(N):
                    for j in range(T):
                        land_hd(k, j).wait_recv()
        else:

            @pl.when(s < S - 1)
            def _():
                gather_rows()

        @pl.when(s > 0)
        def _():
            gm = dot_nn(gfull[...], wo[...]).astype(BF)
            gv = jnp.concatenate(
                [dot_tn(probs_ref[h], gm[:, h * hd : (h + 1) * hd]) for h in range(heads)], axis=1
            ).astype(BF)
            for c in chunks:
                gc = dot_nn(gv, wv[:, c])
                part[:, c] = gc
                gpartb[:, c] = gc.astype(BF)
            for k in range(1, T):
                copy_f(k).start()
            total = part[rows_at(i)]
            for k in range(1, T):
                copy_f(k).wait_recv()
            for k in range(1, T):
                total = total + in_f[k - 1].astype(F32)
            scaled = gain * total
            gx = rrows * scaled - rrows**3 * xrows * jnp.mean(xrows * scaled, axis=-1, keepdims=True)
            grow[...] = (gfull[rows_at(i)].astype(F32) + gx).astype(BF)

            def plain():
                for j in range(T):
                    copy_h(j, i).start()
                for j in range(T):
                    copy_h(j, i).wait_send()

            if fused:

                @pl.when(s == 1)
                def _():
                    for k in range(N):
                        for j in range(T):
                            copy_hd(k, j, i).start()
                    for k in range(N):
                        for j in range(T):
                            copy_hd(k, j, i).wait_send()

                if S > 2:
                    pl.when(s > 1)(plain)
            else:
                plain()
            for k in range(1, T):
                copy_f(k).wait_send()

    if fused:

        def spread():
            for k in range(1, N):
                copy_x(k).start()
            gall[d] = gfull[:, feats_at(d)]
            for k in range(1, N):
                land_x(k).wait_recv()
            for k in range(1, N):
                copy_x(k).wait_send()

        if S > 1:
            pl.when(s > 0)(spread)
        else:
            spread()
        for k in range(1, N):
            copy_act(k, peer(d, N - k, N)).wait_recv()
        prod_ref[...] = dot_tn(
            gall[...].reshape(N * tok, feats), actall[...].reshape(N * tok, act.shape[1])
        )
        for k in range(1, N):
            copy_act(k, d).wait_send()
    else:
        gout_ref[...] = gfull[...]
        actout_ref[...] = act[...]


def home_share(feats, g, q):
    more = 1 if MORE[g] > 0 else -1
    return (feats // 256 + (more if q < abs(MORE[g]) else 0)) * 128


def kernel_pair(
    T, N,
    x_ref, gain_ref, probs_ref, wv_hbm, wd_hbm, wo_hbm, curv_hbm,
    gall, actall,
    wv, wd, wo, curv, act, vals, tvals, part, tbuf, gbuf, xrow, gain1,
    a_src, a_hop, a_land, d_src, d_hop, d_land, f_src, f_hop, f_land,
    grow,
    load_sem, lend_send, lend_recv, act_send, act_recv,
    hop_send, hop_recv, rs_send, rs_recv, ag_send, ag_recv, ag_pass, pass_send,
    h_send, h_self, h_recv, x_send, x_recv,
):
    d = lax.axis_index("dp")
    s = lax.axis_index("section")
    i = lax.axis_index("tensor")
    tok, width = x_ref.shape
    K = TOKEN_CHUNKS
    Q = N
    ck = tok // K
    blk = ck // T
    feats = width // N
    heads = probs_ref.shape[0]
    hd = wv.shape[0] // heads
    end = jnp.logical_or(i == 0, i == T - 1)
    mid = jnp.logical_not(end)
    mate = jnp.bitwise_xor(i, 1)
    cross = jnp.where(end, T - 1 - mate, T - 1 - i)
    other = T - 1 - mate
    far = [k for k in range(2, T - 1)] + [k for k in range(1, T) if k in (1, T - 1)]
    subs = range(Q)

    def peer(me, k, n):
        return lax.rem(me + k, n)

    def at(dd, ss, jj):
        return {"dp": dd, "section": ss, "tensor": jj}

    def chunk(kk):
        return slice(kk * ck, (kk + 1) * ck)

    def rows(kk, j):
        return pl.ds(pl.multiple_of(kk * ck + j * blk, blk), blk)

    def share(g, y, q):
        return home_share(feats, g, q) if y == g else feats - home_share(feats, g, q)

    def part_of(g, y, q):
        lo = share(g, 0, q) if y == 1 else 0
        return slice(lo, lo + share(g, y, q))

    def col(g, y, q):
        c = part_of(g, y, q)
        return slice(q * feats + c.start, q * feats + c.stop)

    def block(b):
        return slice(b * feats, (b + 1) * feats)

    def feats_at(j):
        return pl.ds(pl.multiple_of(j * feats, 128), feats)

    def seq_rows(kk):
        return pl.ds(pl.multiple_of(d * tok + kk * ck, ck), ck)

    def own_rows(kk):
        return pl.ds(pl.multiple_of(d * tok + kk * ck + i * blk, blk), blk)

    def remote(src, dst, send, recv, dev):
        return pltpu.make_async_remote_copy(
            src_ref=src, dst_ref=dst, send_sem=send, recv_sem=recv,
            device_id=dev, device_id_type=MESH,
        )

    def landed(ref, sem):
        remote(ref, ref, sem, sem, at(d, s, i)).wait_recv()

    def sent(ref, sem):
        remote(ref, ref, sem, sem, at(d, s, i)).wait_send()

    loads = [
        pltpu.make_async_copy(src, dst, load_sem.at[k])
        for k, (src, dst) in enumerate(((wv_hbm, wv), (wd_hbm, wd), (wo_hbm, wo), (curv_hbm, curv)))
    ]
    loads[0].start()
    loads[1].start()

    barrier = pltpu.get_barrier_semaphore()
    for a in range(N):
        for b in range(2):
            for c in range(T):
                if a or b or c:
                    pl.semaphore_signal(
                        barrier, inc=1, device_id=at(peer(d, a, N), peer(s, b, 2), peer(i, c, T)),
                        device_id_type=MESH,
                    )
    loads[2].start()
    loads[3].start()

    def mix(kk, buf):
        r = chunk(kk)
        return jnp.concatenate(
            [dot_nn(probs_ref[h, r, :], buf[:, h * hd : (h + 1) * hd]) for h in range(heads)], axis=1
        ).astype(BF)

    def rnorm_of(xf):
        return lax.rsqrt(jnp.mean(xf * xf, axis=-1, keepdims=True) + 1e-06)

    gain = gain_ref[...]

    def values_of(kk):
        r = chunk(kk)
        xf = x_ref[r, :].astype(F32)
        normed = (xf * rnorm_of(xf) * gain).astype(BF)
        vals[r, :] = dot_nt(normed, wv[...]).astype(BF)

    def acts_of(kk):
        act[chunk(kk), :] = mix(kk, vals)

    for kk in range(1, K):
        vals[chunk(kk), :] = jnp.zeros((ck, vals.shape[1]), BF)
        tvals[chunk(kk), :] = jnp.zeros((ck, vals.shape[1]), BF)

    def copy_act(k, owner):
        return remote(act, actall.at[owner], act_send.at[k], act_recv.at[k], at(peer(d, k, N), s, i))

    keep_act = pltpu.make_async_copy(act, actall.at[d], act_send.at[0])

    def keep_rows(kk):
        return pltpu.make_async_copy(gbuf.at[chunk(kk), feats_at(d)], gall.at[seq_rows(kk)], x_send.at[K + kk])

    lend = [
        remote(x_ref.at[rows(kk, i)], xrow.at[kk], lend_send.at[kk], lend_recv.at[kk], at(d, 0, i))
        for kk in range(K)
    ] + [remote(gain_ref, gain1, lend_send.at[K], lend_recv.at[K], at(d, 0, i))]

    A, D_, F_ = (0, a_src, a_hop, a_land, 0), (1, d_src, d_hop, d_land, 1), (2, f_src, f_hop, f_land, 1)

    def cw(p, y, q):
        return slice(0, share(p[4], y, q) + (128 if p[0] == 2 and q == 0 else 0))

    def hop(p, kk, q):
        y = 1 - p[4]
        c = cw(p, y, q)
        r = chunk(kk)
        remote(
            p[1].at[y, q, r, c], p[2].at[q, r, c], hop_send.at[p[0], kk, q], hop_recv.at[p[0], kk, q], at(d, y, i)
        ).start()

    def hop_done(p, kk, q):
        sent(p[1].at[1 - p[4], q, chunk(kk), cw(p, 1 - p[4], q)], hop_send.at[p[0], kk, q])

    def scatter(p, me, kk, q):
        c = cw(p, me, q)
        if me != p[4]:
            landed(p[2].at[q, chunk(kk), c], hop_recv.at[p[0], kk, q])
        buf = p[1].at[me, q] if me == p[4] else p[2].at[q]
        for k in far:
            j = peer(i, k, T)
            remote(
                buf.at[rows(kk, j), c], p[3].at[q, kk, k - 1, :, c], rs_send.at[p[0], kk, q],
                rs_recv.at[p[0], kk, q], at(d, me, j),
            ).start()

    def scatter_done(p, me, kk, q):
        sent(p[3].at[q, kk, :, :, cw(p, me, q)], rs_send.at[p[0], kk, q])

    def collect(p, me, kk, q, local):
        c = cw(p, me, q)
        total = p[2][q, rows(kk, i), c].astype(F32) if me != p[4] else local
        landed(p[3].at[q, kk, :, :, c], rs_recv.at[p[0], kk, q])
        for k in range(T - 1):
            total = total + p[3][q, kk, k, :, c].astype(F32)
        return total

    def spread_copies(n, buf, me, kk, q):
        src = buf.at[rows(kk, i), col(n, me, q)]
        if not RELAY[n]:
            return [
                remote(src, src, ag_send.at[n, kk, q, k], ag_recv.at[n, me, kk, q], at(d, 1, peer(i, k, T)))
                for k in far + ([0] if me == 0 else [])
            ]
        out = [
            remote(src, src, ag_send.at[n, kk, q, 1], ag_pass.at[n, me, kk, q], at(d, me, cross)),
            remote(src, src, ag_send.at[n, kk, q, 2], ag_recv.at[n, me, kk, q], at(d, 1, mate)),
        ]
        if me == 0:
            out.append(remote(src, src, ag_send.at[n, kk, q, 0], ag_recv.at[n, me, kk, q], at(d, 1, i)))
        return out

    def pass_copies(n, buf, me, kk, q):
        out = []
        for m, j in ((0, cross), (1, other)):
            src = buf.at[rows(kk, j), col(n, me, q)]
            land = ag_pass if me == 1 else ag_recv
            out.append(remote(src, src, pass_send.at[n, kk, q, m], land.at[n, me, kk, q], at(d, 1, mate)))
            if me == 0:
                out.append(remote(src, src, pass_send.at[n, kk, q, 2 + m], land.at[n, me, kk, q], at(d, 1, i)))
        return out

    def spread(n, buf, me, kk, q):
        for copy in spread_copies(n, buf, me, kk, q):
            copy.start()

    def pass_on(n, buf, me, kk, q):
        if not RELAY[n]:
            return
        pair = buf.at[kk * ck : kk * ck + 2 * blk, col(n, me, q)]
        if me == 1:
            landed(pair, ag_pass.at[n, me, kk, q])

        @pl.when(mid)
        def _():
            if me == 0:
                landed(pair, ag_pass.at[n, me, kk, q])
            for copy in pass_copies(n, buf, me, kk, q):
                copy.start()

    def spread_done(n, buf, me, kk, q):
        for copy in spread_copies(n, buf, me, kk, q):
            copy.wait_send()
        if RELAY[n]:

            @pl.when(mid)
            def _():
                for copy in pass_copies(n, buf, me, kk, q):
                    copy.wait_send()

    def gathered(n, buf, y, kk, q):
        count = T if y == 0 else T - 1
        if RELAY[n] and y == 1:
            pass_on(n, buf, 1, kk, q)
            count = 1
        landed(buf.at[kk * ck : kk * ck + count * blk, col(n, y, q)], ag_recv.at[n, y, kk, q])

    def ready(n, buf, kk, b):
        for y in (1, 0):
            gathered(n, buf, y, kk, b)

    def pack(p, buf, kk, b):
        home = p[4]
        for y in (1 - home, home):
            p[1][y, b, chunk(kk), 0 : share(home, y, b)] = buf[chunk(kk), col(home, y, b)].astype(BF)
            if y == home:
                scatter(p, home, kk, b)
            else:
                hop(p, kk, b)

    def done(me, sums, gathers):
        for kk in range(K):
            for q in subs:
                for p in sums:
                    if me == p[4]:
                        hop_done(p, kk, q)
                    scatter_done(p, me, kk, q)
                for n, buf in gathers:
                    spread_done(n, buf, me, kk, q)

    def tangent(me, kk, q):
        r = rows(kk, i)
        c = col(0, me, q)
        tbuf[r, c] = collect(A, me, kk, q, part[r, c]).astype(BF)
        spread(0, tbuf, me, kk, q)

    def seed(me, kk, q):
        r = rows(kk, i)
        c = col(1, me, q)
        total = collect(D_, me, kk, q, part[r, c])
        gbuf[r, c] = (curv[r, c].astype(F32) * total.astype(BF).astype(F32)).astype(BF)
        spread(1, gbuf, me, kk, q)

    def hand(me, kk, q, start):
        dd = q
        c = part_of(1, me, q)
        src = grow.at[kk, q, :, 0 : share(1, me, q)]
        dst = gall.at[own_rows(kk), c]

        if start:
            for k in far:
                remote(src, dst, h_send.at[kk, q], h_recv.at[kk, me], at(dd, 0, peer(i, k, T))).start()
        else:
            sent(gall.at[0 : (T - 1) * blk, c], h_send.at[kk, q])

        def direct():
            if start:
                remote(src, dst, h_self.at[kk, q], h_recv.at[kk, me], at(dd, 0, i)).start()
            else:
                sent(src, h_self.at[kk, q])

        if me == 1:
            direct()
        else:
            pl.when(d != dd)(direct)

            @pl.when(d == dd)
            def _():
                own = pltpu.make_async_copy(src, dst, h_self.at[kk, q])
                own.start() if start else own.wait()

    def adjoint(me, kk, xr, gn, rr):
        weight = None
        for q in subs:
            c = col(1, me, q)
            wide = share(1, me, q)
            local = f_src[1, q, rows(kk, i), cw(F_, 1, q)].astype(F32) if me == 1 else None
            total = collect(F_, me, kk, q, local)
            if q == 0:
                weight = jnp.sum(total[:, wide:], axis=-1, keepdims=True) * (rr * rr * (2.0 / 128 / width))
                total = total[:, :wide]
            g1 = gbuf[rows(kk, i), c].astype(F32) + (rr * gn[:, c]) * total - xr[:, c] * weight
            grow[kk, q, :, 0:wide] = g1.astype(BF)
            hand(me, kk, q, True)

    @pl.when(s == 0)
    def _():
        loads[0].wait()
        values_of(0)
        acts_of(0)
        pl.semaphore_wait(barrier, N * 2 * T - 1)
        loads[1].wait()
        for kk in range(K):
            if kk:
                values_of(kk)
                acts_of(kk)
            for b in range(N):
                part[chunk(kk), block(b)] = dot_nt(act[chunk(kk), :], wd[block(b), :])
                pack(A, part, kk, b)
        for k in range(1, N):
            copy_act(k, d).start()
        keep_act.start()
        for kk in range(K):
            for q in subs:
                tangent(0, kk, q)
        for kk in range(K):
            for q in subs:
                pass_on(0, tbuf, 0, kk, q)
        for copy in lend:
            copy.wait_recv()
        loads[2].wait()
        loads[3].wait()
        for kk in range(K):
            for q in subs:
                scatter(D_, 0, kk, q)
        done(0, (A,), ())
        for kk in range(K):
            for q in subs:
                seed(0, kk, q)
        for kk in range(K):
            for q in subs:
                pass_on(1, gbuf, 0, kk, q)
        done(0, (), ((0, tbuf),))
        for k in range(1, N):
            copy_act(k, d).wait_send()
        keep_act.wait()
        gn = gain1[...]
        for kk in reversed(range(K)):
            for q in subs:
                scatter(F_, 0, kk, q)
        done(0, (D_,), ((1, gbuf),))
        for kk in reversed(range(K)):
            xr = xrow[kk].astype(F32)
            rr = rnorm_of(xr)
            adjoint(0, kk, xr, gn, rr)
        for k in range(1, N):
            copy_act(k, peer(d, N - k, N)).wait_recv()
        done(0, (F_,), ())
        for kk in reversed(range(K)):
            for q in subs:
                hand(0, kk, q, False)
        for n, kk in enumerate(reversed(range(K))):

            for dd in range(N):

                @pl.when(d == dd)
                def _():
                    landed(gall.at[0 : N * ck - blk, part_of(1, 0, dd)], h_recv.at[kk, 0])
                    landed(gall.at[0 : N * ck, part_of(1, 1, dd)], h_recv.at[kk, 1])

    @pl.when(s == 1)
    def _():
        loads[0].wait()
        for kk in range(K):
            values_of(kk)
            acts_of(kk)
        pl.semaphore_wait(barrier, N * 2 * T - 1)
        for copy in lend:
            copy.start()
        for k in range(1, N):
            copy_act(k, d).start()
        keep_act.start()
        loads[1].wait()
        for b in range(N):
            part[:, block(b)] = dot_nt(act[...], wd[block(b), :])
        loads[2].wait()
        loads[3].wait()
        for kk in range(K):
            for q in subs:
                scatter(A, 1, kk, q)
        for kk in range(K):
            for q in subs:
                tangent(1, kk, q)
        for kk in range(K):
            r = chunk(kk)
            tv = None
            mean = None
            for b in range(N):
                ready(0, tbuf, kk, b)
                c = block(b)
                tf = tbuf[r, c].astype(F32)
                dotted = jnp.sum(x_ref[r, c].astype(F32) * tf, axis=-1, keepdims=True)
                more = dot_nt((gain[:, c] * tf).astype(BF), wv[:, c])
                tv = more if tv is None else tv + more
                mean = dotted if mean is None else mean + dotted
            rr = rnorm_of(x_ref[r, :].astype(F32))
            tvals[r, :] = (rr * tv - (rr * rr * (1.0 / width) * mean) * vals[r, :].astype(F32)).astype(BF)
            tmix = mix(kk, tvals)
            for b in range(N):
                part[r, block(b)] = part[r, block(b)] + dot_nt(tmix, wo[block(b), :])
                mine = rows(kk, i)
                part[mine, block(b)] = part[mine, block(b)] + tbuf[mine, block(b)].astype(F32)
                pack(D_, part, kk, b)
        for copy in lend:
            copy.wait_send()
        done(1, (A,), ())
        for kk in range(K):
            for q in subs:
                seed(1, kk, q)
        done(1, (), ((0, tbuf),))
        for k in range(1, N):
            copy_act(k, d).wait_send()
        keep_act.wait()

        def copy_x(kk, k):
            dd = peer(d, k, N)
            return remote(
                gbuf.at[chunk(kk), feats_at(dd)], gall.at[seq_rows(kk)], x_send.at[kk], x_recv.at[kk], at(dd, s, i)
            )

        gms = []
        for kk in range(K):
            gm = None
            for b in range(N):
                ready(1, gbuf, kk, b)
                more = dot_nn(gbuf[chunk(kk), block(b)], wo[block(b), :])
                gm = more if gm is None else gm + more
            gms.append(gm.astype(BF))
        pending = None
        for kk in reversed(range(K)):
            r = chunk(kk)
            more = jnp.concatenate(
                [dot_tn(probs_ref[h, r, :], gms[kk][:, h * hd : (h + 1) * hd]) for h in range(heads)], axis=1
            )
            pending = more if pending is None else pending + more
            gv = pending[r, :].astype(BF)
            weight = jnp.sum(gv.astype(F32) * vals[r, :].astype(F32), axis=-1, keepdims=True)
            high = weight.astype(BF).astype(F32)
            lane = lax.broadcasted_iota(jnp.int32, (ck, 128), 1)
            extra = jnp.where(lane < 64, high, weight - high).astype(BF)
            for y in (0, 1):
                f_src[y, 0, r, share(1, y, 0) : share(1, y, 0) + 128] = extra
            for b in range(N):
                part[r, block(b)] = dot_nn(gv, wv[:, block(b)])
                pack(F_, part, kk, b)
        for kk in range(K):
            for k in range(1, N):
                copy_x(kk, k).start()
            keep_rows(kk).start()
        done(1, (D_,), ((1, gbuf),))
        for k in range(1, N):
            copy_act(k, peer(d, N - k, N)).wait_recv()
        for kk in range(K):
            landed(gall.at[0 : (N - 1) * ck], x_recv.at[kk])
        for kk in reversed(range(K)):
            xr = x_ref[rows(kk, i), :].astype(F32)
            adjoint(1, kk, xr, gain, rnorm_of(xr))
        done(1, (F_,), ())
        for kk in range(K):
            sent(gall.at[0 : (N - 1) * ck], x_send.at[kk])
            keep_rows(kk).wait()
            for q in subs:
                hand(1, kk, q, False)


def call_pair(T, N, x, norm_gain, probs, w_val, w_dir, w_out, curvature):
    tok, width = x.shape
    hf = w_val.shape[0]
    K = TOKEN_CHUNKS
    Q = N
    ck = tok // K
    blk = ck // T
    feats = width // N
    wide = max(max(home_share(feats, g, q), feats - home_share(feats, g, q)) for g in (0, 1) for q in range(N))
    vm = functools.partial(pl.BlockSpec, memory_space=pltpu.VMEM)
    hbm = functools.partial(pl.BlockSpec, memory_space=pl.ANY)
    sem = pltpu.SemaphoreType.DMA

    def sums(cols):
        return [
            pltpu.VMEM((2, Q, tok, cols), BF),
            pltpu.VMEM((Q, tok, cols), BF),
            pltpu.VMEM((Q, K, T - 1, blk, cols), BF),
        ]

    scratch = [
        pltpu.VMEM((hf, width), BF),
        pltpu.VMEM((width, hf), BF),
        pltpu.VMEM((width, hf), BF),
        pltpu.VMEM((tok, width), BF),
        pltpu.VMEM((tok, hf), BF),
        pltpu.VMEM((tok, hf), BF),
        pltpu.VMEM((tok, hf), BF),
        pltpu.VMEM((tok, width), F32),
        pltpu.VMEM((tok, width), BF),
        pltpu.VMEM((tok, width), BF),
        pltpu.VMEM((K, blk, width), BF),
        pltpu.VMEM((1, width), F32),
        *sums(wide), *sums(wide), *sums(wide + 128),
        pltpu.VMEM((K, Q, blk, wide), BF),
        sem((4,)),
        sem((K + 1,)), sem((K + 1,)),
        sem((N,)), sem((N,)),
        sem((3, K, Q)), sem((3, K, Q)),
        sem((3, K, Q)), sem((3, K, Q)),
        sem((2, K, Q, T)), sem((2, 2, K, Q)), sem((2, 2, K, Q)), sem((2, K, Q, T)),
        sem((K, Q)), sem((K, Q)), sem((K, 2)),
        sem((2 * K,)), sem((K,)),
    ]
    adjoints, acts = pl.pallas_call(
        functools.partial(kernel_pair, T, N),
        out_shape=(
            jax.ShapeDtypeStruct((N * tok, feats), BF), jax.ShapeDtypeStruct((N, tok, hf), BF),
        ),
        in_specs=[vm(), vm(), vm(), hbm(), hbm(), hbm(), hbm()],
        out_specs=(hbm(), hbm()),
        scratch_shapes=scratch,
        compiler_params=pltpu.CompilerParams(
            collective_id=0, has_side_effects=True, vmem_limit_bytes=56 * 1024 * 1024
        ),
    )(x, norm_gain, probs, w_val, w_dir, w_out, curvature)
    return dot_tn(adjoints, acts.reshape(N * tok, hf))


def per_device(section_input, norm_gain, value_weight, attn_probs, out_weight, direction, curvature):
    x = section_input[0]
    w_val = value_weight[0]
    w_out = out_weight[0]
    w_dir = direction[0]
    probs = attn_probs[0]
    S = lax.axis_size("section")
    T = lax.axis_size("tensor")
    N = lax.axis_size("dp")
    tok, width = x.shape
    hf = w_val.shape[0]
    rows = tok // T
    feats = width // N
    fused = feats % 128 == 0 and feats * N == width
    blocks = tok % (16 * T * TOKEN_CHUNKS) == 0
    if fused and S == 2 and T == 4 and feats % 256 == 0 and blocks:
        return call_pair(T, N, x, norm_gain, probs, w_val, w_dir, w_out, curvature)[None]
    vm = functools.partial(pl.BlockSpec, memory_space=pltpu.VMEM)
    hbm = functools.partial(pl.BlockSpec, memory_space=pl.ANY)
    if fused:
        outs = jax.ShapeDtypeStruct((feats, hf), F32)
        out_specs = vm()
    else:
        outs = (jax.ShapeDtypeStruct((tok, width), BF), jax.ShapeDtypeStruct((tok, hf), BF))
        out_specs = (vm(), vm())
    sem = pltpu.SemaphoreType.DMA
    wide = N if fused else 1
    scratch = [
        pltpu.VMEM((hf, width), BF),
        pltpu.VMEM((width, hf), BF),
        pltpu.VMEM((width, hf), BF),
        pltpu.VMEM((tok, width), BF),
        pltpu.VMEM((tok, hf), BF),
        pltpu.VMEM((tok, width), F32),
        pltpu.VMEM((tok, width), BF),
        pltpu.VMEM((T, rows, width), BF),
        pltpu.VMEM((T, rows, width), BF),
        pltpu.VMEM((T, rows, width), BF),
        pltpu.VMEM((tok, width), BF),
        pltpu.VMEM((tok, width), BF),
        pltpu.VMEM((tok, width), BF),
        pltpu.VMEM((tok, width), BF),
        pltpu.VMEM((rows, width), F32),
        pltpu.VMEM((rows, width), BF),
        pltpu.VMEM((wide, tok, hf), BF),
        pltpu.VMEM((wide, tok, feats if fused else 128), BF),
        sem((4,)),
        sem((N,)), sem((N,)),
        sem((T,)), sem((T,)),
        sem((T,)), sem((T,)),
        sem((T,)), sem((T,)),
        sem((T,)), sem((T,)),
        sem((T,)), sem((T,)),
        sem((wide, T)), sem((wide, T)),
        sem((N,)), sem((N,)),
    ]
    result = pl.pallas_call(
        functools.partial(kernel, fused, S, T, N),
        out_shape=outs,
        in_specs=[vm(), vm(), vm(), hbm(), hbm(), hbm(), hbm()],
        out_specs=out_specs,
        scratch_shapes=scratch,
        compiler_params=pltpu.CompilerParams(
            collective_id=0, has_side_effects=True, vmem_limit_bytes=56 * 1024 * 1024
        ),
    )(x, norm_gain, probs, w_val, w_dir, w_out, curvature)
    if fused:
        return result[None]
    adjoint, act = result
    product = lax.psum_scatter(
        dot_tn(adjoint, act).astype(BF), "dp", scatter_dimension=0, tiled=True
    ).astype(F32)
    return product[None]


def solution(mesh):
    in_specs = (
        P("section", "dp", None),
        P("section", None),
        P("section", "tensor", None),
        P("section", "tensor", "dp", None),
        P("section", None, "tensor"),
        P("section", None, "tensor"),
        P("dp", None),
    )
    out_specs = P("section", "dp", "tensor")
    return jax.shard_map(
        per_device, mesh=mesh, in_specs=in_specs, out_specs=out_specs, check_vma=False
    )
```

```python
import functools

import jax
import jax.numpy as jnp
from jax import lax
from jax.experimental import pallas as pl
from jax.experimental.pallas import tpu as pltpu
from jax.sharding import PartitionSpec as P

MESH = pl.DeviceIdType.MESH
BF = jnp.bfloat16
F32 = jnp.float32
TOKEN_CHUNKS = 2
MORE = (1, 0)
RELAY = (True, False)


def dot_nt(a, b):
    return lax.dot_general(a, b, (((1,), (1,)), ((), ())), preferred_element_type=F32)


def dot_tn(a, b):
    return lax.dot_general(a, b, (((0,), (0,)), ((), ())), preferred_element_type=F32)


def dot_nn(a, b):
    return lax.dot_general(a, b, (((1,), (0,)), ((), ())), preferred_element_type=F32)


def kernel(
    fused, S, T, N,
    x_ref, gain_ref, probs_ref, wv_hbm, wd_hbm, wo_hbm, curv_hbm,
    *rest,
):
    if fused:
        prod_ref, rest = rest[0], rest[1:]
    else:
        gout_ref, actout_ref, rest = rest[0], rest[1], rest[2:]
    (
        wv, wd, wo, curv, act, part, partb, in_a, in_d, in_f, gpartb, normed, tn, gfull, trow, grow,
        actall, gall,
        load_sem, act_send, act_recv, a_send, a_recv, tn_send, tn_recv, d_send, d_recv,
        s_send, s_recv, f_send, f_recv, h_send, h_recv, x_send, x_recv,
    ) = rest
    d = lax.axis_index("dp")
    s = lax.axis_index("section")
    i = lax.axis_index("tensor")
    tok, width = x_ref.shape
    rows = tok // T
    heads = probs_ref.shape[0]
    hd = wv.shape[0] // heads
    feats = width // N
    CH = 512 if width % 512 == 0 else width
    chunks = [slice(c, c + CH) for c in range(0, width, CH)]

    def rows_at(j):
        return pl.ds(pl.multiple_of(j * rows, rows), rows)

    def feats_at(j):
        return pl.ds(pl.multiple_of(j * feats, 128), feats)

    def peer(me, k, n):
        return lax.rem(me + k, n)

    loads = [
        pltpu.make_async_copy(src, dst, load_sem.at[k])
        for k, (src, dst) in enumerate(((wv_hbm, wv), (wd_hbm, wd), (wo_hbm, wo), (curv_hbm, curv)))
    ]
    for copy in loads:
        copy.start()

    barrier = pltpu.get_barrier_semaphore()

    def greet(dev):
        pl.semaphore_signal(barrier, inc=1, device_id=dev, device_id_type=MESH)

    for k in range(1, T):
        greet({"dp": d, "section": s, "tensor": peer(i, k, T)})
    for k in range(1, N):
        greet({"dp": peer(d, k, N), "section": s, "tensor": i})
    for low in range(S - 1):
        wide = N if (fused and low == 0) else 1

        @pl.when(s == low)
        def _():
            for k in range(wide):
                for j in range(T):
                    greet({"dp": peer(d, k, N), "section": s + 1, "tensor": j})

        @pl.when(s == low + 1)
        def _():
            for k in range(wide):
                for j in range(T):
                    greet({"dp": peer(d, k, N), "section": s - 1, "tensor": j})

    gain = gain_ref[...]
    xf = x_ref[...].astype(F32)
    rnorm = lax.rsqrt(jnp.mean(xf * xf, axis=-1, keepdims=True) + 1e-06)
    normed[...] = (xf * rnorm * gain).astype(BF)

    def mix(vals):
        return jnp.concatenate(
            [dot_nn(probs_ref[h], vals[:, h * hd : (h + 1) * hd]) for h in range(heads)], axis=1
        )

    loads[0].wait()
    act[...] = mix(dot_nt(normed[...], wv[...]).astype(BF)).astype(BF)

    for here in range(S):
        count = T - 1 + N - 1
        for low in (here - 1, here):
            if 0 <= low < S - 1:
                count += T * (N if (fused and low == 0) else 1)

        @pl.when(s == here)
        def _():
            pl.semaphore_wait(barrier, count)

    def remote(src, dst, send, recv, dev):
        return pltpu.make_async_remote_copy(
            src_ref=src, dst_ref=dst, send_sem=send, recv_sem=recv,
            device_id=dev, device_id_type=MESH,
        )

    def at(dd, ss, jj):
        return {"dp": dd, "section": ss, "tensor": jj}

    def copy_act(k, owner):
        return remote(act, actall.at[owner], act_send.at[k], act_recv.at[k], at(peer(d, k, N), s, i))

    def copy_a(j, owner):
        return remote(partb.at[rows_at(j)], in_a.at[owner], a_send.at[j], a_recv.at[owner], at(d, s + 1, j))

    def copy_tn(k, owner):
        return remote(
            tn.at[rows_at(owner)], tn.at[rows_at(owner)], tn_send.at[k], tn_recv.at[k], at(d, s, peer(i, k, T))
        )

    def copy_d(k):
        j = peer(i, k, T)
        return remote(partb.at[rows_at(j)], in_d.at[k - 1], d_send.at[k], d_recv.at[k], at(d, s, j))

    def copy_s(k, owner):
        return remote(
            gfull.at[rows_at(owner)], gfull.at[rows_at(owner)], s_send.at[k], s_recv.at[k],
            at(d, s, peer(i, k, T)),
        )

    def copy_f(k):
        j = peer(i, k, T)
        return remote(gpartb.at[rows_at(j)], in_f.at[k - 1], f_send.at[k], f_recv.at[k], at(d, s, j))

    def copy_h(j, owner):
        return remote(grow, gfull.at[rows_at(owner)], h_send.at[0, j], h_recv.at[0, owner], at(d, s - 1, j))

    def copy_hd(k, j, owner):
        dd = peer(d, k, N)
        return remote(
            grow.at[:, feats_at(dd)], gall.at[lax.rem(d, N), rows_at(owner)],
            h_send.at[k, j], h_recv.at[k, owner], at(dd, s - 1, j),
        )

    def land_hd(k, owner):
        src = peer(d, N - k, N)
        return remote(
            grow.at[:, feats_at(d)], gall.at[src, rows_at(owner)],
            h_send.at[k, owner], h_recv.at[k, owner], at(d, s, i),
        )

    def copy_x(k):
        dd = peer(d, k, N)
        return remote(gfull.at[:, feats_at(dd)], gall.at[d], x_send.at[k], x_recv.at[k], at(dd, s, i))

    def land_x(k):
        src = peer(d, N - k, N)
        return remote(gfull.at[:, feats_at(d)], gall.at[src], x_send.at[k], x_recv.at[k], at(d, s, i))

    if fused:
        for k in range(1, N):
            copy_act(k, d).start()
        actall[d] = act[...]

    xrows = x_ref[rows_at(i)].astype(F32)
    rrows = lax.rsqrt(jnp.mean(xrows * xrows, axis=-1, keepdims=True) + 1e-06)

    loads[1].wait()
    for c in chunks:
        base = dot_nt(act[...], wd[c, :])
        part[:, c] = base

    loads[2].wait()
    loads[3].wait()

    @pl.when(s == 0)
    def _():
        partb[...] = part[...].astype(BF)

    @pl.when(s > 0)
    def _():
        total = None
        for j in range(T):
            remote(partb.at[rows_at(j)], in_a.at[j], a_send.at[j], a_recv.at[j], at(d, s, i)).wait_recv()
        for j in range(T):
            piece = in_a[j].astype(F32)
            total = piece if total is None else total + piece
        tfloat = total.astype(BF).astype(F32)
        trow[...] = tfloat
        tn[rows_at(i)] = (
            gain * (rrows * tfloat - rrows**3 * xrows * jnp.mean(xrows * tfloat, axis=-1, keepdims=True))
        ).astype(BF)
        for k in range(1, T):
            copy_tn(k, i).start()
        for k in range(1, T):
            copy_tn(k, peer(i, T - k, T)).wait_recv()
        tmix = mix(dot_nt(tn[...], wv[...]).astype(BF)).astype(BF)
        for c in chunks:
            part[:, c] = part[:, c] + dot_nt(tmix, wo[c, :])
        part[rows_at(i)] = part[rows_at(i)] + trow[...]
        partb[...] = part[...].astype(BF)
        for k in range(1, T):
            copy_tn(k, i).wait_send()

    if S > 1:

        @pl.when(s < S - 1)
        def _():
            for j in range(T):
                copy_a(j, i).start()

    @pl.when(s == S - 1)
    def _():
        for k in range(1, T):
            copy_d(k).start()
        total = part[rows_at(i)]
        for k in range(1, T):
            copy_d(k).wait_recv()
        for k in range(1, T):
            total = total + in_d[k - 1].astype(F32)
        tlast = total.astype(BF).astype(F32)
        gfull[rows_at(i)] = (curv[rows_at(i)].astype(F32) * tlast).astype(BF)
        for k in range(1, T):
            copy_s(k, i).start()
        for k in range(1, T):
            copy_s(k, peer(i, T - k, T)).wait_recv()
        for k in range(1, T):
            copy_s(k, i).wait_send()
            copy_d(k).wait_send()

    if S > 1:

        @pl.when(s < S - 1)
        def _():
            for j in range(T):
                copy_a(j, i).wait_send()

        def gather_rows():
            for j in range(T):
                remote(grow, gfull.at[rows_at(j)], h_send.at[0, j], h_recv.at[0, j], at(d, s, i)).wait_recv()

        if fused:
            if S > 2:

                @pl.when(jnp.logical_and(s > 0, s < S - 1))
                def _():
                    gather_rows()

            @pl.when(s == 0)
            def _():
                for k in range(N):
                    for j in range(T):
                        land_hd(k, j).wait_recv()
        else:

            @pl.when(s < S - 1)
            def _():
                gather_rows()

        @pl.when(s > 0)
        def _():
            gm = dot_nn(gfull[...], wo[...]).astype(BF)
            gv = jnp.concatenate(
                [dot_tn(probs_ref[h], gm[:, h * hd : (h + 1) * hd]) for h in range(heads)], axis=1
            ).astype(BF)
            for c in chunks:
                gc = dot_nn(gv, wv[:, c])
                part[:, c] = gc
                gpartb[:, c] = gc.astype(BF)
            for k in range(1, T):
                copy_f(k).start()
            total = part[rows_at(i)]
            for k in range(1, T):
                copy_f(k).wait_recv()
            for k in range(1, T):
                total = total + in_f[k - 1].astype(F32)
            scaled = gain * total
            gx = rrows * scaled - rrows**3 * xrows * jnp.mean(xrows * scaled, axis=-1, keepdims=True)
            grow[...] = (gfull[rows_at(i)].astype(F32) + gx).astype(BF)

            def plain():
                for j in range(T):
                    copy_h(j, i).start()
                for j in range(T):
                    copy_h(j, i).wait_send()

            if fused:

                @pl.when(s == 1)
                def _():
                    for k in range(N):
                        for j in range(T):
                            copy_hd(k, j, i).start()
                    for k in range(N):
                        for j in range(T):
                            copy_hd(k, j, i).wait_send()

                if S > 2:
                    pl.when(s > 1)(plain)
            else:
                plain()
            for k in range(1, T):
                copy_f(k).wait_send()

    if fused:

        def spread():
            for k in range(1, N):
                copy_x(k).start()
            gall[d] = gfull[:, feats_at(d)]
            for k in range(1, N):
                land_x(k).wait_recv()
            for k in range(1, N):
                copy_x(k).wait_send()

        if S > 1:
            pl.when(s > 0)(spread)
        else:
            spread()
        for k in range(1, N):
            copy_act(k, peer(d, N - k, N)).wait_recv()
        prod_ref[...] = dot_tn(
            gall[...].reshape(N * tok, feats), actall[...].reshape(N * tok, act.shape[1])
        )
        for k in range(1, N):
            copy_act(k, d).wait_send()
    else:
        gout_ref[...] = gfull[...]
        actout_ref[...] = act[...]


def home_share(feats, g, q):
    more = 1 if MORE[g] > 0 else -1
    return (feats // 256 + (more if q < abs(MORE[g]) else 0)) * 128


def kernel_pair(
    T, N,
    x_ref, gain_ref, probs_ref, wv_hbm, wd_hbm, wo_hbm, curv_hbm,
    gall, actall,
    wv, wd, wo, curv, act, vals, tvals, part, tbuf, gbuf, xrow, gain1,
    a_src, a_hop, a_land, d_src, d_hop, d_land, f_src, f_hop, f_land,
    grow,
    load_sem, lend_send, lend_recv, act_send, act_recv,
    hop_send, hop_recv, rs_send, rs_recv, ag_send, ag_recv, ag_pass, pass_send,
    h_send, h_self, h_recv, x_send, x_recv,
):
    d = lax.axis_index("dp")
    s = lax.axis_index("section")
    i = lax.axis_index("tensor")
    tok, width = x_ref.shape
    K = TOKEN_CHUNKS
    Q = N
    ck = tok // K
    blk = ck // T
    feats = width // N
    heads = probs_ref.shape[0]
    hd = wv.shape[0] // heads
    end = jnp.logical_or(i == 0, i == T - 1)
    mid = jnp.logical_not(end)
    mate = jnp.bitwise_xor(i, 1)
    cross = jnp.where(end, T - 1 - mate, T - 1 - i)
    other = T - 1 - mate
    far = [k for k in range(2, T - 1)] + [k for k in range(1, T) if k in (1, T - 1)]
    subs = range(Q)

    def peer(me, k, n):
        return lax.rem(me + k, n)

    def at(dd, ss, jj):
        return {"dp": dd, "section": ss, "tensor": jj}

    def chunk(kk):
        return slice(kk * ck, (kk + 1) * ck)

    def rows(kk, j):
        return pl.ds(pl.multiple_of(kk * ck + j * blk, blk), blk)

    def share(g, y, q):
        return home_share(feats, g, q) if y == g else feats - home_share(feats, g, q)

    def part_of(g, y, q):
        lo = share(g, 0, q) if y == 1 else 0
        return slice(lo, lo + share(g, y, q))

    def col(g, y, q):
        c = part_of(g, y, q)
        return slice(q * feats + c.start, q * feats + c.stop)

    def block(b):
        return slice(b * feats, (b + 1) * feats)

    def feats_at(j):
        return pl.ds(pl.multiple_of(j * feats, 128), feats)

    def seq_rows(kk):
        return pl.ds(pl.multiple_of(d * tok + kk * ck, ck), ck)

    def own_rows(kk):
        return pl.ds(pl.multiple_of(d * tok + kk * ck + i * blk, blk), blk)

    def remote(src, dst, send, recv, dev):
        return pltpu.make_async_remote_copy(
            src_ref=src, dst_ref=dst, send_sem=send, recv_sem=recv,
            device_id=dev, device_id_type=MESH,
        )

    def landed(ref, sem):
        remote(ref, ref, sem, sem, at(d, s, i)).wait_recv()

    def sent(ref, sem):
        remote(ref, ref, sem, sem, at(d, s, i)).wait_send()

    loads = [
        pltpu.make_async_copy(src, dst, load_sem.at[k])
        for k, (src, dst) in enumerate(((wv_hbm, wv), (wd_hbm, wd), (wo_hbm, wo), (curv_hbm, curv)))
    ]
    loads[0].start()
    loads[1].start()

    barrier = pltpu.get_barrier_semaphore()
    for a in range(N):
        for b in range(2):
            for c in range(T):
                if (a == 0) != (b == 0 and c == 0):
                    pl.semaphore_signal(
                        barrier, inc=1, device_id=at(peer(d, a, N), peer(s, b, 2), peer(i, c, T)),
                        device_id_type=MESH,
                    )
    loads[2].start()
    loads[3].start()

    def mix(kk, buf):
        r = chunk(kk)
        return jnp.concatenate(
            [dot_nn(probs_ref[h, r, :], buf[:, h * hd : (h + 1) * hd]) for h in range(heads)], axis=1
        ).astype(BF)

    def rnorm_of(xf):
        return lax.rsqrt(jnp.mean(xf * xf, axis=-1, keepdims=True) + 1e-06)

    gain = gain_ref[...]

    def values_of(kk):
        r = chunk(kk)
        xf = x_ref[r, :].astype(F32)
        normed = (xf * rnorm_of(xf) * gain).astype(BF)
        vals[r, :] = dot_nt(normed, wv[...]).astype(BF)

    def acts_of(kk):
        act[chunk(kk), :] = mix(kk, vals)

    for kk in range(1, K):
        vals[chunk(kk), :] = jnp.zeros((ck, vals.shape[1]), BF)
        tvals[chunk(kk), :] = jnp.zeros((ck, vals.shape[1]), BF)

    def copy_act(k, owner):
        return remote(act, actall.at[owner], act_send.at[k], act_recv.at[k], at(peer(d, k, N), s, i))

    keep_act = pltpu.make_async_copy(act, actall.at[d], act_send.at[0])

    def keep_rows(kk):
        return pltpu.make_async_copy(gbuf.at[chunk(kk), feats_at(d)], gall.at[seq_rows(kk)], x_send.at[K + kk])

    lend = [
        remote(x_ref.at[rows(kk, i)], xrow.at[kk], lend_send.at[kk], lend_recv.at[kk], at(d, 0, i))
        for kk in range(K)
    ] + [remote(gain_ref, gain1, lend_send.at[K], lend_recv.at[K], at(d, 0, i))]

    A, D_, F_ = (0, a_src, a_hop, a_land, 0), (1, d_src, d_hop, d_land, 1), (2, f_src, f_hop, f_land, 1)

    def cw(p, y, q):
        return slice(0, share(p[4], y, q) + (128 if p[0] == 2 and q == 0 else 0))

    def hop(p, kk, q):
        y = 1 - p[4]
        c = cw(p, y, q)
        r = chunk(kk)
        remote(
            p[1].at[y, q, r, c], p[2].at[q, r, c], hop_send.at[p[0], kk, q], hop_recv.at[p[0], kk, q], at(d, y, i)
        ).start()

    def hop_done(p, kk, q):
        sent(p[1].at[1 - p[4], q, chunk(kk), cw(p, 1 - p[4], q)], hop_send.at[p[0], kk, q])

    def scatter(p, me, kk, q):
        c = cw(p, me, q)
        if me != p[4]:
            landed(p[2].at[q, chunk(kk), c], hop_recv.at[p[0], kk, q])
        buf = p[1].at[me, q] if me == p[4] else p[2].at[q]
        for k in far:
            j = peer(i, k, T)
            remote(
                buf.at[rows(kk, j), c], p[3].at[q, kk, k - 1, :, c], rs_send.at[p[0], kk, q],
                rs_recv.at[p[0], kk, q], at(d, me, j),
            ).start()

    def scatter_done(p, me, kk, q):
        sent(p[3].at[q, kk, :, :, cw(p, me, q)], rs_send.at[p[0], kk, q])

    def collect(p, me, kk, q, local):
        c = cw(p, me, q)
        total = p[2][q, rows(kk, i), c].astype(F32) if me != p[4] else local
        landed(p[3].at[q, kk, :, :, c], rs_recv.at[p[0], kk, q])
        for k in range(T - 1):
            total = total + p[3][q, kk, k, :, c].astype(F32)
        return total

    def spread_copies(n, buf, me, kk, q):
        src = buf.at[rows(kk, i), col(n, me, q)]
        if not RELAY[n]:
            return [
                remote(src, src, ag_send.at[n, kk, q, k], ag_recv.at[n, me, kk, q], at(d, 1, peer(i, k, T)))
                for k in far + ([0] if me == 0 else [])
            ]
        out = [
            remote(src, src, ag_send.at[n, kk, q, 1], ag_pass.at[n, me, kk, q], at(d, me, cross)),
            remote(src, src, ag_send.at[n, kk, q, 2], ag_recv.at[n, me, kk, q], at(d, 1, mate)),
        ]
        if me == 0:
            out.append(remote(src, src, ag_send.at[n, kk, q, 0], ag_recv.at[n, me, kk, q], at(d, 1, i)))
        return out

    def pass_copies(n, buf, me, kk, q):
        out = []
        for m, j in ((0, cross), (1, other)):
            src = buf.at[rows(kk, j), col(n, me, q)]
            land = ag_pass if me == 1 else ag_recv
            out.append(remote(src, src, pass_send.at[n, kk, q, m], land.at[n, me, kk, q], at(d, 1, mate)))
            if me == 0:
                out.append(remote(src, src, pass_send.at[n, kk, q, 2 + m], land.at[n, me, kk, q], at(d, 1, i)))
        return out

    def spread(n, buf, me, kk, q):
        for copy in spread_copies(n, buf, me, kk, q):
            copy.start()

    def pass_on(n, buf, me, kk, q):
        if not RELAY[n]:
            return
        pair = buf.at[kk * ck : kk * ck + 2 * blk, col(n, me, q)]
        if me == 1:
            landed(pair, ag_pass.at[n, me, kk, q])

        @pl.when(mid)
        def _():
            if me == 0:
                landed(pair, ag_pass.at[n, me, kk, q])
            for copy in pass_copies(n, buf, me, kk, q):
                copy.start()

    def spread_done(n, buf, me, kk, q):
        for copy in spread_copies(n, buf, me, kk, q):
            copy.wait_send()
        if RELAY[n]:

            @pl.when(mid)
            def _():
                for copy in pass_copies(n, buf, me, kk, q):
                    copy.wait_send()

    def gathered(n, buf, y, kk, q):
        count = T if y == 0 else T - 1
        if RELAY[n] and y == 1:
            count = 1
        landed(buf.at[kk * ck : kk * ck + count * blk, col(n, y, q)], ag_recv.at[n, y, kk, q])

    def ready(n, buf, kk, b):
        for y in (1, 0):
            gathered(n, buf, y, kk, b)

    def pack(p, buf, kk, b):
        home = p[4]
        for y in (1 - home, home):
            p[1][y, b, chunk(kk), 0 : share(home, y, b)] = buf[chunk(kk), col(home, y, b)].astype(BF)
            if y == home:
                scatter(p, home, kk, b)
            else:
                hop(p, kk, b)

    def done(me, sums, gathers):
        for kk in range(K):
            for q in subs:
                for p in sums:
                    if me == p[4]:
                        hop_done(p, kk, q)
                    scatter_done(p, me, kk, q)
                for n, buf in gathers:
                    spread_done(n, buf, me, kk, q)

    def tangent(me, kk, q):
        r = rows(kk, i)
        c = col(0, me, q)
        tbuf[r, c] = collect(A, me, kk, q, part[r, c]).astype(BF)
        spread(0, tbuf, me, kk, q)

    def seed(me, kk, q):
        r = rows(kk, i)
        c = col(1, me, q)
        total = collect(D_, me, kk, q, part[r, c])
        gbuf[r, c] = (curv[r, c].astype(F32) * total.astype(BF).astype(F32)).astype(BF)
        spread(1, gbuf, me, kk, q)

    def hand(me, kk, q, start):
        dd = q
        c = part_of(1, me, q)
        src = grow.at[kk, q, :, 0 : share(1, me, q)]
        dst = gall.at[own_rows(kk), c]

        if start:
            for k in far:
                remote(src, dst, h_send.at[kk, q], h_recv.at[kk, me], at(dd, 0, peer(i, k, T))).start()
        else:
            sent(gall.at[0 : (T - 1) * blk, c], h_send.at[kk, q])

        def direct():
            if start:
                remote(src, dst, h_self.at[kk, q], h_recv.at[kk, me], at(dd, 0, i)).start()
            else:
                sent(src, h_self.at[kk, q])

        if me == 1:
            direct()
        else:
            pl.when(d != dd)(direct)

            @pl.when(d == dd)
            def _():
                own = pltpu.make_async_copy(src, dst, h_self.at[kk, q])
                own.start() if start else own.wait()

    def adjoint(me, kk, xr, gn, rr):
        weight = None
        for q in subs:
            c = col(1, me, q)
            wide = share(1, me, q)
            local = f_src[1, q, rows(kk, i), cw(F_, 1, q)].astype(F32) if me == 1 else None
            total = collect(F_, me, kk, q, local)
            if q == 0:
                weight = jnp.sum(total[:, wide:], axis=-1, keepdims=True) * (rr * rr * (2.0 / 128 / width))
                total = total[:, :wide]
            g1 = gbuf[rows(kk, i), c].astype(F32) + (rr * gn[:, c]) * total - xr[:, c] * weight
            grow[kk, q, :, 0:wide] = g1.astype(BF)
            hand(me, kk, q, True)

    @pl.when(s == 0)
    def _():
        loads[0].wait()
        values_of(0)
        acts_of(0)
        pl.semaphore_wait(barrier, 2 * T + N - 2)
        loads[1].wait()
        for kk in range(K):
            if kk:
                values_of(kk)
                acts_of(kk)
            for b in range(N):
                part[chunk(kk), block(b)] = dot_nt(act[chunk(kk), :], wd[block(b), :])
                pack(A, part, kk, b)
        for k in range(1, N):
            copy_act(k, d).start()
        keep_act.start()
        for kk in range(K):
            for q in subs:
                tangent(0, kk, q)
        for kk in range(K):
            for q in subs:
                pass_on(0, tbuf, 0, kk, q)
        for copy in lend:
            copy.wait_recv()
        loads[2].wait()
        loads[3].wait()
        for kk in range(K):
            for q in subs:
                scatter(D_, 0, kk, q)
        done(0, (A,), ())
        for kk in range(K):
            for q in subs:
                seed(0, kk, q)
        for kk in range(K):
            for q in subs:
                pass_on(1, gbuf, 0, kk, q)
        done(0, (), ((0, tbuf),))
        for k in range(1, N):
            copy_act(k, d).wait_send()
        keep_act.wait()
        gn = gain1[...]
        for kk in reversed(range(K)):
            for q in subs:
                scatter(F_, 0, kk, q)
        done(0, (D_,), ((1, gbuf),))
        for kk in reversed(range(K)):
            xr = xrow[kk].astype(F32)
            rr = rnorm_of(xr)
            adjoint(0, kk, xr, gn, rr)
        for k in range(1, N):
            copy_act(k, peer(d, N - k, N)).wait_recv()
        done(0, (F_,), ())
        for kk in reversed(range(K)):
            for q in subs:
                hand(0, kk, q, False)
        for n, kk in enumerate(reversed(range(K))):

            for dd in range(N):

                @pl.when(d == dd)
                def _():
                    landed(gall.at[0 : N * ck - blk, part_of(1, 0, dd)], h_recv.at[kk, 0])
                    landed(gall.at[0 : N * ck, part_of(1, 1, dd)], h_recv.at[kk, 1])

    @pl.when(s == 1)
    def _():
        loads[0].wait()
        for kk in range(K):
            values_of(kk)
            acts_of(kk)
        pl.semaphore_wait(barrier, 2 * T + N - 2)
        for copy in lend:
            copy.start()
        for k in range(1, N):
            copy_act(k, d).start()
        keep_act.start()
        loads[1].wait()
        for b in range(N):
            part[:, block(b)] = dot_nt(act[...], wd[block(b), :])
        loads[2].wait()
        loads[3].wait()
        for kk in range(K):
            for q in subs:
                scatter(A, 1, kk, q)
        for kk in range(K):
            for q in subs:
                tangent(1, kk, q)
        for kk in range(K):
            r = chunk(kk)
            tv = None
            mean = None
            for b in range(N):
                pass_on(0, tbuf, 1, kk, b)
            for b in range(N):
                ready(0, tbuf, kk, b)
                c = block(b)
                tf = tbuf[r, c].astype(F32)
                dotted = jnp.sum(x_ref[r, c].astype(F32) * tf, axis=-1, keepdims=True)
                more = dot_nt((gain[:, c] * tf).astype(BF), wv[:, c])
                tv = more if tv is None else tv + more
                mean = dotted if mean is None else mean + dotted
            rr = rnorm_of(x_ref[r, :].astype(F32))
            tvals[r, :] = (rr * tv - (rr * rr * (1.0 / width) * mean) * vals[r, :].astype(F32)).astype(BF)
            tmix = mix(kk, tvals)
            for b in range(N):
                part[r, block(b)] = part[r, block(b)] + dot_nt(tmix, wo[block(b), :])
                mine = rows(kk, i)
                part[mine, block(b)] = part[mine, block(b)] + tbuf[mine, block(b)].astype(F32)
                pack(D_, part, kk, b)
        for copy in lend:
            copy.wait_send()
        done(1, (A,), ())
        for kk in range(K):
            for q in subs:
                seed(1, kk, q)
        done(1, (), ((0, tbuf),))
        for k in range(1, N):
            copy_act(k, d).wait_send()
        keep_act.wait()

        def copy_x(kk, k):
            dd = peer(d, k, N)
            return remote(
                gbuf.at[chunk(kk), feats_at(dd)], gall.at[seq_rows(kk)], x_send.at[kk], x_recv.at[kk], at(dd, s, i)
            )

        gms = []
        for kk in range(K):
            gm = None
            for b in range(N):
                pass_on(1, gbuf, 1, kk, b)
            for b in range(N):
                ready(1, gbuf, kk, b)
                more = dot_nn(gbuf[chunk(kk), block(b)], wo[block(b), :])
                gm = more if gm is None else gm + more
            gms.append(gm.astype(BF))
        pending = None
        for kk in reversed(range(K)):
            r = chunk(kk)
            more = jnp.concatenate(
                [dot_tn(probs_ref[h, r, :], gms[kk][:, h * hd : (h + 1) * hd]) for h in range(heads)], axis=1
            )
            pending = more if pending is None else pending + more
            gv = pending[r, :].astype(BF)
            weight = jnp.sum(gv.astype(F32) * vals[r, :].astype(F32), axis=-1, keepdims=True)
            high = weight.astype(BF).astype(F32)
            lane = lax.broadcasted_iota(jnp.int32, (ck, 128), 1)
            extra = jnp.where(lane < 64, high, weight - high).astype(BF)
            for y in (0, 1):
                f_src[y, 0, r, share(1, y, 0) : share(1, y, 0) + 128] = extra
            for b in range(N):
                part[r, block(b)] = dot_nn(gv, wv[:, block(b)])
                pack(F_, part, kk, b)
        for kk in range(K):
            for k in range(1, N):
                copy_x(kk, k).start()
            keep_rows(kk).start()
        done(1, (D_,), ((1, gbuf),))
        for k in range(1, N):
            copy_act(k, peer(d, N - k, N)).wait_recv()
        for kk in range(K):
            landed(gall.at[0 : (N - 1) * ck], x_recv.at[kk])
        for kk in reversed(range(K)):
            xr = x_ref[rows(kk, i), :].astype(F32)
            adjoint(1, kk, xr, gain, rnorm_of(xr))
        done(1, (F_,), ())
        for kk in range(K):
            sent(gall.at[0 : (N - 1) * ck], x_send.at[kk])
            keep_rows(kk).wait()
            for q in subs:
                hand(1, kk, q, False)


def call_pair(T, N, x, norm_gain, probs, w_val, w_dir, w_out, curvature):
    tok, width = x.shape
    hf = w_val.shape[0]
    K = TOKEN_CHUNKS
    Q = N
    ck = tok // K
    blk = ck // T
    feats = width // N
    wide = max(max(home_share(feats, g, q), feats - home_share(feats, g, q)) for g in (0, 1) for q in range(N))
    vm = functools.partial(pl.BlockSpec, memory_space=pltpu.VMEM)
    hbm = functools.partial(pl.BlockSpec, memory_space=pl.ANY)
    sem = pltpu.SemaphoreType.DMA

    def sums(cols):
        return [
            pltpu.VMEM((2, Q, tok, cols), BF),
            pltpu.VMEM((Q, tok, cols), BF),
            pltpu.VMEM((Q, K, T - 1, blk, cols), BF),
        ]

    scratch = [
        pltpu.VMEM((hf, width), BF),
        pltpu.VMEM((width, hf), BF),
        pltpu.VMEM((width, hf), BF),
        pltpu.VMEM((tok, width), BF),
        pltpu.VMEM((tok, hf), BF),
        pltpu.VMEM((tok, hf), BF),
        pltpu.VMEM((tok, hf), BF),
        pltpu.VMEM((tok, width), F32),
        pltpu.VMEM((tok, width), BF),
        pltpu.VMEM((tok, width), BF),
        pltpu.VMEM((K, blk, width), BF),
        pltpu.VMEM((1, width), F32),
        *sums(wide), *sums(wide), *sums(wide + 128),
        pltpu.VMEM((K, Q, blk, wide), BF),
        sem((4,)),
        sem((K + 1,)), sem((K + 1,)),
        sem((N,)), sem((N,)),
        sem((3, K, Q)), sem((3, K, Q)),
        sem((3, K, Q)), sem((3, K, Q)),
        sem((2, K, Q, T)), sem((2, 2, K, Q)), sem((2, 2, K, Q)), sem((2, K, Q, T)),
        sem((K, Q)), sem((K, Q)), sem((K, 2)),
        sem((2 * K,)), sem((K,)),
    ]
    adjoints, acts = pl.pallas_call(
        functools.partial(kernel_pair, T, N),
        out_shape=(
            jax.ShapeDtypeStruct((N * tok, feats), BF), jax.ShapeDtypeStruct((N, tok, hf), BF),
        ),
        in_specs=[vm(), vm(), vm(), hbm(), hbm(), hbm(), hbm()],
        out_specs=(hbm(), hbm()),
        scratch_shapes=scratch,
        compiler_params=pltpu.CompilerParams(
            collective_id=0, has_side_effects=True, vmem_limit_bytes=56 * 1024 * 1024
        ),
    )(x, norm_gain, probs, w_val, w_dir, w_out, curvature)
    return dot_tn(adjoints, acts.reshape(N * tok, hf))


def per_device(section_input, norm_gain, value_weight, attn_probs, out_weight, direction, curvature):
    x = section_input[0]
    w_val = value_weight[0]
    w_out = out_weight[0]
    w_dir = direction[0]
    probs = attn_probs[0]
    S = lax.axis_size("section")
    T = lax.axis_size("tensor")
    N = lax.axis_size("dp")
    tok, width = x.shape
    hf = w_val.shape[0]
    rows = tok // T
    feats = width // N
    fused = feats % 128 == 0 and feats * N == width
    blocks = tok % (16 * T * TOKEN_CHUNKS) == 0
    if fused and S == 2 and T == 4 and feats % 256 == 0 and blocks:
        return call_pair(T, N, x, norm_gain, probs, w_val, w_dir, w_out, curvature)[None]
    vm = functools.partial(pl.BlockSpec, memory_space=pltpu.VMEM)
    hbm = functools.partial(pl.BlockSpec, memory_space=pl.ANY)
    if fused:
        outs = jax.ShapeDtypeStruct((feats, hf), F32)
        out_specs = vm()
    else:
        outs = (jax.ShapeDtypeStruct((tok, width), BF), jax.ShapeDtypeStruct((tok, hf), BF))
        out_specs = (vm(), vm())
    sem = pltpu.SemaphoreType.DMA
    wide = N if fused else 1
    scratch = [
        pltpu.VMEM((hf, width), BF),
        pltpu.VMEM((width, hf), BF),
        pltpu.VMEM((width, hf), BF),
        pltpu.VMEM((tok, width), BF),
        pltpu.VMEM((tok, hf), BF),
        pltpu.VMEM((tok, width), F32),
        pltpu.VMEM((tok, width), BF),
        pltpu.VMEM((T, rows, width), BF),
        pltpu.VMEM((T, rows, width), BF),
        pltpu.VMEM((T, rows, width), BF),
        pltpu.VMEM((tok, width), BF),
        pltpu.VMEM((tok, width), BF),
        pltpu.VMEM((tok, width), BF),
        pltpu.VMEM((tok, width), BF),
        pltpu.VMEM((rows, width), F32),
        pltpu.VMEM((rows, width), BF),
        pltpu.VMEM((wide, tok, hf), BF),
        pltpu.VMEM((wide, tok, feats if fused else 128), BF),
        sem((4,)),
        sem((N,)), sem((N,)),
        sem((T,)), sem((T,)),
        sem((T,)), sem((T,)),
        sem((T,)), sem((T,)),
        sem((T,)), sem((T,)),
        sem((T,)), sem((T,)),
        sem((wide, T)), sem((wide, T)),
        sem((N,)), sem((N,)),
    ]
    result = pl.pallas_call(
        functools.partial(kernel, fused, S, T, N),
        out_shape=outs,
        in_specs=[vm(), vm(), vm(), hbm(), hbm(), hbm(), hbm()],
        out_specs=out_specs,
        scratch_shapes=scratch,
        compiler_params=pltpu.CompilerParams(
            collective_id=0, has_side_effects=True, vmem_limit_bytes=56 * 1024 * 1024
        ),
    )(x, norm_gain, probs, w_val, w_dir, w_out, curvature)
    if fused:
        return result[None]
    adjoint, act = result
    product = lax.psum_scatter(
        dot_tn(adjoint, act).astype(BF), "dp", scatter_dimension=0, tiled=True
    ).astype(F32)
    return product[None]


def solution(mesh):
    in_specs = (
        P("section", "dp", None),
        P("section", None),
        P("section", "tensor", None),
        P("section", "tensor", "dp", None),
        P("section", None, "tensor"),
        P("section", None, "tensor"),
        P("dp", None),
    )
    out_specs = P("section", "dp", "tensor")
    return jax.shard_map(
        per_device, mesh=mesh, in_specs=in_specs, out_specs=out_specs, check_vma=False
    )
```

```python
import functools

import jax
import jax.numpy as jnp
from jax import lax
from jax.experimental import pallas as pl
from jax.experimental.pallas import tpu as pltpu
from jax.sharding import PartitionSpec as P

MESH = pl.DeviceIdType.MESH
BF = jnp.bfloat16
F32 = jnp.float32
TOKEN_CHUNKS = 2
MORE = (1, 0)
RELAY = (True, False)


def dot_nt(a, b):
    return lax.dot_general(a, b, (((1,), (1,)), ((), ())), preferred_element_type=F32)


def dot_tn(a, b):
    return lax.dot_general(a, b, (((0,), (0,)), ((), ())), preferred_element_type=F32)


def dot_nn(a, b):
    return lax.dot_general(a, b, (((1,), (0,)), ((), ())), preferred_element_type=F32)


def kernel(
    fused, S, T, N,
    x_ref, gain_ref, probs_ref, wv_hbm, wd_hbm, wo_hbm, curv_hbm,
    *rest,
):
    if fused:
        prod_ref, rest = rest[0], rest[1:]
    else:
        gout_ref, actout_ref, rest = rest[0], rest[1], rest[2:]
    (
        wv, wd, wo, curv, act, part, partb, in_a, in_d, in_f, gpartb, normed, tn, gfull, trow, grow,
        actall, gall,
        load_sem, act_send, act_recv, a_send, a_recv, tn_send, tn_recv, d_send, d_recv,
        s_send, s_recv, f_send, f_recv, h_send, h_recv, x_send, x_recv,
    ) = rest
    d = lax.axis_index("dp")
    s = lax.axis_index("section")
    i = lax.axis_index("tensor")
    tok, width = x_ref.shape
    rows = tok // T
    heads = probs_ref.shape[0]
    hd = wv.shape[0] // heads
    feats = width // N
    CH = 512 if width % 512 == 0 else width
    chunks = [slice(c, c + CH) for c in range(0, width, CH)]

    def rows_at(j):
        return pl.ds(pl.multiple_of(j * rows, rows), rows)

    def feats_at(j):
        return pl.ds(pl.multiple_of(j * feats, 128), feats)

    def peer(me, k, n):
        return lax.rem(me + k, n)

    loads = [
        pltpu.make_async_copy(src, dst, load_sem.at[k])
        for k, (src, dst) in enumerate(((wv_hbm, wv), (wd_hbm, wd), (wo_hbm, wo), (curv_hbm, curv)))
    ]
    for copy in loads:
        copy.start()

    barrier = pltpu.get_barrier_semaphore()

    def greet(dev):
        pl.semaphore_signal(barrier, inc=1, device_id=dev, device_id_type=MESH)

    for k in range(1, T):
        greet({"dp": d, "section": s, "tensor": peer(i, k, T)})
    for k in range(1, N):
        greet({"dp": peer(d, k, N), "section": s, "tensor": i})
    for low in range(S - 1):
        wide = N if (fused and low == 0) else 1

        @pl.when(s == low)
        def _():
            for k in range(wide):
                for j in range(T):
                    greet({"dp": peer(d, k, N), "section": s + 1, "tensor": j})

        @pl.when(s == low + 1)
        def _():
            for k in range(wide):
                for j in range(T):
                    greet({"dp": peer(d, k, N), "section": s - 1, "tensor": j})

    gain = gain_ref[...]
    xf = x_ref[...].astype(F32)
    rnorm = lax.rsqrt(jnp.mean(xf * xf, axis=-1, keepdims=True) + 1e-06)
    normed[...] = (xf * rnorm * gain).astype(BF)

    def mix(vals):
        return jnp.concatenate(
            [dot_nn(probs_ref[h], vals[:, h * hd : (h + 1) * hd]) for h in range(heads)], axis=1
        )

    loads[0].wait()
    act[...] = mix(dot_nt(normed[...], wv[...]).astype(BF)).astype(BF)

    for here in range(S):
        count = T - 1 + N - 1
        for low in (here - 1, here):
            if 0 <= low < S - 1:
                count += T * (N if (fused and low == 0) else 1)

        @pl.when(s == here)
        def _():
            pl.semaphore_wait(barrier, count)

    def remote(src, dst, send, recv, dev):
        return pltpu.make_async_remote_copy(
            src_ref=src, dst_ref=dst, send_sem=send, recv_sem=recv,
            device_id=dev, device_id_type=MESH,
        )

    def at(dd, ss, jj):
        return {"dp": dd, "section": ss, "tensor": jj}

    def copy_act(k, owner):
        return remote(act, actall.at[owner], act_send.at[k], act_recv.at[k], at(peer(d, k, N), s, i))

    def copy_a(j, owner):
        return remote(partb.at[rows_at(j)], in_a.at[owner], a_send.at[j], a_recv.at[owner], at(d, s + 1, j))

    def copy_tn(k, owner):
        return remote(
            tn.at[rows_at(owner)], tn.at[rows_at(owner)], tn_send.at[k], tn_recv.at[k], at(d, s, peer(i, k, T))
        )

    def copy_d(k):
        j = peer(i, k, T)
        return remote(partb.at[rows_at(j)], in_d.at[k - 1], d_send.at[k], d_recv.at[k], at(d, s, j))

    def copy_s(k, owner):
        return remote(
            gfull.at[rows_at(owner)], gfull.at[rows_at(owner)], s_send.at[k], s_recv.at[k],
            at(d, s, peer(i, k, T)),
        )

    def copy_f(k):
        j = peer(i, k, T)
        return remote(gpartb.at[rows_at(j)], in_f.at[k - 1], f_send.at[k], f_recv.at[k], at(d, s, j))

    def copy_h(j, owner):
        return remote(grow, gfull.at[rows_at(owner)], h_send.at[0, j], h_recv.at[0, owner], at(d, s - 1, j))

    def copy_hd(k, j, owner):
        dd = peer(d, k, N)
        return remote(
            grow.at[:, feats_at(dd)], gall.at[lax.rem(d, N), rows_at(owner)],
            h_send.at[k, j], h_recv.at[k, owner], at(dd, s - 1, j),
        )

    def land_hd(k, owner):
        src = peer(d, N - k, N)
        return remote(
            grow.at[:, feats_at(d)], gall.at[src, rows_at(owner)],
            h_send.at[k, owner], h_recv.at[k, owner], at(d, s, i),
        )

    def copy_x(k):
        dd = peer(d, k, N)
        return remote(gfull.at[:, feats_at(dd)], gall.at[d], x_send.at[k], x_recv.at[k], at(dd, s, i))

    def land_x(k):
        src = peer(d, N - k, N)
        return remote(gfull.at[:, feats_at(d)], gall.at[src], x_send.at[k], x_recv.at[k], at(d, s, i))

    if fused:
        for k in range(1, N):
            copy_act(k, d).start()
        actall[d] = act[...]

    xrows = x_ref[rows_at(i)].astype(F32)
    rrows = lax.rsqrt(jnp.mean(xrows * xrows, axis=-1, keepdims=True) + 1e-06)

    loads[1].wait()
    for c in chunks:
        base = dot_nt(act[...], wd[c, :])
        part[:, c] = base

    loads[2].wait()
    loads[3].wait()

    @pl.when(s == 0)
    def _():
        partb[...] = part[...].astype(BF)

    @pl.when(s > 0)
    def _():
        total = None
        for j in range(T):
            remote(partb.at[rows_at(j)], in_a.at[j], a_send.at[j], a_recv.at[j], at(d, s, i)).wait_recv()
        for j in range(T):
            piece = in_a[j].astype(F32)
            total = piece if total is None else total + piece
        tfloat = total.astype(BF).astype(F32)
        trow[...] = tfloat
        tn[rows_at(i)] = (
            gain * (rrows * tfloat - rrows**3 * xrows * jnp.mean(xrows * tfloat, axis=-1, keepdims=True))
        ).astype(BF)
        for k in range(1, T):
            copy_tn(k, i).start()
        for k in range(1, T):
            copy_tn(k, peer(i, T - k, T)).wait_recv()
        tmix = mix(dot_nt(tn[...], wv[...]).astype(BF)).astype(BF)
        for c in chunks:
            part[:, c] = part[:, c] + dot_nt(tmix, wo[c, :])
        part[rows_at(i)] = part[rows_at(i)] + trow[...]
        partb[...] = part[...].astype(BF)
        for k in range(1, T):
            copy_tn(k, i).wait_send()

    if S > 1:

        @pl.when(s < S - 1)
        def _():
            for j in range(T):
                copy_a(j, i).start()

    @pl.when(s == S - 1)
    def _():
        for k in range(1, T):
            copy_d(k).start()
        total = part[rows_at(i)]
        for k in range(1, T):
            copy_d(k).wait_recv()
        for k in range(1, T):
            total = total + in_d[k - 1].astype(F32)
        tlast = total.astype(BF).astype(F32)
        gfull[rows_at(i)] = (curv[rows_at(i)].astype(F32) * tlast).astype(BF)
        for k in range(1, T):
            copy_s(k, i).start()
        for k in range(1, T):
            copy_s(k, peer(i, T - k, T)).wait_recv()
        for k in range(1, T):
            copy_s(k, i).wait_send()
            copy_d(k).wait_send()

    if S > 1:

        @pl.when(s < S - 1)
        def _():
            for j in range(T):
                copy_a(j, i).wait_send()

        def gather_rows():
            for j in range(T):
                remote(grow, gfull.at[rows_at(j)], h_send.at[0, j], h_recv.at[0, j], at(d, s, i)).wait_recv()

        if fused:
            if S > 2:

                @pl.when(jnp.logical_and(s > 0, s < S - 1))
                def _():
                    gather_rows()

            @pl.when(s == 0)
            def _():
                for k in range(N):
                    for j in range(T):
                        land_hd(k, j).wait_recv()
        else:

            @pl.when(s < S - 1)
            def _():
                gather_rows()

        @pl.when(s > 0)
        def _():
            gm = dot_nn(gfull[...], wo[...]).astype(BF)
            gv = jnp.concatenate(
                [dot_tn(probs_ref[h], gm[:, h * hd : (h + 1) * hd]) for h in range(heads)], axis=1
            ).astype(BF)
            for c in chunks:
                gc = dot_nn(gv, wv[:, c])
                part[:, c] = gc
                gpartb[:, c] = gc.astype(BF)
            for k in range(1, T):
                copy_f(k).start()
            total = part[rows_at(i)]
            for k in range(1, T):
                copy_f(k).wait_recv()
            for k in range(1, T):
                total = total + in_f[k - 1].astype(F32)
            scaled = gain * total
            gx = rrows * scaled - rrows**3 * xrows * jnp.mean(xrows * scaled, axis=-1, keepdims=True)
            grow[...] = (gfull[rows_at(i)].astype(F32) + gx).astype(BF)

            def plain():
                for j in range(T):
                    copy_h(j, i).start()
                for j in range(T):
                    copy_h(j, i).wait_send()

            if fused:

                @pl.when(s == 1)
                def _():
                    for k in range(N):
                        for j in range(T):
                            copy_hd(k, j, i).start()
                    for k in range(N):
                        for j in range(T):
                            copy_hd(k, j, i).wait_send()

                if S > 2:
                    pl.when(s > 1)(plain)
            else:
                plain()
            for k in range(1, T):
                copy_f(k).wait_send()

    if fused:

        def spread():
            for k in range(1, N):
                copy_x(k).start()
            gall[d] = gfull[:, feats_at(d)]
            for k in range(1, N):
                land_x(k).wait_recv()
            for k in range(1, N):
                copy_x(k).wait_send()

        if S > 1:
            pl.when(s > 0)(spread)
        else:
            spread()
        for k in range(1, N):
            copy_act(k, peer(d, N - k, N)).wait_recv()
        prod_ref[...] = dot_tn(
            gall[...].reshape(N * tok, feats), actall[...].reshape(N * tok, act.shape[1])
        )
        for k in range(1, N):
            copy_act(k, d).wait_send()
    else:
        gout_ref[...] = gfull[...]
        actout_ref[...] = act[...]


def home_share(feats, g, q):
    more = 1 if MORE[g] > 0 else -1
    return (feats // 256 + (more if q < abs(MORE[g]) else 0)) * 128


def kernel_pair(
    T, N,
    x_hbm, gain_hbm, probs_hbm, wv_hbm, wd_hbm, wo_hbm, curv_hbm,
    gall, actall,
    x_ref, gain_ref, probs_ref, wv, wd, wo, curv, act, vals, tvals, part, tbuf, gbuf, xrow, gain1,
    a_src, a_hop, a_land, d_src, d_hop, d_land, f_src, f_hop, f_land,
    grow,
    load_sem, lend_send, lend_recv, act_send, act_recv,
    hop_send, hop_recv, rs_send, rs_recv, ag_send, ag_recv, ag_pass, pass_send,
    h_send, h_self, h_recv, x_send, x_recv,
):
    d = lax.axis_index("dp")
    s = lax.axis_index("section")
    i = lax.axis_index("tensor")
    tok, width = x_hbm.shape
    K = TOKEN_CHUNKS
    Q = N
    ck = tok // K
    blk = ck // T
    feats = width // N
    heads = probs_ref.shape[0]
    hd = wv.shape[0] // heads
    end = jnp.logical_or(i == 0, i == T - 1)
    mid = jnp.logical_not(end)
    mate = jnp.bitwise_xor(i, 1)
    cross = jnp.where(end, T - 1 - mate, T - 1 - i)
    other = T - 1 - mate
    far = [k for k in range(2, T - 1)] + [k for k in range(1, T) if k in (1, T - 1)]
    subs = range(Q)

    def peer(me, k, n):
        return lax.rem(me + k, n)

    def at(dd, ss, jj):
        return {"dp": dd, "section": ss, "tensor": jj}

    def chunk(kk):
        return slice(kk * ck, (kk + 1) * ck)

    def rows(kk, j):
        return pl.ds(pl.multiple_of(kk * ck + j * blk, blk), blk)

    def share(g, y, q):
        return home_share(feats, g, q) if y == g else feats - home_share(feats, g, q)

    def part_of(g, y, q):
        lo = share(g, 0, q) if y == 1 else 0
        return slice(lo, lo + share(g, y, q))

    def col(g, y, q):
        c = part_of(g, y, q)
        return slice(q * feats + c.start, q * feats + c.stop)

    def block(b):
        return slice(b * feats, (b + 1) * feats)

    def feats_at(j):
        return pl.ds(pl.multiple_of(j * feats, 128), feats)

    def seq_rows(kk):
        return pl.ds(pl.multiple_of(d * tok + kk * ck, ck), ck)

    def own_rows(kk):
        return pl.ds(pl.multiple_of(d * tok + kk * ck + i * blk, blk), blk)

    def remote(src, dst, send, recv, dev):
        return pltpu.make_async_remote_copy(
            src_ref=src, dst_ref=dst, send_sem=send, recv_sem=recv,
            device_id=dev, device_id_type=MESH,
        )

    def landed(ref, sem):
        remote(ref, ref, sem, sem, at(d, s, i)).wait_recv()

    def sent(ref, sem):
        remote(ref, ref, sem, sem, at(d, s, i)).wait_send()

    loads = [
        pltpu.make_async_copy(src, dst, load_sem.at[k])
        for k, (src, dst) in enumerate(((wv_hbm, wv), (wd_hbm, wd), (wo_hbm, wo), (curv_hbm, curv)))
    ]
    first = [
        pltpu.make_async_copy(x_hbm.at[chunk(kk)], x_ref.at[chunk(kk)], load_sem.at[4 + kk]) for kk in range(K)
    ] + [
        pltpu.make_async_copy(gain_hbm, gain_ref, load_sem.at[4 + K]),
        pltpu.make_async_copy(probs_hbm, probs_ref, load_sem.at[5 + K]),
    ]
    first[K].start()
    first[0].start()
    loads[0].start()
    for copy in first[1:K] + first[K + 1 :]:
        copy.start()
    loads[1].start()

    barrier = pltpu.get_barrier_semaphore()
    for a in range(N):
        for b in range(2):
            for c in range(T):
                if (a == 0) != (b == 0 and c == 0):
                    pl.semaphore_signal(
                        barrier, inc=1, device_id=at(peer(d, a, N), peer(s, b, 2), peer(i, c, T)),
                        device_id_type=MESH,
                    )
    loads[2].start()
    loads[3].start()

    def mix(kk, buf):
        r = chunk(kk)
        return jnp.concatenate(
            [dot_nn(probs_ref[h, r, :], buf[:, h * hd : (h + 1) * hd]) for h in range(heads)], axis=1
        ).astype(BF)

    def rnorm_of(xf):
        return lax.rsqrt(jnp.mean(xf * xf, axis=-1, keepdims=True) + 1e-06)

    def values_of(kk):
        first[kk].wait()
        r = chunk(kk)
        xf = x_ref[r, :].astype(F32)
        normed = (xf * rnorm_of(xf) * gain).astype(BF)
        vals[r, :] = dot_nt(normed, wv[...]).astype(BF)

    def acts_of(kk):
        act[chunk(kk), :] = mix(kk, vals)

    first[K].wait()
    gain = gain_ref[...]
    for kk in range(1, K):
        vals[chunk(kk), :] = jnp.zeros((ck, vals.shape[1]), BF)
        tvals[chunk(kk), :] = jnp.zeros((ck, vals.shape[1]), BF)

    def copy_act(k, owner):
        return remote(act, actall.at[owner], act_send.at[k], act_recv.at[k], at(peer(d, k, N), s, i))

    keep_act = pltpu.make_async_copy(act, actall.at[d], act_send.at[0])

    def keep_rows(kk):
        return pltpu.make_async_copy(gbuf.at[chunk(kk), feats_at(d)], gall.at[seq_rows(kk)], x_send.at[K + kk])

    lend = [
        remote(x_ref.at[rows(kk, i)], xrow.at[kk], lend_send.at[kk], lend_recv.at[kk], at(d, 0, i))
        for kk in range(K)
    ] + [remote(gain_ref, gain1, lend_send.at[K], lend_recv.at[K], at(d, 0, i))]

    A, D_, F_ = (0, a_src, a_hop, a_land, 0), (1, d_src, d_hop, d_land, 1), (2, f_src, f_hop, f_land, 1)

    def cw(p, y, q):
        return slice(0, share(p[4], y, q) + (128 if p[0] == 2 and q == 0 else 0))

    def hop(p, kk, q):
        y = 1 - p[4]
        c = cw(p, y, q)
        r = chunk(kk)
        remote(
            p[1].at[y, q, r, c], p[2].at[q, r, c], hop_send.at[p[0], kk, q], hop_recv.at[p[0], kk, q], at(d, y, i)
        ).start()

    def hop_done(p, kk, q):
        sent(p[1].at[1 - p[4], q, chunk(kk), cw(p, 1 - p[4], q)], hop_send.at[p[0], kk, q])

    def scatter(p, me, kk, q):
        c = cw(p, me, q)
        if me != p[4]:
            landed(p[2].at[q, chunk(kk), c], hop_recv.at[p[0], kk, q])
        buf = p[1].at[me, q] if me == p[4] else p[2].at[q]
        for k in far:
            j = peer(i, k, T)
            remote(
                buf.at[rows(kk, j), c], p[3].at[q, kk, k - 1, :, c], rs_send.at[p[0], kk, q],
                rs_recv.at[p[0], kk, q], at(d, me, j),
            ).start()

    def scatter_done(p, me, kk, q):
        sent(p[3].at[q, kk, :, :, cw(p, me, q)], rs_send.at[p[0], kk, q])

    def collect(p, me, kk, q, local):
        c = cw(p, me, q)
        total = p[2][q, rows(kk, i), c].astype(F32) if me != p[4] else local
        landed(p[3].at[q, kk, :, :, c], rs_recv.at[p[0], kk, q])
        for k in range(T - 1):
            total = total + p[3][q, kk, k, :, c].astype(F32)
        return total

    def spread_copies(n, buf, me, kk, q):
        src = buf.at[rows(kk, i), col(n, me, q)]
        if not RELAY[n]:
            return [
                remote(src, src, ag_send.at[n, kk, q, k], ag_recv.at[n, me, kk, q], at(d, 1, peer(i, k, T)))
                for k in far + ([0] if me == 0 else [])
            ]
        out = [
            remote(src, src, ag_send.at[n, kk, q, 1], ag_pass.at[n, me, kk, q], at(d, me, cross)),
            remote(src, src, ag_send.at[n, kk, q, 2], ag_recv.at[n, me, kk, q], at(d, 1, mate)),
        ]
        if me == 0:
            out.append(remote(src, src, ag_send.at[n, kk, q, 0], ag_recv.at[n, me, kk, q], at(d, 1, i)))
        return out

    def pass_copies(n, buf, me, kk, q):
        out = []
        for m, j in ((0, cross), (1, other)):
            src = buf.at[rows(kk, j), col(n, me, q)]
            land = ag_pass if me == 1 else ag_recv
            out.append(remote(src, src, pass_send.at[n, kk, q, m], land.at[n, me, kk, q], at(d, 1, mate)))
            if me == 0:
                out.append(remote(src, src, pass_send.at[n, kk, q, 2 + m], land.at[n, me, kk, q], at(d, 1, i)))
        return out

    def spread(n, buf, me, kk, q):
        for copy in spread_copies(n, buf, me, kk, q):
            copy.start()

    def pass_on(n, buf, me, kk, q):
        if not RELAY[n]:
            return
        pair = buf.at[kk * ck : kk * ck + 2 * blk, col(n, me, q)]
        if me == 1:
            landed(pair, ag_pass.at[n, me, kk, q])

        @pl.when(mid)
        def _():
            if me == 0:
                landed(pair, ag_pass.at[n, me, kk, q])
            for copy in pass_copies(n, buf, me, kk, q):
                copy.start()

    def spread_done(n, buf, me, kk, q):
        for copy in spread_copies(n, buf, me, kk, q):
            copy.wait_send()
        if RELAY[n]:

            @pl.when(mid)
            def _():
                for copy in pass_copies(n, buf, me, kk, q):
                    copy.wait_send()

    def gathered(n, buf, y, kk, q):
        count = T if y == 0 else T - 1
        if RELAY[n] and y == 1:
            count = 1
        landed(buf.at[kk * ck : kk * ck + count * blk, col(n, y, q)], ag_recv.at[n, y, kk, q])

    def ready(n, buf, kk, b):
        for y in (1, 0):
            gathered(n, buf, y, kk, b)

    def pack(p, buf, kk, b):
        home = p[4]
        for y in (1 - home, home):
            p[1][y, b, chunk(kk), 0 : share(home, y, b)] = buf[chunk(kk), col(home, y, b)].astype(BF)
            if y == home:
                scatter(p, home, kk, b)
            else:
                hop(p, kk, b)

    def done(me, sums, gathers):
        for kk in range(K):
            for q in subs:
                for p in sums:
                    if me == p[4]:
                        hop_done(p, kk, q)
                    scatter_done(p, me, kk, q)
                for n, buf in gathers:
                    spread_done(n, buf, me, kk, q)

    def tangent(me, kk, q):
        r = rows(kk, i)
        c = col(0, me, q)
        tbuf[r, c] = collect(A, me, kk, q, part[r, c]).astype(BF)
        spread(0, tbuf, me, kk, q)

    def seed(me, kk, q):
        r = rows(kk, i)
        c = col(1, me, q)
        total = collect(D_, me, kk, q, part[r, c])
        gbuf[r, c] = (curv[r, c].astype(F32) * total.astype(BF).astype(F32)).astype(BF)
        spread(1, gbuf, me, kk, q)

    def hand(me, kk, q, start):
        dd = q
        c = part_of(1, me, q)
        src = grow.at[kk, q, :, 0 : share(1, me, q)]
        dst = gall.at[own_rows(kk), c]

        if start:
            for k in far:
                remote(src, dst, h_send.at[kk, q], h_recv.at[kk, me], at(dd, 0, peer(i, k, T))).start()
        else:
            sent(gall.at[0 : (T - 1) * blk, c], h_send.at[kk, q])

        def direct():
            if start:
                remote(src, dst, h_self.at[kk, q], h_recv.at[kk, me], at(dd, 0, i)).start()
            else:
                sent(src, h_self.at[kk, q])

        if me == 1:
            direct()
        else:
            pl.when(d != dd)(direct)

            @pl.when(d == dd)
            def _():
                own = pltpu.make_async_copy(src, dst, h_self.at[kk, q])
                own.start() if start else own.wait()

    def adjoint(me, kk, xr, gn, rr):
        weight = None
        for q in subs:
            c = col(1, me, q)
            wide = share(1, me, q)
            local = f_src[1, q, rows(kk, i), cw(F_, 1, q)].astype(F32) if me == 1 else None
            total = collect(F_, me, kk, q, local)
            if q == 0:
                weight = jnp.sum(total[:, wide:], axis=-1, keepdims=True) * (rr * rr * (2.0 / 128 / width))
                total = total[:, :wide]
            g1 = gbuf[rows(kk, i), c].astype(F32) + (rr * gn[:, c]) * total - xr[:, c] * weight
            grow[kk, q, :, 0:wide] = g1.astype(BF)
            hand(me, kk, q, True)

    @pl.when(s == 0)
    def _():
        loads[0].wait()
        first[K + 1].wait()
        values_of(0)
        acts_of(0)
        pl.semaphore_wait(barrier, 2 * T + N - 2)
        loads[1].wait()
        for kk in range(K):
            if kk:
                values_of(kk)
                acts_of(kk)
            for b in range(N):
                part[chunk(kk), block(b)] = dot_nt(act[chunk(kk), :], wd[block(b), :])
                pack(A, part, kk, b)
        for k in range(1, N):
            copy_act(k, d).start()
        keep_act.start()
        for kk in range(K):
            for q in subs:
                tangent(0, kk, q)
        for kk in range(K):
            for q in subs:
                pass_on(0, tbuf, 0, kk, q)
        for copy in lend:
            copy.wait_recv()
        loads[2].wait()
        loads[3].wait()
        for kk in range(K):
            for q in subs:
                scatter(D_, 0, kk, q)
        done(0, (A,), ())
        for kk in range(K):
            for q in subs:
                seed(0, kk, q)
        for kk in range(K):
            for q in subs:
                pass_on(1, gbuf, 0, kk, q)
        done(0, (), ((0, tbuf),))
        for k in range(1, N):
            copy_act(k, d).wait_send()
        keep_act.wait()
        gn = gain1[...]
        for kk in reversed(range(K)):
            for q in subs:
                scatter(F_, 0, kk, q)
        done(0, (D_,), ((1, gbuf),))
        for kk in reversed(range(K)):
            xr = xrow[kk].astype(F32)
            rr = rnorm_of(xr)
            adjoint(0, kk, xr, gn, rr)
        for k in range(1, N):
            copy_act(k, peer(d, N - k, N)).wait_recv()
        done(0, (F_,), ())
        for kk in reversed(range(K)):
            for q in subs:
                hand(0, kk, q, False)
        for n, kk in enumerate(reversed(range(K))):

            for dd in range(N):

                @pl.when(d == dd)
                def _():
                    landed(gall.at[0 : N * ck - blk, part_of(1, 0, dd)], h_recv.at[kk, 0])
                    landed(gall.at[0 : N * ck, part_of(1, 1, dd)], h_recv.at[kk, 1])

    @pl.when(s == 1)
    def _():
        loads[0].wait()
        first[K + 1].wait()
        for kk in range(K):
            values_of(kk)
            acts_of(kk)
        pl.semaphore_wait(barrier, 2 * T + N - 2)
        for copy in lend:
            copy.start()
        for k in range(1, N):
            copy_act(k, d).start()
        keep_act.start()
        loads[1].wait()
        for b in range(N):
            part[:, block(b)] = dot_nt(act[...], wd[block(b), :])
        loads[2].wait()
        loads[3].wait()
        for kk in range(K):
            for q in subs:
                scatter(A, 1, kk, q)
        for kk in range(K):
            for q in subs:
                tangent(1, kk, q)
        for kk in range(K):
            r = chunk(kk)
            tv = None
            mean = None
            for b in range(N):
                pass_on(0, tbuf, 1, kk, b)
            for b in range(N):
                ready(0, tbuf, kk, b)
                c = block(b)
                tf = tbuf[r, c].astype(F32)
                dotted = jnp.sum(x_ref[r, c].astype(F32) * tf, axis=-1, keepdims=True)
                more = dot_nt((gain[:, c] * tf).astype(BF), wv[:, c])
                tv = more if tv is None else tv + more
                mean = dotted if mean is None else mean + dotted
            rr = rnorm_of(x_ref[r, :].astype(F32))
            tvals[r, :] = (rr * tv - (rr * rr * (1.0 / width) * mean) * vals[r, :].astype(F32)).astype(BF)
            tmix = mix(kk, tvals)
            for b in range(N):
                part[r, block(b)] = part[r, block(b)] + dot_nt(tmix, wo[block(b), :])
                mine = rows(kk, i)
                part[mine, block(b)] = part[mine, block(b)] + tbuf[mine, block(b)].astype(F32)
                pack(D_, part, kk, b)
        for copy in lend:
            copy.wait_send()
        done(1, (A,), ())
        for kk in range(K):
            for q in subs:
                seed(1, kk, q)
        done(1, (), ((0, tbuf),))
        for k in range(1, N):
            copy_act(k, d).wait_send()
        keep_act.wait()

        def copy_x(kk, k):
            dd = peer(d, k, N)
            return remote(
                gbuf.at[chunk(kk), feats_at(dd)], gall.at[seq_rows(kk)], x_send.at[kk], x_recv.at[kk], at(dd, s, i)
            )

        gms = []
        for kk in range(K):
            gm = None
            for b in range(N):
                pass_on(1, gbuf, 1, kk, b)
            for b in range(N):
                ready(1, gbuf, kk, b)
                more = dot_nn(gbuf[chunk(kk), block(b)], wo[block(b), :])
                gm = more if gm is None else gm + more
            gms.append(gm.astype(BF))
        pending = None
        for kk in reversed(range(K)):
            r = chunk(kk)
            more = jnp.concatenate(
                [dot_tn(probs_ref[h, r, :], gms[kk][:, h * hd : (h + 1) * hd]) for h in range(heads)], axis=1
            )
            pending = more if pending is None else pending + more
            gv = pending[r, :].astype(BF)
            weight = jnp.sum(gv.astype(F32) * vals[r, :].astype(F32), axis=-1, keepdims=True)
            high = weight.astype(BF).astype(F32)
            lane = lax.broadcasted_iota(jnp.int32, (ck, 128), 1)
            extra = jnp.where(lane < 64, high, weight - high).astype(BF)
            for y in (0, 1):
                f_src[y, 0, r, share(1, y, 0) : share(1, y, 0) + 128] = extra
            for b in range(N):
                part[r, block(b)] = dot_nn(gv, wv[:, block(b)])
                pack(F_, part, kk, b)
        for kk in range(K):
            for k in range(1, N):
                copy_x(kk, k).start()
            keep_rows(kk).start()
        done(1, (D_,), ((1, gbuf),))
        for k in range(1, N):
            copy_act(k, peer(d, N - k, N)).wait_recv()
        for kk in range(K):
            landed(gall.at[0 : (N - 1) * ck], x_recv.at[kk])
        for kk in reversed(range(K)):
            xr = x_ref[rows(kk, i), :].astype(F32)
            adjoint(1, kk, xr, gain, rnorm_of(xr))
        done(1, (F_,), ())
        for kk in range(K):
            sent(gall.at[0 : (N - 1) * ck], x_send.at[kk])
            keep_rows(kk).wait()
            for q in subs:
                hand(1, kk, q, False)


def call_pair(T, N, x, norm_gain, probs, w_val, w_dir, w_out, curvature):
    tok, width = x.shape
    hf = w_val.shape[0]
    K = TOKEN_CHUNKS
    Q = N
    ck = tok // K
    blk = ck // T
    feats = width // N
    wide = max(max(home_share(feats, g, q), feats - home_share(feats, g, q)) for g in (0, 1) for q in range(N))
    hbm = functools.partial(pl.BlockSpec, memory_space=pl.ANY)
    sem = pltpu.SemaphoreType.DMA

    def sums(cols):
        return [
            pltpu.VMEM((2, Q, tok, cols), BF),
            pltpu.VMEM((Q, tok, cols), BF),
            pltpu.VMEM((Q, K, T - 1, blk, cols), BF),
        ]

    scratch = [
        pltpu.VMEM((tok, width), BF),
        pltpu.VMEM((1, width), F32),
        pltpu.VMEM(probs.shape, BF),
        pltpu.VMEM((hf, width), BF),
        pltpu.VMEM((width, hf), BF),
        pltpu.VMEM((width, hf), BF),
        pltpu.VMEM((tok, width), BF),
        pltpu.VMEM((tok, hf), BF),
        pltpu.VMEM((tok, hf), BF),
        pltpu.VMEM((tok, hf), BF),
        pltpu.VMEM((tok, width), F32),
        pltpu.VMEM((tok, width), BF),
        pltpu.VMEM((tok, width), BF),
        pltpu.VMEM((K, blk, width), BF),
        pltpu.VMEM((1, width), F32),
        *sums(wide), *sums(wide), *sums(wide + 128),
        pltpu.VMEM((K, Q, blk, wide), BF),
        sem((6 + K,)),
        sem((K + 1,)), sem((K + 1,)),
        sem((N,)), sem((N,)),
        sem((3, K, Q)), sem((3, K, Q)),
        sem((3, K, Q)), sem((3, K, Q)),
        sem((2, K, Q, T)), sem((2, 2, K, Q)), sem((2, 2, K, Q)), sem((2, K, Q, T)),
        sem((K, Q)), sem((K, Q)), sem((K, 2)),
        sem((2 * K,)), sem((K,)),
    ]
    adjoints, acts = pl.pallas_call(
        functools.partial(kernel_pair, T, N),
        out_shape=(
            jax.ShapeDtypeStruct((N * tok, feats), BF), jax.ShapeDtypeStruct((N, tok, hf), BF),
        ),
        in_specs=[hbm()] * 7,
        out_specs=(hbm(), hbm()),
        scratch_shapes=scratch,
        compiler_params=pltpu.CompilerParams(
            collective_id=0, has_side_effects=True, vmem_limit_bytes=56 * 1024 * 1024
        ),
    )(x, norm_gain, probs, w_val, w_dir, w_out, curvature)
    return dot_tn(adjoints, acts.reshape(N * tok, hf))


def per_device(section_input, norm_gain, value_weight, attn_probs, out_weight, direction, curvature):
    x = section_input[0]
    w_val = value_weight[0]
    w_out = out_weight[0]
    w_dir = direction[0]
    probs = attn_probs[0]
    S = lax.axis_size("section")
    T = lax.axis_size("tensor")
    N = lax.axis_size("dp")
    tok, width = x.shape
    hf = w_val.shape[0]
    rows = tok // T
    feats = width // N
    fused = feats % 128 == 0 and feats * N == width
    blocks = tok % (16 * T * TOKEN_CHUNKS) == 0
    if fused and S == 2 and T == 4 and feats % 256 == 0 and blocks:
        return call_pair(T, N, x, norm_gain, probs, w_val, w_dir, w_out, curvature)[None]
    vm = functools.partial(pl.BlockSpec, memory_space=pltpu.VMEM)
    hbm = functools.partial(pl.BlockSpec, memory_space=pl.ANY)
    if fused:
        outs = jax.ShapeDtypeStruct((feats, hf), F32)
        out_specs = vm()
    else:
        outs = (jax.ShapeDtypeStruct((tok, width), BF), jax.ShapeDtypeStruct((tok, hf), BF))
        out_specs = (vm(), vm())
    sem = pltpu.SemaphoreType.DMA
    wide = N if fused else 1
    scratch = [
        pltpu.VMEM((hf, width), BF),
        pltpu.VMEM((width, hf), BF),
        pltpu.VMEM((width, hf), BF),
        pltpu.VMEM((tok, width), BF),
        pltpu.VMEM((tok, hf), BF),
        pltpu.VMEM((tok, width), F32),
        pltpu.VMEM((tok, width), BF),
        pltpu.VMEM((T, rows, width), BF),
        pltpu.VMEM((T, rows, width), BF),
        pltpu.VMEM((T, rows, width), BF),
        pltpu.VMEM((tok, width), BF),
        pltpu.VMEM((tok, width), BF),
        pltpu.VMEM((tok, width), BF),
        pltpu.VMEM((tok, width), BF),
        pltpu.VMEM((rows, width), F32),
        pltpu.VMEM((rows, width), BF),
        pltpu.VMEM((wide, tok, hf), BF),
        pltpu.VMEM((wide, tok, feats if fused else 128), BF),
        sem((4,)),
        sem((N,)), sem((N,)),
        sem((T,)), sem((T,)),
        sem((T,)), sem((T,)),
        sem((T,)), sem((T,)),
        sem((T,)), sem((T,)),
        sem((T,)), sem((T,)),
        sem((wide, T)), sem((wide, T)),
        sem((N,)), sem((N,)),
    ]
    result = pl.pallas_call(
        functools.partial(kernel, fused, S, T, N),
        out_shape=outs,
        in_specs=[vm(), vm(), vm(), hbm(), hbm(), hbm(), hbm()],
        out_specs=out_specs,
        scratch_shapes=scratch,
        compiler_params=pltpu.CompilerParams(
            collective_id=0, has_side_effects=True, vmem_limit_bytes=56 * 1024 * 1024
        ),
    )(x, norm_gain, probs, w_val, w_dir, w_out, curvature)
    if fused:
        return result[None]
    adjoint, act = result
    product = lax.psum_scatter(
        dot_tn(adjoint, act).astype(BF), "dp", scatter_dimension=0, tiled=True
    ).astype(F32)
    return product[None]


def solution(mesh):
    in_specs = (
        P("section", "dp", None),
        P("section", None),
        P("section", "tensor", None),
        P("section", "tensor", "dp", None),
        P("section", None, "tensor"),
        P("section", None, "tensor"),
        P("dp", None),
    )
    out_specs = P("section", "dp", "tensor")
    return jax.shard_map(
        per_device, mesh=mesh, in_specs=in_specs, out_specs=out_specs, check_vma=False
    )
```

```python
import functools

import jax
import jax.numpy as jnp
from jax import lax
from jax.experimental import pallas as pl
from jax.experimental.pallas import tpu as pltpu
from jax.sharding import PartitionSpec as P

MESH = pl.DeviceIdType.MESH
BF = jnp.bfloat16
F32 = jnp.float32
TOKEN_CHUNKS = 2
MORE = (1, 0)
RELAY = (True, False)


def dot_nt(a, b):
    return lax.dot_general(a, b, (((1,), (1,)), ((), ())), preferred_element_type=F32)


def dot_tn(a, b):
    return lax.dot_general(a, b, (((0,), (0,)), ((), ())), preferred_element_type=F32)


def dot_nn(a, b):
    return lax.dot_general(a, b, (((1,), (0,)), ((), ())), preferred_element_type=F32)


def kernel(
    fused, S, T, N,
    x_ref, gain_ref, probs_ref, wv_hbm, wd_hbm, wo_hbm, curv_hbm,
    *rest,
):
    if fused:
        prod_ref, rest = rest[0], rest[1:]
    else:
        gout_ref, actout_ref, rest = rest[0], rest[1], rest[2:]
    (
        wv, wd, wo, curv, act, part, partb, in_a, in_d, in_f, gpartb, normed, tn, gfull, trow, grow,
        actall, gall,
        load_sem, act_send, act_recv, a_send, a_recv, tn_send, tn_recv, d_send, d_recv,
        s_send, s_recv, f_send, f_recv, h_send, h_recv, x_send, x_recv,
    ) = rest
    d = lax.axis_index("dp")
    s = lax.axis_index("section")
    i = lax.axis_index("tensor")
    tok, width = x_ref.shape
    rows = tok // T
    heads = probs_ref.shape[0]
    hd = wv.shape[0] // heads
    feats = width // N
    CH = 512 if width % 512 == 0 else width
    chunks = [slice(c, c + CH) for c in range(0, width, CH)]

    def rows_at(j):
        return pl.ds(pl.multiple_of(j * rows, rows), rows)

    def feats_at(j):
        return pl.ds(pl.multiple_of(j * feats, 128), feats)

    def peer(me, k, n):
        return lax.rem(me + k, n)

    loads = [
        pltpu.make_async_copy(src, dst, load_sem.at[k])
        for k, (src, dst) in enumerate(((wv_hbm, wv), (wd_hbm, wd), (wo_hbm, wo), (curv_hbm, curv)))
    ]
    for copy in loads:
        copy.start()

    barrier = pltpu.get_barrier_semaphore()

    def greet(dev):
        pl.semaphore_signal(barrier, inc=1, device_id=dev, device_id_type=MESH)

    for k in range(1, T):
        greet({"dp": d, "section": s, "tensor": peer(i, k, T)})
    for k in range(1, N):
        greet({"dp": peer(d, k, N), "section": s, "tensor": i})
    for low in range(S - 1):
        wide = N if (fused and low == 0) else 1

        @pl.when(s == low)
        def _():
            for k in range(wide):
                for j in range(T):
                    greet({"dp": peer(d, k, N), "section": s + 1, "tensor": j})

        @pl.when(s == low + 1)
        def _():
            for k in range(wide):
                for j in range(T):
                    greet({"dp": peer(d, k, N), "section": s - 1, "tensor": j})

    gain = gain_ref[...]
    xf = x_ref[...].astype(F32)
    rnorm = lax.rsqrt(jnp.mean(xf * xf, axis=-1, keepdims=True) + 1e-06)
    normed[...] = (xf * rnorm * gain).astype(BF)

    def mix(vals):
        return jnp.concatenate(
            [dot_nn(probs_ref[h], vals[:, h * hd : (h + 1) * hd]) for h in range(heads)], axis=1
        )

    loads[0].wait()
    act[...] = mix(dot_nt(normed[...], wv[...]).astype(BF)).astype(BF)

    for here in range(S):
        count = T - 1 + N - 1
        for low in (here - 1, here):
            if 0 <= low < S - 1:
                count += T * (N if (fused and low == 0) else 1)

        @pl.when(s == here)
        def _():
            pl.semaphore_wait(barrier, count)

    def remote(src, dst, send, recv, dev):
        return pltpu.make_async_remote_copy(
            src_ref=src, dst_ref=dst, send_sem=send, recv_sem=recv,
            device_id=dev, device_id_type=MESH,
        )

    def at(dd, ss, jj):
        return {"dp": dd, "section": ss, "tensor": jj}

    def copy_act(k, owner):
        return remote(act, actall.at[owner], act_send.at[k], act_recv.at[k], at(peer(d, k, N), s, i))

    def copy_a(j, owner):
        return remote(partb.at[rows_at(j)], in_a.at[owner], a_send.at[j], a_recv.at[owner], at(d, s + 1, j))

    def copy_tn(k, owner):
        return remote(
            tn.at[rows_at(owner)], tn.at[rows_at(owner)], tn_send.at[k], tn_recv.at[k], at(d, s, peer(i, k, T))
        )

    def copy_d(k):
        j = peer(i, k, T)
        return remote(partb.at[rows_at(j)], in_d.at[k - 1], d_send.at[k], d_recv.at[k], at(d, s, j))

    def copy_s(k, owner):
        return remote(
            gfull.at[rows_at(owner)], gfull.at[rows_at(owner)], s_send.at[k], s_recv.at[k],
            at(d, s, peer(i, k, T)),
        )

    def copy_f(k):
        j = peer(i, k, T)
        return remote(gpartb.at[rows_at(j)], in_f.at[k - 1], f_send.at[k], f_recv.at[k], at(d, s, j))

    def copy_h(j, owner):
        return remote(grow, gfull.at[rows_at(owner)], h_send.at[0, j], h_recv.at[0, owner], at(d, s - 1, j))

    def copy_hd(k, j, owner):
        dd = peer(d, k, N)
        return remote(
            grow.at[:, feats_at(dd)], gall.at[lax.rem(d, N), rows_at(owner)],
            h_send.at[k, j], h_recv.at[k, owner], at(dd, s - 1, j),
        )

    def land_hd(k, owner):
        src = peer(d, N - k, N)
        return remote(
            grow.at[:, feats_at(d)], gall.at[src, rows_at(owner)],
            h_send.at[k, owner], h_recv.at[k, owner], at(d, s, i),
        )

    def copy_x(k):
        dd = peer(d, k, N)
        return remote(gfull.at[:, feats_at(dd)], gall.at[d], x_send.at[k], x_recv.at[k], at(dd, s, i))

    def land_x(k):
        src = peer(d, N - k, N)
        return remote(gfull.at[:, feats_at(d)], gall.at[src], x_send.at[k], x_recv.at[k], at(d, s, i))

    if fused:
        for k in range(1, N):
            copy_act(k, d).start()
        actall[d] = act[...]

    xrows = x_ref[rows_at(i)].astype(F32)
    rrows = lax.rsqrt(jnp.mean(xrows * xrows, axis=-1, keepdims=True) + 1e-06)

    loads[1].wait()
    for c in chunks:
        base = dot_nt(act[...], wd[c, :])
        part[:, c] = base

    loads[2].wait()
    loads[3].wait()

    @pl.when(s == 0)
    def _():
        partb[...] = part[...].astype(BF)

    @pl.when(s > 0)
    def _():
        total = None
        for j in range(T):
            remote(partb.at[rows_at(j)], in_a.at[j], a_send.at[j], a_recv.at[j], at(d, s, i)).wait_recv()
        for j in range(T):
            piece = in_a[j].astype(F32)
            total = piece if total is None else total + piece
        tfloat = total.astype(BF).astype(F32)
        trow[...] = tfloat
        tn[rows_at(i)] = (
            gain * (rrows * tfloat - rrows**3 * xrows * jnp.mean(xrows * tfloat, axis=-1, keepdims=True))
        ).astype(BF)
        for k in range(1, T):
            copy_tn(k, i).start()
        for k in range(1, T):
            copy_tn(k, peer(i, T - k, T)).wait_recv()
        tmix = mix(dot_nt(tn[...], wv[...]).astype(BF)).astype(BF)
        for c in chunks:
            part[:, c] = part[:, c] + dot_nt(tmix, wo[c, :])
        part[rows_at(i)] = part[rows_at(i)] + trow[...]
        partb[...] = part[...].astype(BF)
        for k in range(1, T):
            copy_tn(k, i).wait_send()

    if S > 1:

        @pl.when(s < S - 1)
        def _():
            for j in range(T):
                copy_a(j, i).start()

    @pl.when(s == S - 1)
    def _():
        for k in range(1, T):
            copy_d(k).start()
        total = part[rows_at(i)]
        for k in range(1, T):
            copy_d(k).wait_recv()
        for k in range(1, T):
            total = total + in_d[k - 1].astype(F32)
        tlast = total.astype(BF).astype(F32)
        gfull[rows_at(i)] = (curv[rows_at(i)].astype(F32) * tlast).astype(BF)
        for k in range(1, T):
            copy_s(k, i).start()
        for k in range(1, T):
            copy_s(k, peer(i, T - k, T)).wait_recv()
        for k in range(1, T):
            copy_s(k, i).wait_send()
            copy_d(k).wait_send()

    if S > 1:

        @pl.when(s < S - 1)
        def _():
            for j in range(T):
                copy_a(j, i).wait_send()

        def gather_rows():
            for j in range(T):
                remote(grow, gfull.at[rows_at(j)], h_send.at[0, j], h_recv.at[0, j], at(d, s, i)).wait_recv()

        if fused:
            if S > 2:

                @pl.when(jnp.logical_and(s > 0, s < S - 1))
                def _():
                    gather_rows()

            @pl.when(s == 0)
            def _():
                for k in range(N):
                    for j in range(T):
                        land_hd(k, j).wait_recv()
        else:

            @pl.when(s < S - 1)
            def _():
                gather_rows()

        @pl.when(s > 0)
        def _():
            gm = dot_nn(gfull[...], wo[...]).astype(BF)
            gv = jnp.concatenate(
                [dot_tn(probs_ref[h], gm[:, h * hd : (h + 1) * hd]) for h in range(heads)], axis=1
            ).astype(BF)
            for c in chunks:
                gc = dot_nn(gv, wv[:, c])
                part[:, c] = gc
                gpartb[:, c] = gc.astype(BF)
            for k in range(1, T):
                copy_f(k).start()
            total = part[rows_at(i)]
            for k in range(1, T):
                copy_f(k).wait_recv()
            for k in range(1, T):
                total = total + in_f[k - 1].astype(F32)
            scaled = gain * total
            gx = rrows * scaled - rrows**3 * xrows * jnp.mean(xrows * scaled, axis=-1, keepdims=True)
            grow[...] = (gfull[rows_at(i)].astype(F32) + gx).astype(BF)

            def plain():
                for j in range(T):
                    copy_h(j, i).start()
                for j in range(T):
                    copy_h(j, i).wait_send()

            if fused:

                @pl.when(s == 1)
                def _():
                    for k in range(N):
                        for j in range(T):
                            copy_hd(k, j, i).start()
                    for k in range(N):
                        for j in range(T):
                            copy_hd(k, j, i).wait_send()

                if S > 2:
                    pl.when(s > 1)(plain)
            else:
                plain()
            for k in range(1, T):
                copy_f(k).wait_send()

    if fused:

        def spread():
            for k in range(1, N):
                copy_x(k).start()
            gall[d] = gfull[:, feats_at(d)]
            for k in range(1, N):
                land_x(k).wait_recv()
            for k in range(1, N):
                copy_x(k).wait_send()

        if S > 1:
            pl.when(s > 0)(spread)
        else:
            spread()
        for k in range(1, N):
            copy_act(k, peer(d, N - k, N)).wait_recv()
        prod_ref[...] = dot_tn(
            gall[...].reshape(N * tok, feats), actall[...].reshape(N * tok, act.shape[1])
        )
        for k in range(1, N):
            copy_act(k, d).wait_send()
    else:
        gout_ref[...] = gfull[...]
        actout_ref[...] = act[...]


def home_share(feats, g, q):
    more = 1 if MORE[g] > 0 else -1
    return (feats // 256 + (more if q < abs(MORE[g]) else 0)) * 128


def kernel_pair(
    T, N,
    x_hbm, gain_hbm, probs_hbm, wv_hbm, wd_hbm, wo_hbm, curv_hbm,
    gall, actall,
    x_ref, gain_ref, probs_ref, wv, wd, wo, curv, act, vals, tvals, part, tbuf, gbuf, xrow, gain1,
    a_src, a_hop, a_land, d_src, d_hop, d_land, f_src, f_hop, f_land,
    grow,
    load_sem, lend_send, lend_recv, act_send, act_recv,
    hop_send, hop_recv, rs_send, rs_recv, ag_send, ag_recv, ag_pass, pass_send,
    h_send, h_self, h_recv, x_send, x_recv,
):
    d = lax.axis_index("dp")
    s = lax.axis_index("section")
    i = lax.axis_index("tensor")
    tok, width = x_hbm.shape
    K = TOKEN_CHUNKS
    Q = N
    ck = tok // K
    blk = ck // T
    feats = width // N
    heads = probs_ref.shape[0]
    hd = wv.shape[0] // heads
    end = jnp.logical_or(i == 0, i == T - 1)
    mid = jnp.logical_not(end)
    mate = jnp.bitwise_xor(i, 1)
    cross = jnp.where(end, T - 1 - mate, T - 1 - i)
    other = T - 1 - mate
    far = [k for k in range(2, T - 1)] + [k for k in range(1, T) if k in (1, T - 1)]
    subs = range(Q)

    def peer(me, k, n):
        return lax.rem(me + k, n)

    def at(dd, ss, jj):
        return {"dp": dd, "section": ss, "tensor": jj}

    def chunk(kk):
        return slice(kk * ck, (kk + 1) * ck)

    def rows(kk, j):
        return pl.ds(pl.multiple_of(kk * ck + j * blk, blk), blk)

    def share(g, y, q):
        return home_share(feats, g, q) if y == g else feats - home_share(feats, g, q)

    def part_of(g, y, q):
        lo = share(g, 0, q) if y == 1 else 0
        return slice(lo, lo + share(g, y, q))

    def col(g, y, q):
        c = part_of(g, y, q)
        return slice(q * feats + c.start, q * feats + c.stop)

    def block(b):
        return slice(b * feats, (b + 1) * feats)

    def feats_at(j):
        return pl.ds(pl.multiple_of(j * feats, 128), feats)

    def seq_rows(kk):
        return pl.ds(pl.multiple_of(d * tok + kk * ck, ck), ck)

    def own_rows(kk):
        return pl.ds(pl.multiple_of(d * tok + kk * ck + i * blk, blk), blk)

    def remote(src, dst, send, recv, dev):
        return pltpu.make_async_remote_copy(
            src_ref=src, dst_ref=dst, send_sem=send, recv_sem=recv,
            device_id=dev, device_id_type=MESH,
        )

    def landed(ref, sem):
        remote(ref, ref, sem, sem, at(d, s, i)).wait_recv()

    def sent(ref, sem):
        remote(ref, ref, sem, sem, at(d, s, i)).wait_send()

    loads = [
        pltpu.make_async_copy(src, dst, load_sem.at[k])
        for k, (src, dst) in enumerate(((wv_hbm, wv), (wd_hbm, wd), (wo_hbm, wo), (curv_hbm, curv)))
    ]
    first = [
        pltpu.make_async_copy(x_hbm.at[chunk(kk)], x_ref.at[chunk(kk)], load_sem.at[4 + kk]) for kk in range(K)
    ] + [
        pltpu.make_async_copy(gain_hbm, gain_ref, load_sem.at[4 + K]),
        pltpu.make_async_copy(probs_hbm, probs_ref, load_sem.at[5 + K]),
    ]
    first[K].start()
    first[0].start()
    loads[0].start()
    for copy in first[1:K] + first[K + 1 :]:
        copy.start()
    loads[1].start()

    barrier = pltpu.get_barrier_semaphore()
    for a in range(N):
        for b in range(2):
            for c in range(T):
                if (a == 0) != (b == 0 and c == 0):
                    pl.semaphore_signal(
                        barrier, inc=1, device_id=at(peer(d, a, N), peer(s, b, 2), peer(i, c, T)),
                        device_id_type=MESH,
                    )
    pl.when(s == 1)(loads[2].start)
    loads[3].start()

    def mix(kk, buf):
        r = chunk(kk)
        return jnp.concatenate(
            [dot_nn(probs_ref[h, r, :], buf[:, h * hd : (h + 1) * hd]) for h in range(heads)], axis=1
        ).astype(BF)

    def rnorm_of(xf):
        return lax.rsqrt(jnp.mean(xf * xf, axis=-1, keepdims=True) + 1e-06)

    def values_of(kk):
        first[kk].wait()
        r = chunk(kk)
        xf = x_ref[r, :].astype(F32)
        normed = (xf * rnorm_of(xf) * gain).astype(BF)
        vals[r, :] = dot_nt(normed, wv[...]).astype(BF)

    def acts_of(kk):
        act[chunk(kk), :] = mix(kk, vals)

    first[K].wait()
    gain = gain_ref[...]
    for kk in range(1, K):
        vals[chunk(kk), :] = jnp.zeros((ck, vals.shape[1]), BF)
        tvals[chunk(kk), :] = jnp.zeros((ck, vals.shape[1]), BF)

    def copy_act(k, owner):
        return remote(act, actall.at[owner], act_send.at[k], act_recv.at[k], at(peer(d, k, N), s, i))

    keep_act = pltpu.make_async_copy(act, actall.at[d], act_send.at[0])

    def keep_rows(kk):
        return pltpu.make_async_copy(gbuf.at[chunk(kk), feats_at(d)], gall.at[seq_rows(kk)], x_send.at[K + kk])

    lend = [
        remote(x_ref.at[rows(kk, i)], xrow.at[kk], lend_send.at[kk], lend_recv.at[kk], at(d, 0, i))
        for kk in range(K)
    ] + [remote(gain_ref, gain1, lend_send.at[K], lend_recv.at[K], at(d, 0, i))]

    A, D_, F_ = (0, a_src, a_hop, a_land, 0), (1, d_src, d_hop, d_land, 1), (2, f_src, f_hop, f_land, 1)

    def cw(p, y, q):
        return slice(0, share(p[4], y, q) + (128 if p[0] == 2 and q == 0 else 0))

    def hop(p, kk, q):
        y = 1 - p[4]
        c = cw(p, y, q)
        r = chunk(kk)
        remote(
            p[1].at[y, q, r, c], p[2].at[q, r, c], hop_send.at[p[0], kk, q], hop_recv.at[p[0], kk, q], at(d, y, i)
        ).start()

    def hop_done(p, kk, q):
        sent(p[1].at[1 - p[4], q, chunk(kk), cw(p, 1 - p[4], q)], hop_send.at[p[0], kk, q])

    def scatter(p, me, kk, q):
        c = cw(p, me, q)
        if me != p[4]:
            landed(p[2].at[q, chunk(kk), c], hop_recv.at[p[0], kk, q])
        buf = p[1].at[me, q] if me == p[4] else p[2].at[q]
        for k in far:
            j = peer(i, k, T)
            remote(
                buf.at[rows(kk, j), c], p[3].at[q, kk, k - 1, :, c], rs_send.at[p[0], kk, q],
                rs_recv.at[p[0], kk, q], at(d, me, j),
            ).start()

    def scatter_done(p, me, kk, q):
        sent(p[3].at[q, kk, :, :, cw(p, me, q)], rs_send.at[p[0], kk, q])

    def collect(p, me, kk, q, local):
        c = cw(p, me, q)
        total = p[2][q, rows(kk, i), c].astype(F32) if me != p[4] else local
        landed(p[3].at[q, kk, :, :, c], rs_recv.at[p[0], kk, q])
        for k in range(T - 1):
            total = total + p[3][q, kk, k, :, c].astype(F32)
        return total

    def spread_copies(n, buf, me, kk, q):
        src = buf.at[rows(kk, i), col(n, me, q)]
        if not RELAY[n]:
            return [
                remote(src, src, ag_send.at[n, kk, q, k], ag_recv.at[n, me, kk, q], at(d, 1, peer(i, k, T)))
                for k in far + ([0] if me == 0 else [])
            ]
        out = [
            remote(src, src, ag_send.at[n, kk, q, 1], ag_pass.at[n, me, kk, q], at(d, me, cross)),
            remote(src, src, ag_send.at[n, kk, q, 2], ag_recv.at[n, me, kk, q], at(d, 1, mate)),
        ]
        if me == 0:
            out.append(remote(src, src, ag_send.at[n, kk, q, 0], ag_recv.at[n, me, kk, q], at(d, 1, i)))
        return out

    def pass_copies(n, buf, me, kk, q):
        out = []
        for m, j in ((0, cross), (1, other)):
            src = buf.at[rows(kk, j), col(n, me, q)]
            land = ag_pass if me == 1 else ag_recv
            out.append(remote(src, src, pass_send.at[n, kk, q, m], land.at[n, me, kk, q], at(d, 1, mate)))
            if me == 0:
                out.append(remote(src, src, pass_send.at[n, kk, q, 2 + m], land.at[n, me, kk, q], at(d, 1, i)))
        return out

    def spread(n, buf, me, kk, q):
        for copy in spread_copies(n, buf, me, kk, q):
            copy.start()

    def pass_on(n, buf, me, kk, q):
        if not RELAY[n]:
            return
        pair = buf.at[kk * ck : kk * ck + 2 * blk, col(n, me, q)]
        if me == 1:
            landed(pair, ag_pass.at[n, me, kk, q])

        @pl.when(mid)
        def _():
            if me == 0:
                landed(pair, ag_pass.at[n, me, kk, q])
            for copy in pass_copies(n, buf, me, kk, q):
                copy.start()

    def spread_done(n, buf, me, kk, q):
        for copy in spread_copies(n, buf, me, kk, q):
            copy.wait_send()
        if RELAY[n]:

            @pl.when(mid)
            def _():
                for copy in pass_copies(n, buf, me, kk, q):
                    copy.wait_send()

    def gathered(n, buf, y, kk, q):
        count = T if y == 0 else T - 1
        if RELAY[n] and y == 1:
            count = 1
        landed(buf.at[kk * ck : kk * ck + count * blk, col(n, y, q)], ag_recv.at[n, y, kk, q])

    def ready(n, buf, kk, b):
        for y in (1, 0):
            gathered(n, buf, y, kk, b)

    def pack(p, buf, kk, b, sides=(0, 1)):
        home = p[4]
        for y in [1 - home] * (0 in sides) + [home] * (1 in sides):
            p[1][y, b, chunk(kk), 0 : share(home, y, b)] = buf[chunk(kk), col(home, y, b)].astype(BF)
            if y == home:
                scatter(p, home, kk, b)
            else:
                hop(p, kk, b)

    def done(me, sums, gathers):
        for kk in range(K):
            for q in subs:
                for p in sums:
                    if me == p[4]:
                        hop_done(p, kk, q)
                    scatter_done(p, me, kk, q)
                for n, buf in gathers:
                    spread_done(n, buf, me, kk, q)

    def tangent(me, kk, q):
        r = rows(kk, i)
        c = col(0, me, q)
        tbuf[r, c] = collect(A, me, kk, q, part[r, c]).astype(BF)
        spread(0, tbuf, me, kk, q)

    def seed(me, kk, q):
        r = rows(kk, i)
        c = col(1, me, q)
        total = collect(D_, me, kk, q, part[r, c])
        gbuf[r, c] = (curv[r, c].astype(F32) * total.astype(BF).astype(F32)).astype(BF)
        spread(1, gbuf, me, kk, q)

    def hand(me, kk, q, start):
        dd = q
        c = part_of(1, me, q)
        src = grow.at[kk, q, :, 0 : share(1, me, q)]
        dst = gall.at[own_rows(kk), c]

        if start:
            for k in far:
                remote(src, dst, h_send.at[kk, q], h_recv.at[kk, me], at(dd, 0, peer(i, k, T))).start()
        else:
            sent(gall.at[0 : (T - 1) * blk, c], h_send.at[kk, q])

        def direct():
            if start:
                remote(src, dst, h_self.at[kk, q], h_recv.at[kk, me], at(dd, 0, i)).start()
            else:
                sent(src, h_self.at[kk, q])

        if me == 1:
            direct()
        else:
            pl.when(d != dd)(direct)

            @pl.when(d == dd)
            def _():
                own = pltpu.make_async_copy(src, dst, h_self.at[kk, q])
                own.start() if start else own.wait()

    def adjoint(me, kk, xr, gn, rr):
        weight = None
        for q in subs:
            c = col(1, me, q)
            wide = share(1, me, q)
            local = f_src[1, q, rows(kk, i), cw(F_, 1, q)].astype(F32) if me == 1 else None
            total = collect(F_, me, kk, q, local)
            if q == 0:
                weight = jnp.sum(total[:, wide:], axis=-1, keepdims=True) * (rr * rr * (2.0 / 128 / width))
                total = total[:, :wide]
            g1 = gbuf[rows(kk, i), c].astype(F32) + (rr * gn[:, c]) * total - xr[:, c] * weight
            grow[kk, q, :, 0:wide] = g1.astype(BF)
            hand(me, kk, q, True)

    @pl.when(s == 0)
    def _():
        loads[0].wait()
        first[K + 1].wait()
        values_of(0)
        acts_of(0)
        pl.semaphore_wait(barrier, 2 * T + N - 2)
        loads[1].wait()
        for kk in range(K):
            if kk:
                values_of(kk)
                acts_of(kk)
            for b in range(N):
                part[chunk(kk), block(b)] = dot_nt(act[chunk(kk), :], wd[block(b), :])
                pack(A, part, kk, b)
        for k in range(1, N):
            copy_act(k, d).start()
        keep_act.start()
        for kk in range(K):
            for q in subs:
                tangent(0, kk, q)
        for kk in range(K):
            for q in subs:
                pass_on(0, tbuf, 0, kk, q)
        for copy in lend:
            copy.wait_recv()
        loads[3].wait()
        for kk in range(K):
            for q in subs:
                scatter(D_, 0, kk, q)
        done(0, (A,), ())
        for kk in range(K):
            for q in subs:
                seed(0, kk, q)
        for kk in range(K):
            for q in subs:
                pass_on(1, gbuf, 0, kk, q)
        done(0, (), ((0, tbuf),))
        for k in range(1, N):
            copy_act(k, d).wait_send()
        keep_act.wait()
        gn = gain1[...]
        for kk in reversed(range(K)):
            for q in subs:
                scatter(F_, 0, kk, q)
        done(0, (D_,), ((1, gbuf),))
        for kk in reversed(range(K)):
            xr = xrow[kk].astype(F32)
            rr = rnorm_of(xr)
            adjoint(0, kk, xr, gn, rr)
        for k in range(1, N):
            copy_act(k, peer(d, N - k, N)).wait_recv()
        done(0, (F_,), ())
        for kk in reversed(range(K)):
            for q in subs:
                hand(0, kk, q, False)
        for n, kk in enumerate(reversed(range(K))):

            for dd in range(N):

                @pl.when(d == dd)
                def _():
                    landed(gall.at[0 : N * ck - blk, part_of(1, 0, dd)], h_recv.at[kk, 0])
                    landed(gall.at[0 : N * ck, part_of(1, 1, dd)], h_recv.at[kk, 1])

    @pl.when(s == 1)
    def _():
        loads[0].wait()
        first[K + 1].wait()
        for kk in range(K):
            values_of(kk)
            acts_of(kk)
        pl.semaphore_wait(barrier, 2 * T + N - 2)
        for copy in lend:
            copy.start()
        for k in range(1, N):
            copy_act(k, d).start()
        keep_act.start()
        loads[1].wait()
        for b in range(N):
            part[:, block(b)] = dot_nt(act[...], wd[block(b), :])
        loads[2].wait()
        loads[3].wait()
        for q in subs:
            scatter(A, 1, 0, q)
        for kk in range(K):
            for q in subs:
                if kk + 1 < K:
                    scatter(A, 1, kk + 1, q)
                tangent(1, kk, q)
        for kk in range(K):
            r = chunk(kk)
            tv = None
            mean = None
            for b in range(N):
                pass_on(0, tbuf, 1, kk, b)
            for b in range(N):
                ready(0, tbuf, kk, b)
                c = block(b)
                tf = tbuf[r, c].astype(F32)
                dotted = jnp.sum(x_ref[r, c].astype(F32) * tf, axis=-1, keepdims=True)
                more = dot_nt((gain[:, c] * tf).astype(BF), wv[:, c])
                tv = more if tv is None else tv + more
                mean = dotted if mean is None else mean + dotted
            rr = rnorm_of(x_ref[r, :].astype(F32))
            tvals[r, :] = (rr * tv - (rr * rr * (1.0 / width) * mean) * vals[r, :].astype(F32)).astype(BF)
            tmix = mix(kk, tvals)
            for b in range(N):
                part[r, block(b)] = part[r, block(b)] + dot_nt(tmix, wo[block(b), :])
                mine = rows(kk, i)
                part[mine, block(b)] = part[mine, block(b)] + tbuf[mine, block(b)].astype(F32)
                pack(D_, part, kk, b)
        for copy in lend:
            copy.wait_send()
        done(1, (A,), ())
        for kk in range(K):
            for q in subs:
                seed(1, kk, q)
        done(1, (), ((0, tbuf),))
        for k in range(1, N):
            copy_act(k, d).wait_send()
        keep_act.wait()

        def copy_x(kk, k):
            dd = peer(d, k, N)
            return remote(
                gbuf.at[chunk(kk), feats_at(dd)], gall.at[seq_rows(kk)], x_send.at[kk], x_recv.at[kk], at(dd, s, i)
            )

        gms = []
        for kk in range(K):
            gm = None
            for b in range(N):
                pass_on(1, gbuf, 1, kk, b)
            for b in range(N):
                ready(1, gbuf, kk, b)
                more = dot_nn(gbuf[chunk(kk), block(b)], wo[block(b), :])
                gm = more if gm is None else gm + more
            gms.append(gm.astype(BF))
        pending = None
        for kk in reversed(range(K)):
            r = chunk(kk)
            more = jnp.concatenate(
                [dot_tn(probs_ref[h, r, :], gms[kk][:, h * hd : (h + 1) * hd]) for h in range(heads)], axis=1
            )
            pending = more if pending is None else pending + more
            gv = pending[r, :].astype(BF)
            weight = jnp.sum(gv.astype(F32) * vals[r, :].astype(F32), axis=-1, keepdims=True)
            high = weight.astype(BF).astype(F32)
            lane = lax.broadcasted_iota(jnp.int32, (ck, 128), 1)
            extra = jnp.where(lane < 64, high, weight - high).astype(BF)
            for y in (0, 1):
                f_src[y, 0, r, share(1, y, 0) : share(1, y, 0) + 128] = extra
            for b in range(N):
                part[r, block(b)] = dot_nn(gv, wv[:, block(b)])
                pack(F_, part, kk, b, (0,))
            for b in range(N):
                pack(F_, part, kk, b, (1,))
        for kk in range(K):
            for k in range(1, N):
                copy_x(kk, k).start()
            keep_rows(kk).start()
        done(1, (D_,), ((1, gbuf),))
        for k in range(1, N):
            copy_act(k, peer(d, N - k, N)).wait_recv()
        for kk in range(K):
            landed(gall.at[0 : (N - 1) * ck], x_recv.at[kk])
        for kk in reversed(range(K)):
            xr = x_ref[rows(kk, i), :].astype(F32)
            adjoint(1, kk, xr, gain, rnorm_of(xr))
        done(1, (F_,), ())
        for kk in range(K):
            sent(gall.at[0 : (N - 1) * ck], x_send.at[kk])
            keep_rows(kk).wait()
            for q in subs:
                hand(1, kk, q, False)


def call_pair(T, N, x, norm_gain, probs, w_val, w_dir, w_out, curvature):
    tok, width = x.shape
    hf = w_val.shape[0]
    K = TOKEN_CHUNKS
    Q = N
    ck = tok // K
    blk = ck // T
    feats = width // N
    wide = max(max(home_share(feats, g, q), feats - home_share(feats, g, q)) for g in (0, 1) for q in range(N))
    hbm = functools.partial(pl.BlockSpec, memory_space=pl.ANY)
    sem = pltpu.SemaphoreType.DMA

    def sums(cols):
        return [
            pltpu.VMEM((2, Q, tok, cols), BF),
            pltpu.VMEM((Q, tok, cols), BF),
            pltpu.VMEM((Q, K, T - 1, blk, cols), BF),
        ]

    scratch = [
        pltpu.VMEM((tok, width), BF),
        pltpu.VMEM((1, width), F32),
        pltpu.VMEM(probs.shape, BF),
        pltpu.VMEM((hf, width), BF),
        pltpu.VMEM((width, hf), BF),
        pltpu.VMEM((width, hf), BF),
        pltpu.VMEM((tok, width), BF),
        pltpu.VMEM((tok, hf), BF),
        pltpu.VMEM((tok, hf), BF),
        pltpu.VMEM((tok, hf), BF),
        pltpu.VMEM((tok, width), F32),
        pltpu.VMEM((tok, width), BF),
        pltpu.VMEM((tok, width), BF),
        pltpu.VMEM((K, blk, width), BF),
        pltpu.VMEM((1, width), F32),
        *sums(wide), *sums(wide), *sums(wide + 128),
        pltpu.VMEM((K, Q, blk, wide), BF),
        sem((6 + K,)),
        sem((K + 1,)), sem((K + 1,)),
        sem((N,)), sem((N,)),
        sem((3, K, Q)), sem((3, K, Q)),
        sem((3, K, Q)), sem((3, K, Q)),
        sem((2, K, Q, T)), sem((2, 2, K, Q)), sem((2, 2, K, Q)), sem((2, K, Q, T)),
        sem((K, Q)), sem((K, Q)), sem((K, 2)),
        sem((2 * K,)), sem((K,)),
    ]
    adjoints, acts = pl.pallas_call(
        functools.partial(kernel_pair, T, N),
        out_shape=(
            jax.ShapeDtypeStruct((N * tok, feats), BF), jax.ShapeDtypeStruct((N, tok, hf), BF),
        ),
        in_specs=[hbm()] * 7,
        out_specs=(hbm(), hbm()),
        scratch_shapes=scratch,
        compiler_params=pltpu.CompilerParams(
            collective_id=0, has_side_effects=True, vmem_limit_bytes=56 * 1024 * 1024
        ),
    )(x, norm_gain, probs, w_val, w_dir, w_out, curvature)
    return dot_tn(adjoints, acts.reshape(N * tok, hf))


def per_device(section_input, norm_gain, value_weight, attn_probs, out_weight, direction, curvature):
    x = section_input[0]
    w_val = value_weight[0]
    w_out = out_weight[0]
    w_dir = direction[0]
    probs = attn_probs[0]
    S = lax.axis_size("section")
    T = lax.axis_size("tensor")
    N = lax.axis_size("dp")
    tok, width = x.shape
    hf = w_val.shape[0]
    rows = tok // T
    feats = width // N
    fused = feats % 128 == 0 and feats * N == width
    blocks = tok % (16 * T * TOKEN_CHUNKS) == 0
    if fused and S == 2 and T == 4 and feats % 256 == 0 and blocks:
        return call_pair(T, N, x, norm_gain, probs, w_val, w_dir, w_out, curvature)[None]
    vm = functools.partial(pl.BlockSpec, memory_space=pltpu.VMEM)
    hbm = functools.partial(pl.BlockSpec, memory_space=pl.ANY)
    if fused:
        outs = jax.ShapeDtypeStruct((feats, hf), F32)
        out_specs = vm()
    else:
        outs = (jax.ShapeDtypeStruct((tok, width), BF), jax.ShapeDtypeStruct((tok, hf), BF))
        out_specs = (vm(), vm())
    sem = pltpu.SemaphoreType.DMA
    wide = N if fused else 1
    scratch = [
        pltpu.VMEM((hf, width), BF),
        pltpu.VMEM((width, hf), BF),
        pltpu.VMEM((width, hf), BF),
        pltpu.VMEM((tok, width), BF),
        pltpu.VMEM((tok, hf), BF),
        pltpu.VMEM((tok, width), F32),
        pltpu.VMEM((tok, width), BF),
        pltpu.VMEM((T, rows, width), BF),
        pltpu.VMEM((T, rows, width), BF),
        pltpu.VMEM((T, rows, width), BF),
        pltpu.VMEM((tok, width), BF),
        pltpu.VMEM((tok, width), BF),
        pltpu.VMEM((tok, width), BF),
        pltpu.VMEM((tok, width), BF),
        pltpu.VMEM((rows, width), F32),
        pltpu.VMEM((rows, width), BF),
        pltpu.VMEM((wide, tok, hf), BF),
        pltpu.VMEM((wide, tok, feats if fused else 128), BF),
        sem((4,)),
        sem((N,)), sem((N,)),
        sem((T,)), sem((T,)),
        sem((T,)), sem((T,)),
        sem((T,)), sem((T,)),
        sem((T,)), sem((T,)),
        sem((T,)), sem((T,)),
        sem((wide, T)), sem((wide, T)),
        sem((N,)), sem((N,)),
    ]
    result = pl.pallas_call(
        functools.partial(kernel, fused, S, T, N),
        out_shape=outs,
        in_specs=[vm(), vm(), vm(), hbm(), hbm(), hbm(), hbm()],
        out_specs=out_specs,
        scratch_shapes=scratch,
        compiler_params=pltpu.CompilerParams(
            collective_id=0, has_side_effects=True, vmem_limit_bytes=56 * 1024 * 1024
        ),
    )(x, norm_gain, probs, w_val, w_dir, w_out, curvature)
    if fused:
        return result[None]
    adjoint, act = result
    product = lax.psum_scatter(
        dot_tn(adjoint, act).astype(BF), "dp", scatter_dimension=0, tiled=True
    ).astype(F32)
    return product[None]


def solution(mesh):
    in_specs = (
        P("section", "dp", None),
        P("section", None),
        P("section", "tensor", None),
        P("section", "tensor", "dp", None),
        P("section", None, "tensor"),
        P("section", None, "tensor"),
        P("dp", None),
    )
    out_specs = P("section", "dp", "tensor")
    return jax.shard_map(
        per_device, mesh=mesh, in_specs=in_specs, out_specs=out_specs, check_vma=False
    )
```

```python
import functools

import jax
import jax.numpy as jnp
from jax import lax
from jax.experimental import pallas as pl
from jax.experimental.pallas import tpu as pltpu
from jax.sharding import PartitionSpec as P

MESH = pl.DeviceIdType.MESH
BF = jnp.bfloat16
F32 = jnp.float32
TOKEN_CHUNKS = 2
MORE = (1, 0)
RELAY = (True, False)


def dot_nt(a, b):
    return lax.dot_general(a, b, (((1,), (1,)), ((), ())), preferred_element_type=F32)


def dot_tn(a, b):
    return lax.dot_general(a, b, (((0,), (0,)), ((), ())), preferred_element_type=F32)


def dot_nn(a, b):
    return lax.dot_general(a, b, (((1,), (0,)), ((), ())), preferred_element_type=F32)


def kernel(
    fused, S, T, N,
    x_ref, gain_ref, probs_ref, wv_hbm, wd_hbm, wo_hbm, curv_hbm,
    *rest,
):
    if fused:
        prod_ref, rest = rest[0], rest[1:]
    else:
        gout_ref, actout_ref, rest = rest[0], rest[1], rest[2:]
    (
        wv, wd, wo, curv, act, part, partb, in_a, in_d, in_f, gpartb, normed, tn, gfull, trow, grow,
        actall, gall,
        load_sem, act_send, act_recv, a_send, a_recv, tn_send, tn_recv, d_send, d_recv,
        s_send, s_recv, f_send, f_recv, h_send, h_recv, x_send, x_recv,
    ) = rest
    d = lax.axis_index("dp")
    s = lax.axis_index("section")
    i = lax.axis_index("tensor")
    tok, width = x_ref.shape
    rows = tok // T
    heads = probs_ref.shape[0]
    hd = wv.shape[0] // heads
    feats = width // N
    CH = 512 if width % 512 == 0 else width
    chunks = [slice(c, c + CH) for c in range(0, width, CH)]

    def rows_at(j):
        return pl.ds(pl.multiple_of(j * rows, rows), rows)

    def feats_at(j):
        return pl.ds(pl.multiple_of(j * feats, 128), feats)

    def peer(me, k, n):
        return lax.rem(me + k, n)

    loads = [
        pltpu.make_async_copy(src, dst, load_sem.at[k])
        for k, (src, dst) in enumerate(((wv_hbm, wv), (wd_hbm, wd), (wo_hbm, wo), (curv_hbm, curv)))
    ]
    for copy in loads:
        copy.start()

    barrier = pltpu.get_barrier_semaphore()

    def greet(dev):
        pl.semaphore_signal(barrier, inc=1, device_id=dev, device_id_type=MESH)

    for k in range(1, T):
        greet({"dp": d, "section": s, "tensor": peer(i, k, T)})
    for k in range(1, N):
        greet({"dp": peer(d, k, N), "section": s, "tensor": i})
    for low in range(S - 1):
        wide = N if (fused and low == 0) else 1

        @pl.when(s == low)
        def _():
            for k in range(wide):
                for j in range(T):
                    greet({"dp": peer(d, k, N), "section": s + 1, "tensor": j})

        @pl.when(s == low + 1)
        def _():
            for k in range(wide):
                for j in range(T):
                    greet({"dp": peer(d, k, N), "section": s - 1, "tensor": j})

    gain = gain_ref[...]
    xf = x_ref[...].astype(F32)
    rnorm = lax.rsqrt(jnp.mean(xf * xf, axis=-1, keepdims=True) + 1e-06)
    normed[...] = (xf * rnorm * gain).astype(BF)

    def mix(vals):
        return jnp.concatenate(
            [dot_nn(probs_ref[h], vals[:, h * hd : (h + 1) * hd]) for h in range(heads)], axis=1
        )

    loads[0].wait()
    act[...] = mix(dot_nt(normed[...], wv[...]).astype(BF)).astype(BF)

    for here in range(S):
        count = T - 1 + N - 1
        for low in (here - 1, here):
            if 0 <= low < S - 1:
                count += T * (N if (fused and low == 0) else 1)

        @pl.when(s == here)
        def _():
            pl.semaphore_wait(barrier, count)

    def remote(src, dst, send, recv, dev):
        return pltpu.make_async_remote_copy(
            src_ref=src, dst_ref=dst, send_sem=send, recv_sem=recv,
            device_id=dev, device_id_type=MESH,
        )

    def at(dd, ss, jj):
        return {"dp": dd, "section": ss, "tensor": jj}

    def copy_act(k, owner):
        return remote(act, actall.at[owner], act_send.at[k], act_recv.at[k], at(peer(d, k, N), s, i))

    def copy_a(j, owner):
        return remote(partb.at[rows_at(j)], in_a.at[owner], a_send.at[j], a_recv.at[owner], at(d, s + 1, j))

    def copy_tn(k, owner):
        return remote(
            tn.at[rows_at(owner)], tn.at[rows_at(owner)], tn_send.at[k], tn_recv.at[k], at(d, s, peer(i, k, T))
        )

    def copy_d(k):
        j = peer(i, k, T)
        return remote(partb.at[rows_at(j)], in_d.at[k - 1], d_send.at[k], d_recv.at[k], at(d, s, j))

    def copy_s(k, owner):
        return remote(
            gfull.at[rows_at(owner)], gfull.at[rows_at(owner)], s_send.at[k], s_recv.at[k],
            at(d, s, peer(i, k, T)),
        )

    def copy_f(k):
        j = peer(i, k, T)
        return remote(gpartb.at[rows_at(j)], in_f.at[k - 1], f_send.at[k], f_recv.at[k], at(d, s, j))

    def copy_h(j, owner):
        return remote(grow, gfull.at[rows_at(owner)], h_send.at[0, j], h_recv.at[0, owner], at(d, s - 1, j))

    def copy_hd(k, j, owner):
        dd = peer(d, k, N)
        return remote(
            grow.at[:, feats_at(dd)], gall.at[lax.rem(d, N), rows_at(owner)],
            h_send.at[k, j], h_recv.at[k, owner], at(dd, s - 1, j),
        )

    def land_hd(k, owner):
        src = peer(d, N - k, N)
        return remote(
            grow.at[:, feats_at(d)], gall.at[src, rows_at(owner)],
            h_send.at[k, owner], h_recv.at[k, owner], at(d, s, i),
        )

    def copy_x(k):
        dd = peer(d, k, N)
        return remote(gfull.at[:, feats_at(dd)], gall.at[d], x_send.at[k], x_recv.at[k], at(dd, s, i))

    def land_x(k):
        src = peer(d, N - k, N)
        return remote(gfull.at[:, feats_at(d)], gall.at[src], x_send.at[k], x_recv.at[k], at(d, s, i))

    if fused:
        for k in range(1, N):
            copy_act(k, d).start()
        actall[d] = act[...]

    xrows = x_ref[rows_at(i)].astype(F32)
    rrows = lax.rsqrt(jnp.mean(xrows * xrows, axis=-1, keepdims=True) + 1e-06)

    loads[1].wait()
    for c in chunks:
        base = dot_nt(act[...], wd[c, :])
        part[:, c] = base

    loads[2].wait()
    loads[3].wait()

    @pl.when(s == 0)
    def _():
        partb[...] = part[...].astype(BF)

    @pl.when(s > 0)
    def _():
        total = None
        for j in range(T):
            remote(partb.at[rows_at(j)], in_a.at[j], a_send.at[j], a_recv.at[j], at(d, s, i)).wait_recv()
        for j in range(T):
            piece = in_a[j].astype(F32)
            total = piece if total is None else total + piece
        tfloat = total.astype(BF).astype(F32)
        trow[...] = tfloat
        tn[rows_at(i)] = (
            gain * (rrows * tfloat - rrows**3 * xrows * jnp.mean(xrows * tfloat, axis=-1, keepdims=True))
        ).astype(BF)
        for k in range(1, T):
            copy_tn(k, i).start()
        for k in range(1, T):
            copy_tn(k, peer(i, T - k, T)).wait_recv()
        tmix = mix(dot_nt(tn[...], wv[...]).astype(BF)).astype(BF)
        for c in chunks:
            part[:, c] = part[:, c] + dot_nt(tmix, wo[c, :])
        part[rows_at(i)] = part[rows_at(i)] + trow[...]
        partb[...] = part[...].astype(BF)
        for k in range(1, T):
            copy_tn(k, i).wait_send()

    if S > 1:

        @pl.when(s < S - 1)
        def _():
            for j in range(T):
                copy_a(j, i).start()

    @pl.when(s == S - 1)
    def _():
        for k in range(1, T):
            copy_d(k).start()
        total = part[rows_at(i)]
        for k in range(1, T):
            copy_d(k).wait_recv()
        for k in range(1, T):
            total = total + in_d[k - 1].astype(F32)
        tlast = total.astype(BF).astype(F32)
        gfull[rows_at(i)] = (curv[rows_at(i)].astype(F32) * tlast).astype(BF)
        for k in range(1, T):
            copy_s(k, i).start()
        for k in range(1, T):
            copy_s(k, peer(i, T - k, T)).wait_recv()
        for k in range(1, T):
            copy_s(k, i).wait_send()
            copy_d(k).wait_send()

    if S > 1:

        @pl.when(s < S - 1)
        def _():
            for j in range(T):
                copy_a(j, i).wait_send()

        def gather_rows():
            for j in range(T):
                remote(grow, gfull.at[rows_at(j)], h_send.at[0, j], h_recv.at[0, j], at(d, s, i)).wait_recv()

        if fused:
            if S > 2:

                @pl.when(jnp.logical_and(s > 0, s < S - 1))
                def _():
                    gather_rows()

            @pl.when(s == 0)
            def _():
                for k in range(N):
                    for j in range(T):
                        land_hd(k, j).wait_recv()
        else:

            @pl.when(s < S - 1)
            def _():
                gather_rows()

        @pl.when(s > 0)
        def _():
            gm = dot_nn(gfull[...], wo[...]).astype(BF)
            gv = jnp.concatenate(
                [dot_tn(probs_ref[h], gm[:, h * hd : (h + 1) * hd]) for h in range(heads)], axis=1
            ).astype(BF)
            for c in chunks:
                gc = dot_nn(gv, wv[:, c])
                part[:, c] = gc
                gpartb[:, c] = gc.astype(BF)
            for k in range(1, T):
                copy_f(k).start()
            total = part[rows_at(i)]
            for k in range(1, T):
                copy_f(k).wait_recv()
            for k in range(1, T):
                total = total + in_f[k - 1].astype(F32)
            scaled = gain * total
            gx = rrows * scaled - rrows**3 * xrows * jnp.mean(xrows * scaled, axis=-1, keepdims=True)
            grow[...] = (gfull[rows_at(i)].astype(F32) + gx).astype(BF)

            def plain():
                for j in range(T):
                    copy_h(j, i).start()
                for j in range(T):
                    copy_h(j, i).wait_send()

            if fused:

                @pl.when(s == 1)
                def _():
                    for k in range(N):
                        for j in range(T):
                            copy_hd(k, j, i).start()
                    for k in range(N):
                        for j in range(T):
                            copy_hd(k, j, i).wait_send()

                if S > 2:
                    pl.when(s > 1)(plain)
            else:
                plain()
            for k in range(1, T):
                copy_f(k).wait_send()

    if fused:

        def spread():
            for k in range(1, N):
                copy_x(k).start()
            gall[d] = gfull[:, feats_at(d)]
            for k in range(1, N):
                land_x(k).wait_recv()
            for k in range(1, N):
                copy_x(k).wait_send()

        if S > 1:
            pl.when(s > 0)(spread)
        else:
            spread()
        for k in range(1, N):
            copy_act(k, peer(d, N - k, N)).wait_recv()
        prod_ref[...] = dot_tn(
            gall[...].reshape(N * tok, feats), actall[...].reshape(N * tok, act.shape[1])
        )
        for k in range(1, N):
            copy_act(k, d).wait_send()
    else:
        gout_ref[...] = gfull[...]
        actout_ref[...] = act[...]


def home_share(feats, g, q):
    more = 1 if MORE[g] > 0 else -1
    return (feats // 256 + (more if q < abs(MORE[g]) else 0)) * 128


def kernel_pair(
    T, N,
    x_hbm, gain_hbm, probs_hbm, wv_hbm, wd_hbm, wo_hbm, curv_hbm,
    gall, actall,
    x_ref, gain_ref, probs_ref, wv, wd, wo, curv, act, vals, tvals, part, tbuf, gbuf, xrow, gain1,
    a_src, a_hop, a_land, d_src, d_hop, d_land, f_src, f_hop, f_land,
    grow,
    load_sem, lend_send, lend_recv, act_send, act_recv,
    hop_send, hop_recv, rs_send, rs_recv, ag_send, ag_recv, ag_pass, pass_send,
    h_send, h_self, h_recv, x_send, x_recv,
):
    d = lax.axis_index("dp")
    s = lax.axis_index("section")
    i = lax.axis_index("tensor")
    tok, width = x_hbm.shape
    K = TOKEN_CHUNKS
    Q = N
    ck = tok // K
    blk = ck // T
    feats = width // N
    heads = probs_ref.shape[0]
    hd = wv.shape[0] // heads
    end = jnp.logical_or(i == 0, i == T - 1)
    mid = jnp.logical_not(end)
    mate = jnp.bitwise_xor(i, 1)
    cross = jnp.where(end, T - 1 - mate, T - 1 - i)
    other = T - 1 - mate
    far = [k for k in range(2, T - 1)] + [k for k in range(1, T) if k in (1, T - 1)]
    subs = range(Q)

    def peer(me, k, n):
        return lax.rem(me + k, n)

    def at(dd, ss, jj):
        return {"dp": dd, "section": ss, "tensor": jj}

    def chunk(kk):
        return slice(kk * ck, (kk + 1) * ck)

    def rows(kk, j):
        return pl.ds(pl.multiple_of(kk * ck + j * blk, blk), blk)

    def share(g, y, q):
        return home_share(feats, g, q) if y == g else feats - home_share(feats, g, q)

    def part_of(g, y, q):
        lo = share(g, 0, q) if y == 1 else 0
        return slice(lo, lo + share(g, y, q))

    def col(g, y, q):
        c = part_of(g, y, q)
        return slice(q * feats + c.start, q * feats + c.stop)

    def block(b):
        return slice(b * feats, (b + 1) * feats)

    def feats_at(j):
        return pl.ds(pl.multiple_of(j * feats, 128), feats)

    def seq_rows(kk):
        return pl.ds(pl.multiple_of(d * tok + kk * ck, ck), ck)

    def own_rows(kk):
        return pl.ds(pl.multiple_of(d * tok + kk * ck + i * blk, blk), blk)

    def remote(src, dst, send, recv, dev):
        return pltpu.make_async_remote_copy(
            src_ref=src, dst_ref=dst, send_sem=send, recv_sem=recv,
            device_id=dev, device_id_type=MESH,
        )

    def landed(ref, sem):
        remote(ref, ref, sem, sem, at(d, s, i)).wait_recv()

    def sent(ref, sem):
        remote(ref, ref, sem, sem, at(d, s, i)).wait_send()

    loads = [
        pltpu.make_async_copy(src, dst, load_sem.at[k])
        for k, (src, dst) in enumerate(((wv_hbm, wv), (wd_hbm, wd), (wo_hbm, wo), (curv_hbm, curv)))
    ]
    first = [
        pltpu.make_async_copy(x_hbm.at[chunk(kk)], x_ref.at[chunk(kk)], load_sem.at[4 + kk]) for kk in range(K)
    ] + [
        pltpu.make_async_copy(gain_hbm, gain_ref, load_sem.at[4 + K]),
        pltpu.make_async_copy(probs_hbm, probs_ref, load_sem.at[5 + K]),
    ]
    first[K].start()
    first[0].start()
    loads[0].start()
    for copy in first[1:K] + first[K + 1 :]:
        copy.start()
    loads[1].start()

    barrier = pltpu.get_barrier_semaphore()
    for a in range(N):
        for b in range(2):
            for c in range(T):
                if (a == 0) != (b == 0 and c == 0):
                    pl.semaphore_signal(
                        barrier, inc=1, device_id=at(peer(d, a, N), peer(s, b, 2), peer(i, c, T)),
                        device_id_type=MESH,
                    )
    pl.when(s == 1)(loads[2].start)
    loads[3].start()

    def mix(kk, buf):
        r = chunk(kk)
        return jnp.concatenate(
            [dot_nn(probs_ref[h, r, :], buf[:, h * hd : (h + 1) * hd]) for h in range(heads)], axis=1
        ).astype(BF)

    def rnorm_of(xf):
        return lax.rsqrt(jnp.mean(xf * xf, axis=-1, keepdims=True) + 1e-06)

    def values_of(kk):
        first[kk].wait()
        r = chunk(kk)
        xf = x_ref[r, :].astype(F32)
        normed = (xf * rnorm_of(xf) * gain).astype(BF)
        vals[r, :] = dot_nt(normed, wv[...]).astype(BF)

    def acts_of(kk):
        act[chunk(kk), :] = mix(kk, vals)

    first[K].wait()
    gain = gain_ref[...]
    for kk in range(1, K):
        vals[chunk(kk), :] = jnp.zeros((ck, vals.shape[1]), BF)
        tvals[chunk(kk), :] = jnp.zeros((ck, vals.shape[1]), BF)

    def copy_act(k, owner):
        return remote(act, actall.at[owner], act_send.at[k], act_recv.at[k], at(peer(d, k, N), s, i))

    keep_act = pltpu.make_async_copy(act, actall.at[d], act_send.at[0])

    def keep_rows(kk):
        return pltpu.make_async_copy(gbuf.at[chunk(kk), feats_at(d)], gall.at[seq_rows(kk)], x_send.at[K + kk])

    lend = [
        remote(x_ref.at[rows(kk, i)], xrow.at[kk], lend_send.at[kk], lend_recv.at[kk], at(d, 0, i))
        for kk in range(K)
    ] + [remote(gain_ref, gain1, lend_send.at[K], lend_recv.at[K], at(d, 0, i))]

    A, D_, F_ = (0, a_src, a_hop, a_land, 0), (1, d_src, d_hop, d_land, 1), (2, f_src, f_hop, f_land, 1)

    def cw(p, y, q):
        return slice(0, share(p[4], y, q) + (128 if p[0] == 2 and q == 0 else 0))

    def hop(p, kk, q):
        y = 1 - p[4]
        c = cw(p, y, q)
        r = chunk(kk)
        remote(
            p[1].at[y, q, r, c], p[2].at[q, r, c], hop_send.at[p[0], kk, q], hop_recv.at[p[0], kk, q], at(d, y, i)
        ).start()

    def hop_done(p, kk, q):
        sent(p[1].at[1 - p[4], q, chunk(kk), cw(p, 1 - p[4], q)], hop_send.at[p[0], kk, q])

    def scatter(p, me, kk, q):
        c = cw(p, me, q)
        if me != p[4]:
            landed(p[2].at[q, chunk(kk), c], hop_recv.at[p[0], kk, q])
        buf = p[1].at[me, q] if me == p[4] else p[2].at[q]
        for k in far:
            j = peer(i, k, T)
            remote(
                buf.at[rows(kk, j), c], p[3].at[q, kk, k - 1, :, c], rs_send.at[p[0], kk, q],
                rs_recv.at[p[0], kk, q], at(d, me, j),
            ).start()

    def scatter_done(p, me, kk, q):
        sent(p[3].at[q, kk, :, :, cw(p, me, q)], rs_send.at[p[0], kk, q])

    def collect(p, me, kk, q, local):
        c = cw(p, me, q)
        total = p[2][q, rows(kk, i), c].astype(F32) if me != p[4] else local
        landed(p[3].at[q, kk, :, :, c], rs_recv.at[p[0], kk, q])
        for k in range(T - 1):
            total = total + p[3][q, kk, k, :, c].astype(F32)
        return total

    def spread_copies(n, buf, me, kk, q):
        src = buf.at[rows(kk, i), col(n, me, q)]
        if not RELAY[n]:
            return [
                remote(src, src, ag_send.at[n, kk, q, k], ag_recv.at[n, me, kk, q], at(d, 1, peer(i, k, T)))
                for k in far + ([0] if me == 0 else [])
            ]
        out = [
            remote(src, src, ag_send.at[n, kk, q, 1], ag_pass.at[n, me, kk, q], at(d, me, cross)),
            remote(src, src, ag_send.at[n, kk, q, 2], ag_recv.at[n, me, kk, q], at(d, 1, mate)),
        ]
        if me == 0:
            out.append(remote(src, src, ag_send.at[n, kk, q, 0], ag_recv.at[n, me, kk, q], at(d, 1, i)))
        return out

    def pass_copies(n, buf, me, kk, q):
        out = []
        for m, j in ((0, cross), (1, other)):
            src = buf.at[rows(kk, j), col(n, me, q)]
            land = ag_pass if me == 1 else ag_recv
            out.append(remote(src, src, pass_send.at[n, kk, q, m], land.at[n, me, kk, q], at(d, 1, mate)))
            if me == 0:
                out.append(remote(src, src, pass_send.at[n, kk, q, 2 + m], land.at[n, me, kk, q], at(d, 1, i)))
        return out

    def spread(n, buf, me, kk, q):
        for copy in spread_copies(n, buf, me, kk, q):
            copy.start()

    def pass_on(n, buf, me, kk, q):
        if not RELAY[n]:
            return
        pair = buf.at[kk * ck : kk * ck + 2 * blk, col(n, me, q)]
        if me == 1:
            landed(pair, ag_pass.at[n, me, kk, q])

        @pl.when(mid)
        def _():
            if me == 0:
                landed(pair, ag_pass.at[n, me, kk, q])
            for copy in pass_copies(n, buf, me, kk, q):
                copy.start()

    def spread_done(n, buf, me, kk, q):
        for copy in spread_copies(n, buf, me, kk, q):
            copy.wait_send()
        if RELAY[n]:

            @pl.when(mid)
            def _():
                for copy in pass_copies(n, buf, me, kk, q):
                    copy.wait_send()

    def gathered(n, buf, y, kk, q):
        count = T if y == 0 else T - 1
        if RELAY[n] and y == 1:
            count = 1
        landed(buf.at[kk * ck : kk * ck + count * blk, col(n, y, q)], ag_recv.at[n, y, kk, q])

    def ready(n, buf, kk, b):
        for y in (1, 0):
            gathered(n, buf, y, kk, b)

    def pack(p, buf, kk, b, sides=(0, 1)):
        home = p[4]
        for y in [1 - home] * (0 in sides) + [home] * (1 in sides):
            p[1][y, b, chunk(kk), 0 : share(home, y, b)] = buf[chunk(kk), col(home, y, b)].astype(BF)
            if y == home:
                scatter(p, home, kk, b)
            else:
                hop(p, kk, b)

    def done(me, sums, gathers):
        for kk in range(K):
            for q in subs:
                for p in sums:
                    if me == p[4]:
                        hop_done(p, kk, q)
                    scatter_done(p, me, kk, q)
                for n, buf in gathers:
                    spread_done(n, buf, me, kk, q)

    def tangent(me, kk, q):
        r = rows(kk, i)
        c = col(0, me, q)
        tbuf[r, c] = collect(A, me, kk, q, part[r, c]).astype(BF)
        spread(0, tbuf, me, kk, q)

    def seed(me, kk, q):
        r = rows(kk, i)
        c = col(1, me, q)
        total = collect(D_, me, kk, q, part[r, c])
        gbuf[r, c] = (curv[r, c].astype(F32) * total.astype(BF).astype(F32)).astype(BF)
        spread(1, gbuf, me, kk, q)

    def hand(me, kk, q, start):
        dd = q
        c = part_of(1, me, q)
        src = grow.at[kk, q, :, 0 : share(1, me, q)]
        dst = gall.at[own_rows(kk), c]

        if start:
            for k in far:
                remote(src, dst, h_send.at[kk, q], h_recv.at[kk, me], at(dd, 0, peer(i, k, T))).start()
        else:
            sent(gall.at[0 : (T - 1) * blk, c], h_send.at[kk, q])

        def direct():
            if start:
                remote(src, dst, h_self.at[kk, q], h_recv.at[kk, me], at(dd, 0, i)).start()
            else:
                sent(src, h_self.at[kk, q])

        if me == 1:
            direct()
        else:
            pl.when(d != dd)(direct)

            @pl.when(d == dd)
            def _():
                own = pltpu.make_async_copy(src, dst, h_self.at[kk, q])
                own.start() if start else own.wait()

    def adjoint(me, kk, xr, gn, rr):
        weight = None
        for q in subs:
            c = col(1, me, q)
            wide = share(1, me, q)
            local = f_src[1, q, rows(kk, i), cw(F_, 1, q)].astype(F32) if me == 1 else None
            total = collect(F_, me, kk, q, local)
            if q == 0:
                weight = jnp.sum(total[:, wide:], axis=-1, keepdims=True) * (rr * rr * (2.0 / 128 / width))
                total = total[:, :wide]
            g1 = gbuf[rows(kk, i), c].astype(F32) + (rr * gn[:, c]) * total - xr[:, c] * weight
            grow[kk, q, :, 0:wide] = g1.astype(BF)
            hand(me, kk, q, True)

    @pl.when(s == 0)
    def _():
        loads[0].wait()
        first[K + 1].wait()
        values_of(0)
        acts_of(0)
        pl.semaphore_wait(barrier, 2 * T + N - 2)
        loads[1].wait()
        for kk in range(K):
            if kk:
                values_of(kk)
                acts_of(kk)
            for b in range(N):
                part[chunk(kk), block(b)] = dot_nt(act[chunk(kk), :], wd[block(b), :])
                pack(A, part, kk, b)
        for k in range(1, N):
            copy_act(k, d).start()
        keep_act.start()
        for kk in range(K):
            for q in subs:
                tangent(0, kk, q)
        for kk in range(K):
            for q in subs:
                pass_on(0, tbuf, 0, kk, q)
        for copy in lend:
            copy.wait_recv()
        loads[3].wait()
        for kk in range(K):
            for q in subs:
                scatter(D_, 0, kk, q)
        done(0, (A,), ())
        for kk in range(K):
            for q in subs:
                seed(0, kk, q)
        for kk in range(K):
            for q in subs:
                pass_on(1, gbuf, 0, kk, q)
        done(0, (), ((0, tbuf),))
        for k in range(1, N):
            copy_act(k, d).wait_send()
        keep_act.wait()
        gn = gain1[...]
        for kk in reversed(range(K)):
            for q in subs:
                scatter(F_, 0, kk, q)
        done(0, (D_,), ((1, gbuf),))
        for kk in reversed(range(K)):
            xr = xrow[kk].astype(F32)
            rr = rnorm_of(xr)
            adjoint(0, kk, xr, gn, rr)
        for k in range(1, N):
            copy_act(k, peer(d, N - k, N)).wait_recv()
        done(0, (F_,), ())
        for kk in reversed(range(K)):
            for q in subs:
                hand(0, kk, q, False)
        for n, kk in enumerate(reversed(range(K))):

            for dd in range(N):

                @pl.when(d == dd)
                def _():
                    landed(gall.at[0 : N * ck - blk, part_of(1, 0, dd)], h_recv.at[kk, 0])
                    landed(gall.at[0 : N * ck, part_of(1, 1, dd)], h_recv.at[kk, 1])

    @pl.when(s == 1)
    def _():
        loads[0].wait()
        first[K + 1].wait()
        for kk in range(K):
            values_of(kk)
            acts_of(kk)
        pl.semaphore_wait(barrier, 2 * T + N - 2)
        for copy in lend:
            copy.start()
        for k in range(1, N):
            copy_act(k, d).start()
        keep_act.start()
        loads[1].wait()
        for b in range(N):
            part[:, block(b)] = dot_nt(act[...], wd[block(b), :])
        loads[2].wait()
        loads[3].wait()
        for q in subs:
            scatter(A, 1, 0, q)
        for kk in range(K):
            for q in subs:
                if kk + 1 < K:
                    scatter(A, 1, kk + 1, q)
                tangent(1, kk, q)
        for kk in range(K):
            r = chunk(kk)
            tv = None
            mean = None
            for b in range(N):
                pass_on(0, tbuf, 1, kk, b)
            for b in range(N):
                ready(0, tbuf, kk, b)
                c = block(b)
                tf = tbuf[r, c].astype(F32)
                dotted = jnp.sum(x_ref[r, c].astype(F32) * tf, axis=-1, keepdims=True)
                more = dot_nt((gain[:, c] * tf).astype(BF), wv[:, c])
                tv = more if tv is None else tv + more
                mean = dotted if mean is None else mean + dotted
            rr = rnorm_of(x_ref[r, :].astype(F32))
            tvals[r, :] = (rr * tv - (rr * rr * (1.0 / width) * mean) * vals[r, :].astype(F32)).astype(BF)
            tmix = mix(kk, tvals)
            for b in range(N):
                part[r, block(b)] = part[r, block(b)] + dot_nt(tmix, wo[block(b), :])
                mine = rows(kk, i)
                part[mine, block(b)] = part[mine, block(b)] + tbuf[mine, block(b)].astype(F32)
                pack(D_, part, kk, b)
        for copy in lend:
            copy.wait_send()
        done(1, (A,), ())
        for kk in range(K):
            for q in subs:
                seed(1, kk, q)
        done(1, (), ((0, tbuf),))
        for k in range(1, N):
            copy_act(k, d).wait_send()
        keep_act.wait()

        def copy_x(kk, k):
            dd = peer(d, k, N)
            return remote(
                gbuf.at[chunk(kk), feats_at(dd)], gall.at[seq_rows(kk)], x_send.at[kk], x_recv.at[kk], at(dd, s, i)
            )

        gms = []
        for kk in range(K):
            gm = None
            for b in range(N):
                pass_on(1, gbuf, 1, kk, b)
            for b in range(N):
                ready(1, gbuf, kk, b)
                more = dot_nn(gbuf[chunk(kk), block(b)], wo[block(b), :])
                gm = more if gm is None else gm + more
            gms.append(gm.astype(BF))
        pending = None
        for kk in reversed(range(K)):
            r = chunk(kk)
            more = jnp.concatenate(
                [dot_tn(probs_ref[h, r, :], gms[kk][:, h * hd : (h + 1) * hd]) for h in range(heads)], axis=1
            )
            pending = more if pending is None else pending + more
            gv = pending[r, :].astype(BF)
            weight = jnp.sum(gv.astype(F32) * vals[r, :].astype(F32), axis=-1, keepdims=True)
            high = weight.astype(BF).astype(F32)
            lane = lax.broadcasted_iota(jnp.int32, (ck, 128), 1)
            extra = jnp.where(lane < 64, high, weight - high).astype(BF)
            for y in (0, 1):
                f_src[y, 0, r, share(1, y, 0) : share(1, y, 0) + 128] = extra
            for b in range(N):
                part[r, block(b)] = dot_nn(gv, wv[:, block(b)])
                pack(F_, part, kk, b, (0,))
            for b in range(N):
                pack(F_, part, kk, b, (1,))
        for kk in range(K):
            for k in range(1, N):
                copy_x(kk, k).start()
            keep_rows(kk).start()
        done(1, (D_,), ((1, gbuf),))
        for k in range(1, N):
            copy_act(k, peer(d, N - k, N)).wait_recv()
        for kk in reversed(range(K)):
            xr = x_ref[rows(kk, i), :].astype(F32)
            adjoint(1, kk, xr, gain, rnorm_of(xr))
        done(1, (F_,), ())
        for kk in range(K):
            landed(gall.at[0 : (N - 1) * ck], x_recv.at[kk])
            sent(gall.at[0 : (N - 1) * ck], x_send.at[kk])
            keep_rows(kk).wait()
            for q in subs:
                hand(1, kk, q, False)


def call_pair(T, N, x, norm_gain, probs, w_val, w_dir, w_out, curvature):
    tok, width = x.shape
    hf = w_val.shape[0]
    K = TOKEN_CHUNKS
    Q = N
    ck = tok // K
    blk = ck // T
    feats = width // N
    wide = max(max(home_share(feats, g, q), feats - home_share(feats, g, q)) for g in (0, 1) for q in range(N))
    hbm = functools.partial(pl.BlockSpec, memory_space=pl.ANY)
    sem = pltpu.SemaphoreType.DMA

    def sums(cols):
        return [
            pltpu.VMEM((2, Q, tok, cols), BF),
            pltpu.VMEM((Q, tok, cols), BF),
            pltpu.VMEM((Q, K, T - 1, blk, cols), BF),
        ]

    scratch = [
        pltpu.VMEM((tok, width), BF),
        pltpu.VMEM((1, width), F32),
        pltpu.VMEM(probs.shape, BF),
        pltpu.VMEM((hf, width), BF),
        pltpu.VMEM((width, hf), BF),
        pltpu.VMEM((width, hf), BF),
        pltpu.VMEM((tok, width), BF),
        pltpu.VMEM((tok, hf), BF),
        pltpu.VMEM((tok, hf), BF),
        pltpu.VMEM((tok, hf), BF),
        pltpu.VMEM((tok, width), F32),
        pltpu.VMEM((tok, width), BF),
        pltpu.VMEM((tok, width), BF),
        pltpu.VMEM((K, blk, width), BF),
        pltpu.VMEM((1, width), F32),
        *sums(wide), *sums(wide), *sums(wide + 128),
        pltpu.VMEM((K, Q, blk, wide), BF),
        sem((6 + K,)),
        sem((K + 1,)), sem((K + 1,)),
        sem((N,)), sem((N,)),
        sem((3, K, Q)), sem((3, K, Q)),
        sem((3, K, Q)), sem((3, K, Q)),
        sem((2, K, Q, T)), sem((2, 2, K, Q)), sem((2, 2, K, Q)), sem((2, K, Q, T)),
        sem((K, Q)), sem((K, Q)), sem((K, 2)),
        sem((2 * K,)), sem((K,)),
    ]
    adjoints, acts = pl.pallas_call(
        functools.partial(kernel_pair, T, N),
        out_shape=(
            jax.ShapeDtypeStruct((N * tok, feats), BF), jax.ShapeDtypeStruct((N, tok, hf), BF),
        ),
        in_specs=[hbm()] * 7,
        out_specs=(hbm(), hbm()),
        scratch_shapes=scratch,
        compiler_params=pltpu.CompilerParams(
            collective_id=0, has_side_effects=True, vmem_limit_bytes=56 * 1024 * 1024
        ),
    )(x, norm_gain, probs, w_val, w_dir, w_out, curvature)
    return dot_tn(adjoints, acts.reshape(N * tok, hf))


def per_device(section_input, norm_gain, value_weight, attn_probs, out_weight, direction, curvature):
    x = section_input[0]
    w_val = value_weight[0]
    w_out = out_weight[0]
    w_dir = direction[0]
    probs = attn_probs[0]
    S = lax.axis_size("section")
    T = lax.axis_size("tensor")
    N = lax.axis_size("dp")
    tok, width = x.shape
    hf = w_val.shape[0]
    rows = tok // T
    feats = width // N
    fused = feats % 128 == 0 and feats * N == width
    blocks = tok % (16 * T * TOKEN_CHUNKS) == 0
    if fused and S == 2 and T == 4 and feats % 256 == 0 and blocks:
        return call_pair(T, N, x, norm_gain, probs, w_val, w_dir, w_out, curvature)[None]
    vm = functools.partial(pl.BlockSpec, memory_space=pltpu.VMEM)
    hbm = functools.partial(pl.BlockSpec, memory_space=pl.ANY)
    if fused:
        outs = jax.ShapeDtypeStruct((feats, hf), F32)
        out_specs = vm()
    else:
        outs = (jax.ShapeDtypeStruct((tok, width), BF), jax.ShapeDtypeStruct((tok, hf), BF))
        out_specs = (vm(), vm())
    sem = pltpu.SemaphoreType.DMA
    wide = N if fused else 1
    scratch = [
        pltpu.VMEM((hf, width), BF),
        pltpu.VMEM((width, hf), BF),
        pltpu.VMEM((width, hf), BF),
        pltpu.VMEM((tok, width), BF),
        pltpu.VMEM((tok, hf), BF),
        pltpu.VMEM((tok, width), F32),
        pltpu.VMEM((tok, width), BF),
        pltpu.VMEM((T, rows, width), BF),
        pltpu.VMEM((T, rows, width), BF),
        pltpu.VMEM((T, rows, width), BF),
        pltpu.VMEM((tok, width), BF),
        pltpu.VMEM((tok, width), BF),
        pltpu.VMEM((tok, width), BF),
        pltpu.VMEM((tok, width), BF),
        pltpu.VMEM((rows, width), F32),
        pltpu.VMEM((rows, width), BF),
        pltpu.VMEM((wide, tok, hf), BF),
        pltpu.VMEM((wide, tok, feats if fused else 128), BF),
        sem((4,)),
        sem((N,)), sem((N,)),
        sem((T,)), sem((T,)),
        sem((T,)), sem((T,)),
        sem((T,)), sem((T,)),
        sem((T,)), sem((T,)),
        sem((T,)), sem((T,)),
        sem((wide, T)), sem((wide, T)),
        sem((N,)), sem((N,)),
    ]
    result = pl.pallas_call(
        functools.partial(kernel, fused, S, T, N),
        out_shape=outs,
        in_specs=[vm(), vm(), vm(), hbm(), hbm(), hbm(), hbm()],
        out_specs=out_specs,
        scratch_shapes=scratch,
        compiler_params=pltpu.CompilerParams(
            collective_id=0, has_side_effects=True, vmem_limit_bytes=56 * 1024 * 1024
        ),
    )(x, norm_gain, probs, w_val, w_dir, w_out, curvature)
    if fused:
        return result[None]
    adjoint, act = result
    product = lax.psum_scatter(
        dot_tn(adjoint, act).astype(BF), "dp", scatter_dimension=0, tiled=True
    ).astype(F32)
    return product[None]


def solution(mesh):
    in_specs = (
        P("section", "dp", None),
        P("section", None),
        P("section", "tensor", None),
        P("section", "tensor", "dp", None),
        P("section", None, "tensor"),
        P("section", None, "tensor"),
        P("dp", None),
    )
    out_specs = P("section", "dp", "tensor")
    return jax.shard_map(
        per_device, mesh=mesh, in_specs=in_specs, out_specs=out_specs, check_vma=False
    )
```
